128 devices in a mesh: space: 32 (over z, y_hi, x), sample: 4 (over y_lo, core).
Axes of the slice: x: 4, y: 4 (y_hi: 2, y_lo: 2; y = y_hi * 2 + y_lo), z: 4, core: 2. Of those that a mesh axis runs over, the one named last changes fastest.
Arguments:
- state_hat: float32 [20, 3, 256, 32, 128], P('sample', None, 'space'), may hold values from -2.4 to 2.4
- adjoint_hat: float32 [20, 3, 256, 32, 128], P('sample', None, 'space'), may hold values from -2.4 to 2.4
- objective_hat: float32 [20, 3, 256, 32, 128], P('sample', None, 'space'), may hold values from -6 to 6
- density: float32 [256, 32, 128], P('space'), may hold values from 0.05 to 1
- region: int32 [256, 32, 128], P('space'), may hold values from 0 to 3
Outputs:
- adjoint_residual: float32 [20, 3, 256, 32, 128], P('sample', None, 'space')
- density_gradient: float32 [256, 32, 128], P('space', 'sample')
The draws below stay inside these ranges and needn't reach their ends.
All inputs are finite; a program needn't handle non-finite values.
Results may differ from the reference program's by a relative error of at most 0.00026.
Values sent between devices are 32-bit elements; how exact they have to be, the bound alone decides.
A program may use at most 128 MiB of HBM per device.

```python
import math
import jax
import jax.numpy as jnp
from jax import lax

NY = 32
NZ = 128
NCOEF = 20
NT = 40
NX = 256


def touch_ends(result, rng, smallest, largest):
    extent = result.shape
    spot = [jax.random.randint(jax.random.fold_in(rng, axis), (), 0, extent[axis]) for axis in range(len(extent))]
    result = result.at[tuple(spot)].set(smallest)
    longest = extent.index(max(extent))
    spot[longest] = (spot[longest] + 1) % extent[longest]
    return result.at[tuple(spot)].set(largest)


def block_scale(key, dims, pieces, low, largest):
    loudness = 1.0
    for dim, parts in pieces:
        heights = jax.random.uniform(jax.random.fold_in(jax.random.fold_in(key, 6), dim), (parts,), jnp.float32, low / len(pieces), largest / len(pieces))
        loudness = loudness * jnp.repeat(jnp.exp(heights), dims[dim] // parts).reshape((-1,) + (1,) * (len(dims) - 1 - dim))
    return loudness


def bell_draw(own_key, shape, width, reach, split=(), held_as=jnp.bfloat16):
    factor_of = block_scale(own_key, shape, split, -0.22, 0.18) if split else 1.0
    drawn = jax.random.normal(own_key, shape, jnp.float32) * width * factor_of
    return jnp.minimum(jnp.maximum(drawn, -reach), reach).astype(held_as)


def setup_inputs(seed: int = 0) -> dict:
    seeds = jax.random.split(jax.random.key(seed), 6)
    state_hat = bell_draw(seeds[0], (NCOEF, 3, NX, NY, NZ), 0.3, 2.4, ((0, 4), (2, 32)), jnp.float32)
    adjoint_hat = bell_draw(seeds[1], (NCOEF, 3, NX, NY, NZ), 0.3, 2.4, ((0, 4), (2, 32)), jnp.float32)
    objective_hat = bell_draw(seeds[2], (NCOEF, 3, NX, NY, NZ), 1.0, 6.0, ((0, 4), (2, 32)), jnp.float32)
    density = jnp.clip(0.05 + 0.95 * jax.random.uniform(seeds[3], (NX, NY, NZ), jnp.float32) ** block_scale(seeds[3], (NX, NY, NZ), ((0, 32),), -0.2, 0.2), 0.05, 1.0)
    region = touch_ends(jax.random.randint(seeds[4], (NX, NY, NZ), 0, 4), jax.random.fold_in(seeds[4], 1), 0, 3).astype(jnp.int32)
    return dict(state_hat=state_hat, adjoint_hat=adjoint_hat, objective_hat=objective_hat, density=density, region=region)


magnet_reluct = 0.95
iron_floor = 0.05
saturation = 1.0


def harmonic_table():
    sample_steps = jnp.arange(NT, dtype=jnp.int32).astype(jnp.float32)
    orders = (jnp.arange(NCOEF // 2, dtype=jnp.int32) + 1).astype(jnp.float32)
    angles = (2.0 * math.pi / NT) * sample_steps[:, None] * orders[None, :]
    return jnp.stack([jnp.cos(angles), jnp.sin(angles)], axis=2).reshape(NT, NCOEF)


def forward_diff(potential, along):
    length = potential.shape[along]
    widths = [(0, 0)] * potential.ndim
    widths[along] = (0, 1)
    padded = jnp.pad(potential, widths)
    return lax.slice_in_dim(padded, 1, length + 1, axis=along) - potential


def backward_diff(potential, along):
    length = potential.shape[along]
    widths = [(0, 0)] * potential.ndim
    widths[along] = (1, 0)
    padded = jnp.pad(potential, widths)
    return lax.slice_in_dim(padded, 0, length, axis=along) - potential


def curl_field(potential):
    part_one, part_two, part_three = potential[0], potential[1], potential[2]
    flux_one = forward_diff(part_three, 1) - forward_diff(part_two, 2)
    flux_two = forward_diff(part_one, 2) - forward_diff(part_three, 0)
    flux_three = forward_diff(part_two, 0) - forward_diff(part_one, 1)
    return jnp.stack([flux_one, flux_two, flux_three], axis=0)


def curl_back(field_h):
    back_one = backward_diff(field_h[1], 2) - backward_diff(field_h[2], 1)
    back_two = backward_diff(field_h[2], 0) - backward_diff(field_h[0], 2)
    back_three = backward_diff(field_h[0], 1) - backward_diff(field_h[1], 0)
    return jnp.stack([back_one, back_two, back_three], axis=0)


def material(density, region):
    iron_share = jnp.where(region == 0, density ** 3, jnp.zeros_like(density))
    iron_slope = jnp.where(region == 0, 3.0 * density ** 2, jnp.zeros_like(density))
    base_reluct = jnp.where(region == 1, magnet_reluct * jnp.ones_like(density), jnp.ones_like(density))
    return iron_share, iron_slope, base_reluct


def reference(state_hat, adjoint_hat, objective_hat, density, region):
    harm_table = harmonic_table()
    iron_share, iron_slope, base_reluct = material(density, region)

    def one_sample(carry, time_row):
        summed, gradient = carry
        state_time = jnp.tensordot(time_row, state_hat, axes=1, precision=lax.Precision.HIGHEST)
        adjoint_time = jnp.tensordot(time_row, adjoint_hat, axes=1, precision=lax.Precision.HIGHEST)
        state_flux = curl_field(state_time)
        adjoint_flux = curl_field(adjoint_time)
        flux_square = jnp.sum(state_flux * state_flux, axis=0)
        flux_inner = jnp.sum(state_flux * adjoint_flux, axis=0)
        iron_curve = iron_floor + (1.0 - iron_floor) * flux_square / (flux_square + saturation)
        curve_slope = (1.0 - iron_floor) * saturation / (flux_square + saturation) ** 2
        reluct_now = base_reluct + iron_share * (iron_curve - 1.0)
        reluct_slope = iron_share * curve_slope
        field_h = reluct_now[None] * adjoint_flux + (2.0 * reluct_slope * flux_inner)[None] * state_flux
        back_field = curl_back(field_h)
        summed = summed + (2.0 / NT) * time_row[:, None, None, None, None] * back_field[None]
        gradient = gradient + iron_slope * (iron_curve - 1.0) * flux_inner
        return (summed, gradient), time_row

    start_carry = (jnp.zeros(state_hat.shape, jnp.float32), jnp.zeros(density.shape, jnp.float32))
    finals, unused = lax.scan(one_sample, start_carry, harm_table)
    return objective_hat - finals[0], -finals[1] / NT
```

```python
import functools
import math

import jax
import jax.numpy as jnp
from jax import lax
from jax.experimental import pallas as pl
from jax.experimental.pallas import tpu as pltpu
from jax.sharding import PartitionSpec as P

NT = 40
NCOEF = 20
NY = 32
NZ = 128
PLANES = 8
GROUP = 4
OWN = NCOEF // GROUP
ROWS = NY // GROUP
FOLDS = NT // 4 + 1

magnet_reluct = 0.95
iron_floor = 0.05

CLASSES = (
    ("cos", (2, 4, 6, 8, 10)),
    ("cos", (1, 3, 5, 7, 9)),
    ("sin", (2, 4, 6, 8, 10)),
    ("sin", (1, 3, 5, 7, 9)),
)


def coef_index(kind, order):
    return 2 * (order - 1) + (0 if kind == "cos" else 1)


def factor(kind, order, n):
    turn = (n * order) % NT
    quarter = NT // 4
    if kind == "sin":
        turn = (turn - quarter) % NT
    if turn % quarter == 0:
        return (1.0, 0.0, -1.0, 0.0)[turn // quarter]
    if turn * 3 % NT == 0 and False:
        return 0.0
    return math.cos(2.0 * math.pi * turn / NT)


def combine(terms, constants):
    total = None
    for term, constant in zip(terms, constants):
        if constant == 0.0:
            continue
        if constant == 1.0:
            piece = term
        elif constant == -1.0:
            piece = -term
        else:
            piece = term * jnp.float32(constant)
        total = piece if total is None else total + piece
    return jnp.zeros_like(terms[0]) if total is None else total


def plane_at(k):
    return lax.rem(k + PLANES // 2, PLANES)


def kernel(
    state_hbm, adjoint_hbm, objective_hbm, density_hbm, region_hbm,
    out_hbm, grad_hbm,
    pot, obj, dens, regn, upper, lower, send, recv, hsend, hrecv, wave, fold, out, grad,
    in_sems, obj_sem, mat_sems, up_send, up_recv, low_send, low_recv,
    f_send, f_recv, b_send, b_recv, out_sems, grad_sem,
):
    me = lax.axis_index("sample")
    block = lax.axis_index("space")
    blocks = lax.axis_size("space")
    above = lax.rem(block + 1, blocks)
    below = lax.rem(block + blocks - 1, blocks)

    def load(k):
        p = plane_at(k)
        return [
            pltpu.make_async_copy(ref.at[:, :, p], pot.at[i, p], in_sems.at[i, p])
            for i, ref in enumerate((state_hbm, adjoint_hbm))
        ]

    @pl.loop(0, PLANES)
    def _(k):
        for copy in load(k):
            copy.start()

    rows = pl.ds(pl.multiple_of(me * ROWS, ROWS), ROWS)
    material = [
        pltpu.make_async_copy(density_hbm.at[:, rows], dens, mat_sems.at[0]),
        pltpu.make_async_copy(region_hbm.at[:, rows], regn, mat_sems.at[1]),
    ]
    for copy in material:
        copy.start()
    objective = pltpu.make_async_copy(objective_hbm, obj, obj_sem)
    objective.start()

    peers = [lax.rem(me + r, GROUP) for r in range(1, GROUP)]
    barrier = pltpu.get_barrier_semaphore()
    for peer in peers:
        pl.semaphore_signal(barrier, inc=1, device_id={"sample": peer}, device_id_type=pl.DeviceIdType.MESH)
    for other in (above, below):
        pl.semaphore_signal(barrier, inc=1, device_id={"space": other}, device_id_type=pl.DeviceIdType.MESH)
    pl.semaphore_wait(barrier, GROUP + 1)

    ups = [
        pltpu.make_async_remote_copy(
            src_ref=ref.at[:, 1:3, 0], dst_ref=upper.at[i],
            send_sem=up_send.at[i], recv_sem=up_recv.at[i],
            device_id={"space": below}, device_id_type=pl.DeviceIdType.MESH,
        )
        for i, ref in enumerate((state_hbm, adjoint_hbm))
    ]
    for copy in ups:
        copy.start()

    def forward(p):
        return [
            pltpu.make_async_remote_copy(
                src_ref=send.at[p, peer], dst_ref=recv.at[p, me],
                send_sem=f_send.at[p, r], recv_sem=f_recv.at[p, r],
                device_id={"sample": peer}, device_id_type=pl.DeviceIdType.MESH,
            )
            for r, peer in enumerate(peers)
        ]

    def backward(p):
        return [
            pltpu.make_async_remote_copy(
                src_ref=hsend.at[p, peer], dst_ref=hrecv.at[p, me],
                send_sem=b_send.at[p, r], recv_sem=b_recv.at[p, r],
                device_id={"sample": peer}, device_id_type=pl.DeviceIdType.MESH,
            )
            for r, peer in enumerate(peers)
        ]

    row_id = lax.broadcasted_iota(jnp.int32, (NY, NZ), 0)
    lane_id = lax.broadcasted_iota(jnp.int32, (NY, NZ), 1)

    def next_row(a):
        return jnp.where(row_id == NY - 1, 0.0, pltpu.roll(a, NY - 1, 0))

    def next_lane(a):
        return jnp.where(lane_id == NZ - 1, 0.0, pltpu.roll(a, NZ - 1, 1))

    def prior_row(a):
        return jnp.where(row_id == 0, 0.0, pltpu.roll(a, 1, 0))

    def prior_lane(a):
        return jnp.where(lane_id == 0, 0.0, pltpu.roll(a, 1, 1))

    def curl(p, j, i, up_one, up_two):
        zero, one, two = pot[i, p, j, 0], pot[i, p, j, 1], pot[i, p, j, 2]
        first = (next_row(two) - two) - (next_lane(one) - one)
        second = (next_lane(zero) - zero) - (up_two - two)
        third = (up_one - one) - (next_row(zero) - zero)
        for c, part in enumerate((first, second, third)):
            send[p, :, 3 * i + c, j] = part.reshape(GROUP, ROWS, NZ)

    def finish_curl(p):
        recv[p, me] = send[p, me]
        for copy in forward(p)[1:] + forward(p)[:1]:
            copy.start()

    @pl.loop(0, PLANES)
    def _(k):
        p = plane_at(k)

        @pl.when(k == 0)
        def _():
            for copy in load(k):
                copy.wait()

        @pl.when((k < PLANES - 1) & (k != PLANES // 2 - 1))
        def _():
            for copy in load(k + 1):
                copy.wait()

        @pl.when(p < PLANES - 1)
        def _():
            @pl.loop(0, OWN)
            def _(j):
                for i in range(2):
                    curl(p, j, i, pot[i, p + 1, j, 1], pot[i, p + 1, j, 2])

        @pl.when(p == PLANES - 1)
        def _():
            for copy in load(k + 1):
                copy.wait()
            for copy in ups:
                copy.wait_recv()
            last = block == blocks - 1

            @pl.loop(0, OWN)
            def _(j):
                for i in range(2):
                    curl(
                        PLANES - 1, j, i,
                        jnp.where(last, 0.0, upper[i, j, 0]),
                        jnp.where(last, 0.0, upper[i, j, 1]),
                    )

        finish_curl(p)

    for copy in material:
        copy.wait()

    def nonlinear(p):
        @pl.loop(0, 6)
        def _(pc):
            for t, (kind, orders) in enumerate(CLASSES):
                where = [coef_index(kind, m) for m in orders]
                terms = [recv[p, c // OWN, pc, c % OWN] for c in where]
                for n in range(FOLDS):
                    wave[n, t, pc] = combine(terms, [factor(kind, m, n) for m in orders])

        density, region = dens[p], regn[p]
        iron = region == 0
        share = jnp.where(iron, density * density * density, 0.0) * jnp.float32(1.0 - iron_floor)
        slope = jnp.where(iron, 3.0 * density * density, 0.0)
        base = jnp.where(region == 1, jnp.float32(magnet_reluct), jnp.float32(1.0))

        def samples(n, total):
            state = [[], [], []]
            adjoint = [[], [], []]
            for pc in range(6):
                ce, co, se, so = (wave[n, t, pc] for t in range(4))
                a, b, d, f = ce + co, ce - co, se + so, se - so
                (state if pc < 3 else adjoint)[pc % 3] = (a + d, a - d, b - f, b + f)
            field = [[], [], []]
            part = None
            for v in range(4):
                s = [state[c][v] for c in range(3)]
                g = [adjoint[c][v] for c in range(3)]
                square = s[0] * s[0] + s[1] * s[1] + s[2] * s[2]
                inner = s[0] * g[0] + s[1] * g[1] + s[2] * g[2]
                r = 1.0 / (square + 1.0)
                t = share * r
                ri = r * inner
                nu = base - t
                mu = (t + t) * ri
                part = ri if part is None else part + ri
                for c in range(3):
                    field[c].append(nu * g[c] + mu * s[c])
            for c in range(3):
                w, x, y, z = field[c]
                a, d = w + x, w - x
                b, f = z + y, z - y
                fold[n, 0, c] = a + b
                fold[n, 1, c] = a - b
                fold[n, 2, c] = d + f
                fold[n, 3, c] = d - f
            ends = (n == 0) | (n == FOLDS - 1)
            return total + part * jnp.where(ends, 0.5, 1.0)

        total = lax.fori_loop(0, FOLDS, samples, jnp.zeros((ROWS, NZ), jnp.float32))
        grad[p] = total * slope * jnp.float32((1.0 - iron_floor) / NT)

        @pl.loop(0, 3)
        def _(c):
            for t, (kind, orders) in enumerate(CLASSES):
                terms = [fold[n, t, c] for n in range(FOLDS)]
                terms[0] = terms[0] * 0.5
                terms[-1] = terms[-1] * 0.5
                for m in orders:
                    got = combine(terms, [factor(kind, m, n) for n in range(FOLDS)])
                    at = coef_index(kind, m)
                    hsend[p, at // OWN, at % OWN, c] = got * jnp.float32(2.0 / NT)

    @pl.loop(0, PLANES)
    def _(k):
        p = plane_at(k)
        for copy in forward(p):
            copy.wait_recv()
        nonlinear(p)
        hrecv[p, me] = hsend[p, me]
        for copy in backward(p)[1:] + backward(p)[:1]:
            copy.start()

    gradient = pltpu.make_async_copy(grad, grad_hbm, grad_sem)
    gradient.start()

    down = pltpu.make_async_remote_copy(
        src_ref=hrecv.at[PLANES - 1, :, :, 1:3], dst_ref=lower,
        send_sem=low_send, recv_sem=low_recv,
        device_id={"space": above}, device_id_type=pl.DeviceIdType.MESH,
    )

    def whole(ref, p, j, c):
        return ref[p, :, j, c].reshape(NY, NZ)

    def store(p):
        return pltpu.make_async_copy(out.at[p], out_hbm.at[:, :, p], out_sems.at[p])

    def curl_back(p, j, low_one, low_two):
        zero, one, two = (whole(hrecv, p, j, c) for c in range(3))
        x_one, x_two = low_one - one, low_two - two
        first = (prior_lane(one) - one) - (prior_row(two) - two)
        second = x_two - (prior_lane(zero) - zero)
        third = (prior_row(zero) - zero) - x_one
        for c, part in enumerate((first, second, third)):
            out[p, j, c] = obj[j, c, p] - part

    def inner_plane(p):
        @pl.loop(0, OWN)
        def _(j):
            curl_back(p, j, whole(hrecv, p - 1, j, 1), whole(hrecv, p - 1, j, 2))

        store(p).start()

    objective.wait()

    @pl.loop(0, PLANES)
    def _(k):
        p = plane_at(k)
        for copy in backward(p):
            copy.wait_recv()

        @pl.when(p == PLANES - 1)
        def _():
            down.start()

        @pl.when((k > 0) & (p > 0))
        def _():
            inner_plane(p)

        @pl.when(p == 0)
        def _():
            down.wait_recv()
            first = block == 0

            @pl.loop(0, OWN)
            def _(j):
                curl_back(
                    0, j,
                    jnp.where(first, 0.0, lower[:, j, 0].reshape(NY, NZ)),
                    jnp.where(first, 0.0, lower[:, j, 1].reshape(NY, NZ)),
                )

            store(p).start()

    inner_plane(PLANES // 2)

    gradient.wait()
    for copy in ups:
        copy.wait_send()
    down.wait_send()

    @pl.loop(0, PLANES)
    def _(p):
        store(p).wait()
        for copy in forward(p) + backward(p):
            copy.wait_send()


def local(state_hat, adjoint_hat, objective_hat, density, region):
    f32 = jnp.float32
    hbm = pl.BlockSpec(memory_space=pl.ANY)
    dma = pltpu.SemaphoreType.DMA
    return pl.pallas_call(
        kernel,
        out_shape=(
            jax.ShapeDtypeStruct((OWN, 3, PLANES, NY, NZ), f32),
            jax.ShapeDtypeStruct((PLANES, ROWS, NZ), f32),
        ),
        in_specs=[hbm] * 5,
        out_specs=(hbm, hbm),
        scratch_shapes=[
            pltpu.VMEM((2, PLANES, OWN, 3, NY, NZ), f32),
            pltpu.VMEM((OWN, 3, PLANES, NY, NZ), f32),
            pltpu.VMEM((PLANES, ROWS, NZ), f32),
            pltpu.VMEM((PLANES, ROWS, NZ), jnp.int32),
            pltpu.VMEM((2, OWN, 2, NY, NZ), f32),
            pltpu.VMEM((GROUP, OWN, 2, ROWS, NZ), f32),
            pltpu.VMEM((PLANES, GROUP, 6, OWN, ROWS, NZ), f32),
            pltpu.VMEM((PLANES, GROUP, 6, OWN, ROWS, NZ), f32),
            pltpu.VMEM((PLANES, GROUP, OWN, 3, ROWS, NZ), f32),
            pltpu.VMEM((PLANES, GROUP, OWN, 3, ROWS, NZ), f32),
            pltpu.VMEM((FOLDS, 4, 6, ROWS, NZ), f32),
            pltpu.VMEM((FOLDS, 4, 3, ROWS, NZ), f32),
            pltpu.VMEM((PLANES, OWN, 3, NY, NZ), f32),
            pltpu.VMEM((PLANES, ROWS, NZ), f32),
            dma((2, PLANES)), dma, dma((2,)), dma((2,)), dma((2,)), dma, dma,
            dma((PLANES, GROUP - 1)), dma((PLANES, GROUP - 1)),
            dma((PLANES, GROUP - 1)), dma((PLANES, GROUP - 1)),
            dma((PLANES,)), dma,
        ],
        compiler_params=pltpu.CompilerParams(
            collective_id=0, has_side_effects=True, vmem_limit_bytes=60 * 1024 * 1024
        ),
    )(state_hat, adjoint_hat, objective_hat, density, region)


def solution(mesh):
    in_specs = (
        P("sample", None, "space", None, None),
        P("sample", None, "space", None, None),
        P("sample", None, "space", None, None),
        P("space", None, None),
        P("space", None, None),
    )
    out_specs = (P("sample", None, "space", None, None), P("space", "sample", None))
    return jax.shard_map(local, mesh=mesh, in_specs=in_specs, out_specs=out_specs, check_vma=False)
```

```python
import math

import jax
import jax.numpy as jnp
from jax import lax
from jax.experimental import pallas as pl
from jax.experimental.pallas import tpu as pltpu
from jax.sharding import PartitionSpec as P

NT = 40
NCOEF = 20
NY = 32
NZ = 128
PLANES = 8
GROUP = 4
OWN = NCOEF // GROUP
ROWS = NY // GROUP
FOLDS = NT // 4 + 1
PAIRS = 2 * OWN
RUN = 4

magnet_reluct = 0.95
iron_floor = 0.05

CLASSES = (
    ("cos", (2, 4, 6, 8, 10)),
    ("cos", (1, 3, 5, 7, 9)),
    ("sin", (2, 4, 6, 8, 10)),
    ("sin", (1, 3, 5, 7, 9)),
)


def coef_index(kind, order):
    return 2 * (order - 1) + (0 if kind == "cos" else 1)


def factor(kind, order, n):
    turn = (n * order) % NT
    quarter = NT // 4
    if kind == "sin":
        turn = (turn - quarter) % NT
    if turn % quarter == 0:
        return (1.0, 0.0, -1.0, 0.0)[turn // quarter]
    return math.cos(2.0 * math.pi * turn / NT)


def combine(terms, constants):
    total = None
    for term, constant in zip(terms, constants):
        if constant == 0.0:
            continue
        if constant == 1.0:
            piece = term
        elif constant == -1.0:
            piece = -term
        else:
            piece = term * jnp.float32(constant)
        total = piece if total is None else total + piece
    return jnp.zeros_like(terms[0]) if total is None else total


def kernel(
    state_hbm, adjoint_hbm, objective_hbm, density_hbm, region_hbm,
    out_hbm, grad_hbm,
    pot, phi, obj, dens, regn, upper, lower, send, recv, phi_send, phi_recv,
    hsend, hrecv, flux, wave, fold, psi, out, grad, grad_in,
    in_sems, obj_sem, mat_sems, up_send, up_recv, low_send, low_recv,
    f_send, f_recv, b_send, b_recv, g_send, g_recv, out_sems, grad_sem,
):
    me = lax.axis_index("sample")
    block = lax.axis_index("space")
    blocks = lax.axis_size("space")
    above = lax.rem(block + 1, blocks)
    below = lax.rem(block + blocks - 1, blocks)
    mesh_id = pl.DeviceIdType.MESH

    def turned(index, where):
        return lax.rem(index + 2 * lax.rem(where // RUN, 2), GROUP)

    odd = lax.rem(block // RUN, 2)
    slab = turned(me, block)
    up_id = {"space": above, "sample": turned(slab, above)}
    down_id = {"space": below, "sample": turned(slab, below)}
    peers = [lax.rem(me + r, GROUP) for r in (2, 3, 1)]

    def load(p):
        return [
            pltpu.make_async_copy(ref.at[:, :, p], pot.at[i, p], in_sems.at[i, p])
            for i, ref in enumerate((state_hbm, adjoint_hbm))
        ]

    @pl.loop(0, PLANES)
    def _(p):
        for copy in load(p):
            copy.start()

    rows = pl.ds(pl.multiple_of(slab * ROWS, ROWS), ROWS)
    material = [
        pltpu.make_async_copy(density_hbm.at[:, rows], dens, mat_sems.at[0]),
        pltpu.make_async_copy(region_hbm.at[:, rows], regn, mat_sems.at[1]),
    ]
    for copy in material:
        copy.start()
    objective = pltpu.make_async_copy(objective_hbm, obj, obj_sem)
    objective.start()

    barrier = pltpu.get_barrier_semaphore()
    for peer in peers:
        pl.semaphore_signal(barrier, inc=1, device_id={"sample": peer}, device_id_type=mesh_id)
    for other in (up_id, down_id):
        pl.semaphore_signal(barrier, inc=1, device_id=other, device_id_type=mesh_id)

    def exchange(source, target, sends, recvs, at):
        return [
            pltpu.make_async_remote_copy(
                src_ref=source(peer), dst_ref=target,
                send_sem=sends.at[at, r], recv_sem=recvs.at[at, r],
                device_id={"sample": peer}, device_id_type=mesh_id,
            )
            for r, peer in enumerate(peers)
        ]

    def forward(p):
        return exchange(lambda peer: send.at[p, turned(peer, block)], recv.at[p, me], f_send, f_recv, p)

    def forward_phi():
        return exchange(lambda peer: phi_send.at[turned(peer, block)], phi_recv.at[me], f_send, f_recv, PLANES)

    def backward(p):
        return exchange(lambda peer: hsend.at[p, peer], hrecv.at[p, slab], b_send, b_recv, p)

    row_id = lax.broadcasted_iota(jnp.int32, (NY, NZ), 0)
    lane_id = lax.broadcasted_iota(jnp.int32, (NY, NZ), 1)
    slab_row = lax.broadcasted_iota(jnp.int32, (ROWS, NZ), 0)
    slab_lane = lax.broadcasted_iota(jnp.int32, (ROWS, NZ), 1)

    def next_row(a):
        return jnp.where(row_id == NY - 1, 0.0, pltpu.roll(a, NY - 1, 0))

    def next_lane(a):
        return jnp.where(lane_id == NZ - 1, 0.0, pltpu.roll(a, NZ - 1, 1))

    def prior_row(a):
        return jnp.where(row_id == 0, 0.0, pltpu.roll(a, 1, 0))

    def prior_lane(a):
        return jnp.where(lane_id == 0, 0.0, pltpu.roll(a, 1, 1))

    def slab_next_row(a, row):
        return jnp.where(slab_row == ROWS - 1, row, pltpu.roll(a, ROWS - 1, 0))

    def slab_next_lane(a):
        return jnp.where(slab_lane == NZ - 1, 0.0, pltpu.roll(a, NZ - 1, 1))

    def slab_prior_row(a):
        return jnp.where(slab_row == 0, 0.0, pltpu.roll(a, 1, 0))

    def slab_prior_lane(a):
        return jnp.where(slab_lane == 0, 0.0, pltpu.roll(a, 1, 1))

    def put_rows(ref, first, at, a):
        for s in range(GROUP - 1):
            ref[s, first + at // ROWS, pl.ds(at % ROWS, 1), :] = a[ROWS * (s + 1):ROWS * (s + 1) + 1, :]

    nothing = jnp.zeros((2, ROWS, NZ), jnp.float32)
    phi_send[GROUP - 1, pl.ds(PAIRS, 2)] = nothing

    @pl.loop(0, PLANES)
    def _(p):
        send[p, GROUP - 1, pl.ds(2 * PAIRS, 2)] = nothing

    for copy in load(0):
        copy.wait()
    for i in range(2):
        for j in range(OWN):
            at = i * OWN + j
            one, two = pot[i, 0, j, 1], pot[i, 0, j, 2]
            send[0, :, at] = one.reshape(GROUP, ROWS, NZ)
            send[0, :, PAIRS + at] = two.reshape(GROUP, ROWS, NZ)
            put_rows(send.at[0], 2 * PAIRS, at, two)
            phi[0, i, j] = pot[i, 0, j, 0]
    recv[0, me] = send[0, slab]
    pl.semaphore_wait(barrier, GROUP + 1)
    for copy in forward(0):
        copy.start()

    @pl.loop(1, PLANES)
    def _(p):
        for copy in load(p):
            copy.wait()

        for i in range(2):
            @pl.loop(0, OWN)
            def _(j):
                phi[p, i, j] = phi[p - 1, i, j] + pot[i, p, j, 0]

    for i in range(2):
        for j in range(OWN):
            at = i * OWN + j
            top = phi[PLANES - 1, i, j]
            phi_send[:, at] = top.reshape(GROUP, ROWS, NZ)
            put_rows(phi_send, PAIRS, at, top)
    phi_recv[me] = phi_send[slab]
    for copy in forward_phi():
        copy.start()

    @pl.loop(0, PLANES - 1)
    def _(k):
        p = PLANES - 1 - k
        for i in range(2):
            for j in range(OWN):
                at = i * OWN + j
                under = phi[p - 1, i, j]
                one = pot[i, p, j, 1] - (next_row(under) - under)
                two = pot[i, p, j, 2] - (next_lane(under) - under)
                send[p, :, at] = one.reshape(GROUP, ROWS, NZ)
                send[p, :, PAIRS + at] = two.reshape(GROUP, ROWS, NZ)
                put_rows(send.at[p], 2 * PAIRS, at, two)
        recv[p, me] = send[p, slab]
        for copy in forward(p):
            copy.start()

    for copy in forward(0):
        copy.wait_recv()
    up = pltpu.make_async_remote_copy(
        src_ref=recv.at[0, :, pl.ds(0, 2 * PAIRS)], dst_ref=upper,
        send_sem=up_send, recv_sem=up_recv, device_id=down_id, device_id_type=mesh_id,
    )
    up.start()
    for copy in material:
        copy.wait()
    psi[...] = jnp.zeros_like(psi)
    for copy in forward_phi():
        copy.wait_recv()
    up.wait_recv()
    last = block == blocks - 1

    @pl.loop(0, GROUP)
    def _(q):
        for at in range(PAIRS):
            top = phi_recv[q, at]
            row = phi_recv[q, PAIRS + at // ROWS, pl.ds(at % ROWS, 1), :]
            one = jnp.where(last, 0.0, upper[q, at])
            two = jnp.where(last, 0.0, upper[q, PAIRS + at])
            recv[PLANES, q, at] = one - (slab_next_row(top, row) - top)
            recv[PLANES, q, PAIRS + at] = two - (slab_next_lane(top) - top)

    down = pltpu.make_async_remote_copy(
        src_ref=hsend.at[PLANES, :, pl.ds(0, PAIRS)], dst_ref=lower,
        send_sem=low_send, recv_sem=low_recv, device_id=up_id, device_id_type=mesh_id,
    )

    def nonlinear(p):
        @pl.loop(0, GROUP)
        def _(q):
            for i in range(2):
                for j in range(OWN):
                    at = i * OWN + j
                    one, two = recv[p, q, at], recv[p, q, PAIRS + at]
                    row = recv[p, q, 2 * PAIRS + at // ROWS, pl.ds(at % ROWS, 1), :]
                    flux[3 * i, q, j] = (slab_next_row(two, row) - two) - (slab_next_lane(one) - one)
                    flux[3 * i + 1, q, j] = two - recv[p + 1, q, PAIRS + at]
                    flux[3 * i + 2, q, j] = recv[p + 1, q, at] - one

        @pl.loop(0, 6)
        def _(pc):
            for t, (kind, orders) in enumerate(CLASSES):
                where = [coef_index(kind, m) for m in orders]
                terms = [flux[pc, c // OWN, c % OWN] for c in where]
                for n in range(FOLDS):
                    wave[n, t, pc] = combine(terms, [factor(kind, m, n) for m in orders])

        density, region = dens[p], regn[p]
        iron = region == 0
        share = jnp.where(iron, density * density * density, 0.0) * jnp.float32(1.0 - iron_floor)
        slope = jnp.where(iron, 3.0 * density * density, 0.0)
        base = jnp.where(region == 1, jnp.float32(magnet_reluct), jnp.float32(1.0))

        def samples(n, total):
            state = [[], [], []]
            adjoint = [[], [], []]
            for pc in range(6):
                ce, co, se, so = (wave[n, t, pc] for t in range(4))
                a, b, d, f = ce + co, ce - co, se + so, se - so
                (state if pc < 3 else adjoint)[pc % 3] = (a + d, a - d, b - f, b + f)
            field = [[], [], []]
            part = None
            for v in range(4):
                s = [state[c][v] for c in range(3)]
                g = [adjoint[c][v] for c in range(3)]
                square = s[0] * s[0] + s[1] * s[1] + s[2] * s[2]
                inner = s[0] * g[0] + s[1] * g[1] + s[2] * g[2]
                r = 1.0 / (square + 1.0)
                t = share * r
                ri = r * inner
                nu = base - t
                mu = (t + t) * ri
                part = ri if part is None else part + ri
                for c in range(3):
                    field[c].append(nu * g[c] + mu * s[c])
            for c in range(3):
                w, x, y, z = field[c]
                a, d = w + x, w - x
                b, f = z + y, z - y
                fold[n, 0, c] = a + b
                fold[n, 1, c] = a - b
                fold[n, 2, c] = d + f
                fold[n, 3, c] = d - f
            ends = (n == 0) | (n == FOLDS - 1)
            return total + part * jnp.where(ends, 0.5, 1.0)

        total = lax.fori_loop(0, FOLDS, samples, jnp.zeros((ROWS, NZ), jnp.float32))
        grad[p] = total * slope * jnp.float32((1.0 - iron_floor) / NT)

        for t, (kind, orders) in enumerate(CLASSES):
            for c in (1, 2, 0):
                terms = [fold[n, t, c] for n in range(FOLDS)]
                for m in orders:
                    scales = [
                        factor(kind, m, n) * (1.0 if 0 < n < FOLDS - 1 else 0.5) * 2.0 / NT
                        for n in range(FOLDS)
                    ]
                    got = combine(terms, scales)
                    at = coef_index(kind, m)
                    q, j = at // OWN, at % OWN
                    old = psi[at]
                    if c == 1:
                        hsend[p + 1, q, j] = got - (slab_prior_row(old) - old)
                    elif c == 2:
                        hsend[p + 1, q, OWN + j] = got - (slab_prior_lane(old) - old)
                    else:
                        hsend[p + 1, q, PAIRS, pl.ds(j, 1), :] = old[ROWS - 1:, :]
                        psi[at] = old + got

    def give_back(p):
        hrecv[p, slab] = hsend[p, me]
        for copy in backward(p):
            copy.start()

    @pl.loop(0, PLANES)
    def _(k):
        p = PLANES - 1 - k

        @pl.when(p > 0)
        def _():
            for copy in forward(p):
                copy.wait_recv()

        nonlinear(p)

        @pl.when(k == 0)
        def _():
            down.start()

        give_back(p + 1)

    down.wait_recv()
    first = block == 0
    for q in range(GROUP):
        for j in range(OWN):
            old = psi[q * OWN + j]
            one = jnp.where(first, 0.0, lower[q, j])
            two = jnp.where(first, 0.0, lower[q, OWN + j])
            hsend[0, q, j] = one - (slab_prior_row(old) - old)
            hsend[0, q, OWN + j] = two - (slab_prior_lane(old) - old)
            hsend[0, q, PAIRS, pl.ds(j, 1), :] = old[ROWS - 1:, :]
    give_back(0)

    swap = pltpu.make_async_remote_copy(
        src_ref=grad, dst_ref=grad_in, send_sem=g_send, recv_sem=g_recv,
        device_id={"sample": lax.rem(me + 2, GROUP)}, device_id_type=mesh_id,
    )
    gradient = pltpu.make_async_copy(grad, grad_hbm, grad_sem)
    swapped = pltpu.make_async_copy(grad_in, grad_hbm, grad_sem)

    @pl.when(odd == 1)
    def _():
        swap.start()

    @pl.when(odd == 0)
    def _():
        gradient.start()

    def store(p):
        return pltpu.make_async_copy(out.at[p], out_hbm.at[:, :, p], out_sems.at[p])

    def field_one(p, j):
        parts = []
        for s in range(GROUP):
            own = hrecv[p, s, j]
            if s:
                row = hrecv[p, s - 1, PAIRS, pl.ds(j, 1), :]
                own = own - jnp.where(slab_row == 0, row, 0.0)
            parts.append(own)
        return jnp.concatenate(parts, axis=0)

    def field_two(p, j):
        return hrecv[p, :, OWN + j].reshape(NY, NZ)

    objective.wait()
    for copy in backward(PLANES):
        copy.wait_recv()

    @pl.loop(0, PLANES)
    def _(k):
        p = PLANES - 1 - k
        for copy in backward(p):
            copy.wait_recv()

        for j in range(OWN):
            one, two = field_one(p + 1, j), field_two(p + 1, j)
            first_part = (prior_lane(one) - one) - (prior_row(two) - two)
            second_part = field_two(p, j) - two
            third_part = one - field_one(p, j)
            for c, part in enumerate((first_part, second_part, third_part)):
                out[p, j, c] = obj[j, c, p] - part
        store(p).start()

    @pl.when(odd == 1)
    def _():
        swap.wait_recv()
        swapped.start()
        swapped.wait()
        swap.wait_send()

    @pl.when(odd == 0)
    def _():
        gradient.wait()

    up.wait_send()
    down.wait_send()
    for copy in forward_phi() + backward(PLANES):
        copy.wait_send()

    @pl.loop(0, PLANES)
    def _(p):
        store(p).wait()
        for copy in forward(p) + backward(p):
            copy.wait_send()


def local(state_hat, adjoint_hat, objective_hat, density, region):
    f32 = jnp.float32
    hbm = pl.BlockSpec(memory_space=pl.ANY)
    dma = pltpu.SemaphoreType.DMA
    links = (PLANES + 1, GROUP - 1)
    return pl.pallas_call(
        kernel,
        out_shape=(
            jax.ShapeDtypeStruct((OWN, 3, PLANES, NY, NZ), f32),
            jax.ShapeDtypeStruct((PLANES, ROWS, NZ), f32),
        ),
        in_specs=[hbm] * 5,
        out_specs=(hbm, hbm),
        scratch_shapes=[
            pltpu.VMEM((2, PLANES, OWN, 3, NY, NZ), f32),
            pltpu.VMEM((PLANES, 2, OWN, NY, NZ), f32),
            pltpu.VMEM((OWN, 3, PLANES, NY, NZ), f32),
            pltpu.VMEM((PLANES, ROWS, NZ), f32),
            pltpu.VMEM((PLANES, ROWS, NZ), jnp.int32),
            pltpu.VMEM((GROUP, 2 * PAIRS, ROWS, NZ), f32),
            pltpu.VMEM((GROUP, PAIRS, ROWS, NZ), f32),
            pltpu.VMEM((PLANES, GROUP, 2 * PAIRS + 2, ROWS, NZ), f32),
            pltpu.VMEM((PLANES + 1, GROUP, 2 * PAIRS + 2, ROWS, NZ), f32),
            pltpu.VMEM((GROUP, PAIRS + 2, ROWS, NZ), f32),
            pltpu.VMEM((GROUP, PAIRS + 2, ROWS, NZ), f32),
            pltpu.VMEM((PLANES + 1, GROUP, PAIRS + 1, ROWS, NZ), f32),
            pltpu.VMEM((PLANES + 1, GROUP, PAIRS + 1, ROWS, NZ), f32),
            pltpu.VMEM((6, GROUP, OWN, ROWS, NZ), f32),
            pltpu.VMEM((FOLDS, 4, 6, ROWS, NZ), f32),
            pltpu.VMEM((FOLDS, 4, 3, ROWS, NZ), f32),
            pltpu.VMEM((NCOEF, ROWS, NZ), f32),
            pltpu.VMEM((PLANES, OWN, 3, NY, NZ), f32),
            pltpu.VMEM((PLANES, ROWS, NZ), f32),
            pltpu.VMEM((PLANES, ROWS, NZ), f32),
            dma((2, PLANES)), dma, dma((2,)), dma, dma, dma, dma,
            dma(links), dma(links), dma(links), dma(links),
            dma, dma, dma((PLANES,)), dma,
        ],
        compiler_params=pltpu.CompilerParams(
            collective_id=0, has_side_effects=True, vmem_limit_bytes=60 * 1024 * 1024
        ),
    )(state_hat, adjoint_hat, objective_hat, density, region)


def solution(mesh):
    in_specs = (
        P("sample", None, "space", None, None),
        P("sample", None, "space", None, None),
        P("sample", None, "space", None, None),
        P("space", None, None),
        P("space", None, None),
    )
    out_specs = (P("sample", None, "space", None, None), P("space", "sample", None))
    return jax.shard_map(local, mesh=mesh, in_specs=in_specs, out_specs=out_specs, check_vma=False)
```

```python
import math

import jax
import jax.numpy as jnp
from jax import lax
from jax.experimental import pallas as pl
from jax.experimental.pallas import tpu as pltpu
from jax.sharding import PartitionSpec as P

NT = 40
NCOEF = 20
NY = 32
NZ = 128
PLANES = 8
GROUP = 4
OWN = NCOEF // GROUP
ROWS = NY // GROUP
FOLDS = NT // 4 + 1
PAIRS = 2 * OWN
RUN = 4

magnet_reluct = 0.95
iron_floor = 0.05

CLASSES = (
    ("cos", (2, 4, 6, 8, 10)),
    ("cos", (1, 3, 5, 7, 9)),
    ("sin", (2, 4, 6, 8, 10)),
    ("sin", (1, 3, 5, 7, 9)),
)


def coef_index(kind, order):
    return 2 * (order - 1) + (0 if kind == "cos" else 1)


def factor(kind, order, n):
    turn = (n * order) % NT
    quarter = NT // 4
    if kind == "sin":
        turn = (turn - quarter) % NT
    if turn % quarter == 0:
        return (1.0, 0.0, -1.0, 0.0)[turn // quarter]
    return math.cos(2.0 * math.pi * turn / NT)


def combine(terms, constants):
    total = None
    for term, constant in zip(terms, constants):
        if constant == 0.0:
            continue
        if constant == 1.0:
            piece = term
        elif constant == -1.0:
            piece = -term
        else:
            piece = term * jnp.float32(constant)
        total = piece if total is None else total + piece
    return jnp.zeros_like(terms[0]) if total is None else total


def kernel(
    state_hbm, adjoint_hbm, objective_hbm, density_hbm, region_hbm,
    out, grad_out,
    pot, phi, obj, dens, regn, upper, lower, send, recv, phi_send, phi_recv,
    hsend, hrecv, flux, wave, fold, psi, grad,
    in_sems, obj_sem, mat_sems, up_send, up_recv, low_send, low_recv,
    f_send, f_recv, b_send, b_recv, g_send, g_recv,
):
    me = lax.axis_index("sample")
    block = lax.axis_index("space")
    blocks = lax.axis_size("space")
    above = lax.rem(block + 1, blocks)
    below = lax.rem(block + blocks - 1, blocks)
    mesh_id = pl.DeviceIdType.MESH

    def turned(index, where):
        return lax.rem(index + 2 * lax.rem(where // RUN, 2), GROUP)

    odd = lax.rem(block // RUN, 2)
    slab = turned(me, block)
    up_id = {"space": above, "sample": turned(slab, above)}
    down_id = {"space": below, "sample": turned(slab, below)}
    peers = [lax.rem(me + r, GROUP) for r in (2, 3, 1)]

    def load(p):
        return [
            pltpu.make_async_copy(ref.at[:, :, p], pot.at[i, p], in_sems.at[i, p])
            for i, ref in enumerate((state_hbm, adjoint_hbm))
        ]

    @pl.loop(0, PLANES)
    def _(p):
        for copy in load(p):
            copy.start()

    rows = pl.ds(pl.multiple_of(slab * ROWS, ROWS), ROWS)
    material = [
        pltpu.make_async_copy(density_hbm.at[:, rows], dens, mat_sems.at[0]),
        pltpu.make_async_copy(region_hbm.at[:, rows], regn, mat_sems.at[1]),
    ]
    for copy in material:
        copy.start()
    objective = pltpu.make_async_copy(objective_hbm, obj, obj_sem)
    objective.start()

    barrier = pltpu.get_barrier_semaphore()
    for peer in peers:
        pl.semaphore_signal(barrier, inc=1, device_id={"sample": peer}, device_id_type=mesh_id)
    has_above, has_below = block < blocks - 1, block > 0

    @pl.when(has_above)
    def _():
        pl.semaphore_signal(barrier, inc=1, device_id=up_id, device_id_type=mesh_id)

    @pl.when(has_below)
    def _():
        pl.semaphore_signal(barrier, inc=1, device_id=down_id, device_id_type=mesh_id)

    def exchange(source, target, sends, recvs, at):
        return [
            pltpu.make_async_remote_copy(
                src_ref=source(peer), dst_ref=target,
                send_sem=sends.at[at, r], recv_sem=recvs.at[at, r],
                device_id={"sample": peer}, device_id_type=mesh_id,
            )
            for r, peer in enumerate(peers)
        ]

    def forward(p):
        return exchange(lambda peer: send.at[p, turned(peer, block)], recv.at[p, me], f_send, f_recv, p)

    def forward_phi():
        return exchange(lambda peer: phi_send.at[turned(peer, block)], phi_recv.at[me], f_send, f_recv, PLANES)

    def backward(p):
        return exchange(lambda peer: hsend.at[p, peer], hrecv.at[p, slab], b_send, b_recv, p)

    row_id = lax.broadcasted_iota(jnp.int32, (NY, NZ), 0)
    lane_id = lax.broadcasted_iota(jnp.int32, (NY, NZ), 1)
    slab_row = lax.broadcasted_iota(jnp.int32, (ROWS, NZ), 0)
    slab_lane = lax.broadcasted_iota(jnp.int32, (ROWS, NZ), 1)

    def next_row(a):
        return jnp.where(row_id == NY - 1, 0.0, pltpu.roll(a, NY - 1, 0))

    def next_lane(a):
        return jnp.where(lane_id == NZ - 1, 0.0, pltpu.roll(a, NZ - 1, 1))

    def prior_row(a):
        return jnp.where(row_id == 0, 0.0, pltpu.roll(a, 1, 0))

    def prior_lane(a):
        return jnp.where(lane_id == 0, 0.0, pltpu.roll(a, 1, 1))

    def slab_next_row(a, row):
        return jnp.where(slab_row == ROWS - 1, row, pltpu.roll(a, ROWS - 1, 0))

    def slab_next_lane(a):
        return jnp.where(slab_lane == NZ - 1, 0.0, pltpu.roll(a, NZ - 1, 1))

    def slab_prior_row(a):
        return jnp.where(slab_row == 0, 0.0, pltpu.roll(a, 1, 0))

    def slab_prior_lane(a):
        return jnp.where(slab_lane == 0, 0.0, pltpu.roll(a, 1, 1))

    def put_rows(ref, first, at, a):
        for s in range(GROUP - 1):
            ref[s, first + at // ROWS, pl.ds(at % ROWS, 1), :] = a[ROWS * (s + 1):ROWS * (s + 1) + 1, :]

    nothing = jnp.zeros((2, ROWS, NZ), jnp.float32)
    phi_send[GROUP - 1, pl.ds(PAIRS, 2)] = nothing

    @pl.loop(0, PLANES)
    def _(p):
        send[p, GROUP - 1, pl.ds(2 * PAIRS, 2)] = nothing

    for copy in load(0):
        copy.wait()
    for i in range(2):
        for j in range(OWN):
            at = i * OWN + j
            one, two = pot[i, 0, j, 1], pot[i, 0, j, 2]
            send[0, :, at] = one.reshape(GROUP, ROWS, NZ)
            send[0, :, PAIRS + at] = two.reshape(GROUP, ROWS, NZ)
            put_rows(send.at[0], 2 * PAIRS, at, two)
            phi[0, i, j] = pot[i, 0, j, 0]
    recv[0, me] = send[0, slab]
    pl.semaphore_wait(barrier, GROUP - 1 + has_above.astype(jnp.int32) + has_below.astype(jnp.int32))
    for copy in forward(0):
        copy.start()

    @pl.loop(1, PLANES)
    def _(p):
        for copy in load(p):
            copy.wait()

        for i in range(2):
            @pl.loop(0, OWN)
            def _(j):
                phi[p, i, j] = phi[p - 1, i, j] + pot[i, p, j, 0]

    for i in range(2):
        for j in range(OWN):
            at = i * OWN + j
            top = phi[PLANES - 1, i, j]
            phi_send[:, at] = top.reshape(GROUP, ROWS, NZ)
            put_rows(phi_send, PAIRS, at, top)
    phi_recv[me] = phi_send[slab]
    for copy in forward_phi():
        copy.start()

    @pl.loop(0, PLANES - 1)
    def _(k):
        p = PLANES - 1 - k
        for i in range(2):
            for j in range(OWN):
                at = i * OWN + j
                under = phi[p - 1, i, j]
                one = pot[i, p, j, 1] - (next_row(under) - under)
                two = pot[i, p, j, 2] - (next_lane(under) - under)
                send[p, :, at] = one.reshape(GROUP, ROWS, NZ)
                send[p, :, PAIRS + at] = two.reshape(GROUP, ROWS, NZ)
                put_rows(send.at[p], 2 * PAIRS, at, two)
        recv[p, me] = send[p, slab]
        for copy in forward(p):
            copy.start()

    for copy in forward(0):
        copy.wait_recv()
    up = pltpu.make_async_remote_copy(
        src_ref=recv.at[0, :, pl.ds(0, 2 * PAIRS)], dst_ref=upper,
        send_sem=up_send, recv_sem=up_recv, device_id=down_id, device_id_type=mesh_id,
    )

    @pl.when(has_below)
    def _():
        up.start()

    @pl.when(jnp.logical_not(has_above))
    def _():
        upper[...] = jnp.zeros_like(upper)

    @pl.when(jnp.logical_not(has_below))
    def _():
        lower[...] = jnp.zeros_like(lower)

    for copy in material:
        copy.wait()
    psi[...] = jnp.zeros_like(psi)
    for copy in forward_phi():
        copy.wait_recv()

    @pl.when(has_above)
    def _():
        up.wait_recv()

    @pl.loop(0, GROUP)
    def _(q):
        for at in range(PAIRS):
            top = phi_recv[q, at]
            row = phi_recv[q, PAIRS + at // ROWS, pl.ds(at % ROWS, 1), :]
            one = upper[q, at]
            two = upper[q, PAIRS + at]
            recv[PLANES, q, at] = one - (slab_next_row(top, row) - top)
            recv[PLANES, q, PAIRS + at] = two - (slab_next_lane(top) - top)

    down = pltpu.make_async_remote_copy(
        src_ref=hsend.at[PLANES, :, pl.ds(0, PAIRS)], dst_ref=lower,
        send_sem=low_send, recv_sem=low_recv, device_id=up_id, device_id_type=mesh_id,
    )

    def nonlinear(p):
        @pl.loop(0, GROUP)
        def _(q):
            for i in range(2):
                for j in range(OWN):
                    at = i * OWN + j
                    one, two = recv[p, q, at], recv[p, q, PAIRS + at]
                    row = recv[p, q, 2 * PAIRS + at // ROWS, pl.ds(at % ROWS, 1), :]
                    flux[3 * i, q, j] = (slab_next_row(two, row) - two) - (slab_next_lane(one) - one)
                    flux[3 * i + 1, q, j] = two - recv[p + 1, q, PAIRS + at]
                    flux[3 * i + 2, q, j] = recv[p + 1, q, at] - one

        @pl.loop(0, 6)
        def _(pc):
            for t, (kind, orders) in enumerate(CLASSES):
                where = [coef_index(kind, m) for m in orders]
                terms = [flux[pc, c // OWN, c % OWN] for c in where]
                for n in range(FOLDS):
                    wave[n, t, pc] = combine(terms, [factor(kind, m, n) for m in orders])

        density, region = dens[p], regn[p]
        iron = region == 0
        share = jnp.where(iron, density * density * density, 0.0) * jnp.float32(1.0 - iron_floor)
        slope = jnp.where(iron, 3.0 * density * density, 0.0)
        base = jnp.where(region == 1, jnp.float32(magnet_reluct), jnp.float32(1.0))

        def samples(n, total):
            state = [[], [], []]
            adjoint = [[], [], []]
            for pc in range(6):
                ce, co, se, so = (wave[n, t, pc] for t in range(4))
                a, b, d, f = ce + co, ce - co, se + so, se - so
                (state if pc < 3 else adjoint)[pc % 3] = (a + d, a - d, b - f, b + f)
            field = [[], [], []]
            part = None
            for v in range(4):
                s = [state[c][v] for c in range(3)]
                g = [adjoint[c][v] for c in range(3)]
                square = s[0] * s[0] + s[1] * s[1] + s[2] * s[2]
                inner = s[0] * g[0] + s[1] * g[1] + s[2] * g[2]
                r = 1.0 / (square + 1.0)
                t = share * r
                ri = r * inner
                nu = base - t
                mu = (t + t) * ri
                part = ri if part is None else part + ri
                for c in range(3):
                    field[c].append(nu * g[c] + mu * s[c])
            for c in range(3):
                w, x, y, z = field[c]
                a, d = w + x, w - x
                b, f = z + y, z - y
                fold[n, 0, c] = a + b
                fold[n, 1, c] = a - b
                fold[n, 2, c] = d + f
                fold[n, 3, c] = d - f
            ends = (n == 0) | (n == FOLDS - 1)
            return total + part * jnp.where(ends, 0.5, 1.0)

        total = lax.fori_loop(0, FOLDS, samples, jnp.zeros((ROWS, NZ), jnp.float32))
        grad[p] = total * slope * jnp.float32((1.0 - iron_floor) / NT)

        for t, (kind, orders) in enumerate(CLASSES):
            for c in (1, 2, 0):
                terms = [fold[n, t, c] for n in range(FOLDS)]
                for m in orders:
                    scales = [
                        factor(kind, m, n) * (1.0 if 0 < n < FOLDS - 1 else 0.5) * 2.0 / NT
                        for n in range(FOLDS)
                    ]
                    got = combine(terms, scales)
                    at = coef_index(kind, m)
                    q, j = at // OWN, at % OWN
                    old = psi[at]
                    if c == 1:
                        hsend[p + 1, q, j] = got - (slab_prior_row(old) - old)
                    elif c == 2:
                        hsend[p + 1, q, OWN + j] = got - (slab_prior_lane(old) - old)
                    else:
                        hsend[p + 1, q, PAIRS, pl.ds(j, 1), :] = old[ROWS - 1:, :]
                        psi[at] = old + got

    def give_back(p):
        hrecv[p, slab] = hsend[p, me]
        for copy in backward(p):
            copy.start()

    @pl.loop(0, PLANES)
    def _(k):
        p = PLANES - 1 - k

        @pl.when(p > 0)
        def _():
            for copy in forward(p):
                copy.wait_recv()

        nonlinear(p)

        @pl.when((k == 0) & has_above)
        def _():
            down.start()

        give_back(p + 1)

    @pl.when(has_below)
    def _():
        down.wait_recv()

    for q in range(GROUP):
        for j in range(OWN):
            old = psi[q * OWN + j]
            one = lower[q, j]
            two = lower[q, OWN + j]
            hsend[0, q, j] = one - (slab_prior_row(old) - old)
            hsend[0, q, OWN + j] = two - (slab_prior_lane(old) - old)
            hsend[0, q, PAIRS, pl.ds(j, 1), :] = old[ROWS - 1:, :]
    give_back(0)

    swap = pltpu.make_async_remote_copy(
        src_ref=grad, dst_ref=grad_out, send_sem=g_send, recv_sem=g_recv,
        device_id={"sample": lax.rem(me + 2, GROUP)}, device_id_type=mesh_id,
    )

    @pl.when(odd == 1)
    def _():
        swap.start()

    @pl.when(odd == 0)
    def _():
        grad_out[...] = grad[...]

    def field_one(p, j):
        parts = []
        for s in range(GROUP):
            own = hrecv[p, s, j]
            if s:
                row = hrecv[p, s - 1, PAIRS, pl.ds(j, 1), :]
                own = own - jnp.where(slab_row == 0, row, 0.0)
            parts.append(own)
        return jnp.concatenate(parts, axis=0)

    def field_two(p, j):
        return hrecv[p, :, OWN + j].reshape(NY, NZ)

    objective.wait()
    for copy in backward(PLANES):
        copy.wait_recv()

    @pl.loop(0, PLANES)
    def _(k):
        p = PLANES - 1 - k
        for copy in backward(p):
            copy.wait_recv()

        for j in range(OWN):
            one, two = field_one(p + 1, j), field_two(p + 1, j)
            first_part = (prior_lane(one) - one) - (prior_row(two) - two)
            second_part = field_two(p, j) - two
            third_part = one - field_one(p, j)
            for c, part in enumerate((first_part, second_part, third_part)):
                out[j, c, p] = obj[j, c, p] - part

    @pl.when(odd == 1)
    def _():
        swap.wait()

    @pl.when(has_below)
    def _():
        up.wait_send()

    @pl.when(has_above)
    def _():
        down.wait_send()

    for copy in forward_phi() + backward(PLANES):
        copy.wait_send()

    @pl.loop(0, PLANES)
    def _(p):
        for copy in forward(p) + backward(p):
            copy.wait_send()


def write_out(held, held_grad, out_hbm, grad_hbm, sems):
    copies = [pltpu.make_async_copy(held.at[j], out_hbm.at[j], sems.at[j]) for j in range(OWN)]
    copies.append(pltpu.make_async_copy(held_grad, grad_hbm, sems.at[OWN]))
    for copy in copies:
        copy.start()
    for copy in copies:
        copy.wait()


def local(state_hat, adjoint_hat, objective_hat, density, region):
    f32 = jnp.float32
    hbm = pl.BlockSpec(memory_space=pl.ANY)
    dma = pltpu.SemaphoreType.DMA
    links = (PLANES + 1, GROUP - 1)
    residual = (OWN, 3, PLANES, NY, NZ)
    gradient = (PLANES, ROWS, NZ)
    vmem = pl.BlockSpec(memory_space=pltpu.VMEM)
    held = pl.pallas_call(
        kernel,
        out_shape=(pltpu.VMEM(residual, f32), pltpu.VMEM(gradient, f32)),
        in_specs=[hbm] * 5,
        out_specs=(vmem, vmem),
        scratch_shapes=[
            pltpu.VMEM((2, PLANES, OWN, 3, NY, NZ), f32),
            pltpu.VMEM((PLANES, 2, OWN, NY, NZ), f32),
            pltpu.VMEM((OWN, 3, PLANES, NY, NZ), f32),
            pltpu.VMEM((PLANES, ROWS, NZ), f32),
            pltpu.VMEM((PLANES, ROWS, NZ), jnp.int32),
            pltpu.VMEM((GROUP, 2 * PAIRS, ROWS, NZ), f32),
            pltpu.VMEM((GROUP, PAIRS, ROWS, NZ), f32),
            pltpu.VMEM((PLANES, GROUP, 2 * PAIRS + 2, ROWS, NZ), f32),
            pltpu.VMEM((PLANES + 1, GROUP, 2 * PAIRS + 2, ROWS, NZ), f32),
            pltpu.VMEM((GROUP, PAIRS + 2, ROWS, NZ), f32),
            pltpu.VMEM((GROUP, PAIRS + 2, ROWS, NZ), f32),
            pltpu.VMEM((PLANES + 1, GROUP, PAIRS + 1, ROWS, NZ), f32),
            pltpu.VMEM((PLANES + 1, GROUP, PAIRS + 1, ROWS, NZ), f32),
            pltpu.VMEM((6, GROUP, OWN, ROWS, NZ), f32),
            pltpu.VMEM((FOLDS, 4, 6, ROWS, NZ), f32),
            pltpu.VMEM((FOLDS, 4, 3, ROWS, NZ), f32),
            pltpu.VMEM((NCOEF, ROWS, NZ), f32),
            pltpu.VMEM((PLANES, ROWS, NZ), f32),
            dma((2, PLANES)), dma, dma((2,)), dma, dma, dma, dma,
            dma(links), dma(links), dma(links), dma(links),
            dma, dma,
        ],
        compiler_params=pltpu.CompilerParams(
            collective_id=0, has_side_effects=True, vmem_limit_bytes=60 * 1024 * 1024
        ),
    )(state_hat, adjoint_hat, objective_hat, density, region)
    return pl.pallas_call(
        write_out,
        out_shape=(jax.ShapeDtypeStruct(residual, f32), jax.ShapeDtypeStruct(gradient, f32)),
        in_specs=[vmem, vmem],
        out_specs=(hbm, hbm),
        scratch_shapes=[dma((OWN + 1,))],
        compiler_params=pltpu.CompilerParams(vmem_limit_bytes=1024 * 1024),
    )(*held)


def solution(mesh):
    in_specs = (
        P("sample", None, "space", None, None),
        P("sample", None, "space", None, None),
        P("sample", None, "space", None, None),
        P("space", None, None),
        P("space", None, None),
    )
    out_specs = (P("sample", None, "space", None, None), P("space", "sample", None))
    return jax.shard_map(local, mesh=mesh, in_specs=in_specs, out_specs=out_specs, check_vma=False)
```

```python
import math

import jax
import jax.numpy as jnp
from jax import lax
from jax.experimental import pallas as pl
from jax.experimental.pallas import tpu as pltpu
from jax.sharding import PartitionSpec as P

NT = 40
NCOEF = 20
NY = 32
NZ = 128
PLANES = 8
GROUP = 4
OWN = NCOEF // GROUP
ROWS = NY // GROUP
FOLDS = NT // 4 + 1
PAIRS = 2 * OWN
RUN = 4

magnet_reluct = 0.95
iron_floor = 0.05

CLASSES = (
    ("cos", (2, 4, 6, 8, 10)),
    ("cos", (1, 3, 5, 7, 9)),
    ("sin", (2, 4, 6, 8, 10)),
    ("sin", (1, 3, 5, 7, 9)),
)


def coef_index(kind, order):
    return 2 * (order - 1) + (0 if kind == "cos" else 1)


def factor(kind, order, n):
    turn = (n * order) % NT
    quarter = NT // 4
    if kind == "sin":
        turn = (turn - quarter) % NT
    if turn % quarter == 0:
        return (1.0, 0.0, -1.0, 0.0)[turn // quarter]
    return math.cos(2.0 * math.pi * turn / NT)


def combine(terms, constants):
    total = None
    for term, constant in zip(terms, constants):
        if constant == 0.0:
            continue
        if constant == 1.0:
            piece = term
        elif constant == -1.0:
            piece = -term
        else:
            piece = term * jnp.float32(constant)
        total = piece if total is None else total + piece
    return jnp.zeros_like(terms[0]) if total is None else total


def kernel(
    state_hbm, adjoint_hbm, objective_hbm, density_hbm, region_hbm,
    out, grad_out,
    pot, phi, obj, dens, regn, upper, lower, send, recv, phi_send, phi_recv, edge,
    hsend, hrecv, flux, wave, fold, psi, psi_edge, fix, grad,
    in_sems, obj_sem, mat_sems, own_sems, up_send, up_recv, low_send, low_recv,
    f_send, f_recv, b_send, b_recv, e_send, e_recv, c_send, c_recv,
    s_send, s_recv, x_send, x_recv, g_send, g_recv, ready,
):
    me = lax.axis_index("sample")
    block = lax.axis_index("space")
    blocks = lax.axis_size("space")
    above = lax.rem(block + 1, blocks)
    below = lax.rem(block + blocks - 1, blocks)
    has_above, has_below = block < blocks - 1, block > 0
    mesh_id = pl.DeviceIdType.MESH

    def turned(index, where):
        return lax.rem(index + 2 * lax.rem(where // RUN, 2), GROUP)

    swaps = lax.rem(block // RUN, 2) == 1
    slab = turned(me, block)
    odd_slab = lax.rem(me, 2) == 1
    even_slab = jnp.logical_not(odd_slab)
    partner = me + 1 - 2 * lax.rem(me, 2)
    middle = turned(1, block)
    is_middle = me == middle
    off_middle = me != middle
    up_id = {"space": above, "sample": turned(slab, above)}
    down_id = {"space": below, "sample": turned(slab, below)}
    peers = [lax.rem(me + r, GROUP) for r in (2, 3, 1)]
    arguments = (state_hbm, adjoint_hbm)

    def to_sample(source, target, send_sem, recv_sem, peer):
        return pltpu.make_async_remote_copy(
            src_ref=source, dst_ref=target, send_sem=send_sem, recv_sem=recv_sem,
            device_id={"sample": peer}, device_id_type=mesh_id,
        )

    barrier = pltpu.get_barrier_semaphore()
    for peer in peers:
        pl.semaphore_signal(barrier, inc=1, device_id={"sample": peer}, device_id_type=mesh_id)

    @pl.when(has_below)
    def _():
        pl.semaphore_signal(barrier, inc=1, device_id=down_id, device_id_type=mesh_id)

    def slab_rows(s):
        return pl.ds(pl.multiple_of(s * ROWS, ROWS), ROWS)

    def load(p):
        return [
            pltpu.make_async_copy(ref.at[:, :, p], pot.at[i, p], in_sems.at[i, p])
            for i, ref in enumerate(arguments)
        ]

    own = [
        pltpu.make_async_copy(
            ref.at[:, pl.ds(1, 2), 0, slab_rows(slab)], recv.at[0, me, pl.ds(i * OWN, OWN)], own_sems.at[i]
        )
        for i, ref in enumerate(arguments)
    ]
    for copy in own:
        copy.start()

    @pl.loop(0, PLANES)
    def _(p):
        for copy in load(p):
            copy.start()

    material = [
        pltpu.make_async_copy(density_hbm.at[:, slab_rows(slab)], dens, mat_sems.at[0]),
        pltpu.make_async_copy(region_hbm.at[:, slab_rows(slab)], regn, mat_sems.at[1]),
    ]
    for copy in material:
        copy.start()
    objective = pltpu.make_async_copy(objective_hbm, obj, obj_sem)
    objective.start()

    def forward_first():
        return [
            to_sample(
                ref.at[:, pl.ds(1, 2), 0, slab_rows(turned(peer, block))],
                recv.at[0, me, pl.ds(i * OWN, OWN)],
                f_send.at[i * (PLANES + 1), r], f_recv.at[i * (PLANES + 1), r], peer,
            )
            for r, peer in enumerate(peers)
            for i, ref in enumerate(arguments)
        ]

    def forward(p):
        return [
            to_sample(
                send.at[p, turned(peer, block)], recv.at[p, me], f_send.at[p, r], f_recv.at[p, r], peer
            )
            for r, peer in enumerate(peers)
        ]

    def forward_phi():
        return [
            to_sample(
                phi_send.at[turned(peer, block)], phi_recv.at[me],
                f_send.at[PLANES, r], f_recv.at[PLANES, r], peer,
            )
            for r, peer in enumerate(peers)
        ]

    def backward(p):
        return [
            to_sample(hsend.at[p, peer], hrecv.at[p, slab], b_send.at[p, r], b_recv.at[p, r], peer)
            for r, peer in enumerate(peers)
        ]

    top_row, end_row = pl.ds(0, 1), pl.ds(ROWS - 1, 1)

    def middle_row(p, q):
        source = send.at[p, 2, :, 1, top_row]
        return to_sample(source, edge.at[p, q, :, top_row], e_send.at[p], e_recv.at[p, q], middle)

    def middle_phi(q):
        source = phi_send.at[2, :, top_row]
        return to_sample(source, edge.at[PLANES, q, :, top_row], e_send.at[PLANES], e_recv.at[PLANES, q], middle)

    def chip_row(p):
        return to_sample(recv.at[p, :, :, 1, top_row], edge.at[p, :, :, top_row], c_send.at[p], c_recv.at[p], partner)

    def chip_phi():
        return to_sample(
            phi_recv.at[:, :, top_row], edge.at[PLANES, :, :, top_row],
            c_send.at[PLANES], c_recv.at[PLANES], partner,
        )

    def psi_row(p):
        return to_sample(psi.at[p, :, end_row], psi_edge.at[p, :, end_row], s_send.at[p], s_recv.at[p], partner)

    def fix_row(p):
        return [
            to_sample(psi.at[p, pl.ds(peer * OWN, OWN), end_row], fix.at[p, :, end_row], x_send.at[p, r], x_recv.at[p], peer)
            for r, peer in enumerate(peers)
        ]

    row_id = lax.broadcasted_iota(jnp.int32, (NY, NZ), 0)
    lane_id = lax.broadcasted_iota(jnp.int32, (NY, NZ), 1)
    slab_row = lax.broadcasted_iota(jnp.int32, (ROWS, NZ), 0)
    slab_lane = lax.broadcasted_iota(jnp.int32, (ROWS, NZ), 1)

    def next_row(a):
        return jnp.where(row_id == NY - 1, 0.0, pltpu.roll(a, NY - 1, 0))

    def next_lane(a):
        return jnp.where(lane_id == NZ - 1, 0.0, pltpu.roll(a, NZ - 1, 1))

    def prior_row(a):
        return jnp.where(row_id == 0, 0.0, pltpu.roll(a, 1, 0))

    def prior_lane(a):
        return jnp.where(lane_id == 0, 0.0, pltpu.roll(a, 1, 1))

    def slab_next_row(a, row):
        return jnp.where(slab_row == ROWS - 1, row, pltpu.roll(a, ROWS - 1, 0))

    def slab_next_lane(a):
        return jnp.where(slab_lane == NZ - 1, 0.0, pltpu.roll(a, NZ - 1, 1))

    def slab_prior_row(a, row):
        return jnp.where(slab_row == 0, row, pltpu.roll(a, 1, 0))

    def slab_prior_lane(a):
        return jnp.where(slab_lane == 0, 0.0, pltpu.roll(a, 1, 1))

    pl.semaphore_wait(barrier, GROUP - 1 + has_above.astype(jnp.int32))
    for copy in forward_first():
        copy.start()

    @pl.when(has_above)
    def _():
        pl.semaphore_signal(ready, inc=1, device_id=up_id, device_id_type=mesh_id)

    for copy in load(0):
        copy.wait()
    for i in range(2):
        for j in range(OWN):
            phi[0, i, j] = pot[i, 0, j, 0]
            send[0, 2, i * OWN + j, 1] = pot[i, 0, j, 2, pl.ds(2 * ROWS, ROWS), :]

    @pl.loop(1, PLANES)
    def _(p):
        for copy in load(p):
            copy.wait()

        for i in range(2):
            @pl.loop(0, OWN)
            def _(j):
                phi[p, i, j] = phi[p - 1, i, j] + pot[i, p, j, 0]

    for i in range(2):
        for j in range(OWN):
            phi_send[:, i * OWN + j] = phi[PLANES - 1, i, j].reshape(GROUP, ROWS, NZ)
    phi_recv[me] = phi_send[slab]
    for copy in forward_phi():
        copy.start()

    @pl.when(off_middle)
    def _():
        middle_phi(me).start()
        middle_row(0, me).start()

    @pl.when(is_middle)
    def _():
        for ij in range(PAIRS):
            edge[PLANES, me, ij] = phi_send[2, ij]
            edge[0, me, ij] = send[0, 2, ij, 1]

    @pl.loop(0, PLANES - 1)
    def _(k):
        p = PLANES - 1 - k
        for i in range(2):
            for j in range(OWN):
                under = phi[p - 1, i, j]
                one = pot[i, p, j, 1] - (next_row(under) - under)
                two = pot[i, p, j, 2] - (next_lane(under) - under)
                send[p, :, i * OWN + j, 0] = one.reshape(GROUP, ROWS, NZ)
                send[p, :, i * OWN + j, 1] = two.reshape(GROUP, ROWS, NZ)
        for copy in forward(p):
            copy.start()

        @pl.when(off_middle)
        def _():
            middle_row(p, me).start()

        @pl.when(is_middle)
        def _():
            for ij in range(PAIRS):
                edge[p, me, ij] = send[p, 2, ij, 1]

        recv[p, me] = send[p, slab]

    psi[PLANES] = jnp.zeros((NCOEF, ROWS, NZ), jnp.float32)
    psi_edge[PLANES] = jnp.zeros((NCOEF, ROWS, NZ), jnp.float32)
    fix[PLANES] = jnp.zeros((OWN, ROWS, NZ), jnp.float32)

    @pl.when(even_slab)
    def _():
        @pl.loop(0, PLANES)
        def _(p):
            psi_edge[p] = jnp.zeros((NCOEF, ROWS, NZ), jnp.float32)

    @pl.when(slab == GROUP - 1)
    def _():
        @pl.loop(0, PLANES + 1)
        def _(p):
            edge[p] = jnp.zeros((GROUP, PAIRS, ROWS, NZ), jnp.float32)

    @pl.when(jnp.logical_not(has_above))
    def _():
        upper[...] = jnp.zeros_like(upper)

    @pl.when(jnp.logical_not(has_below))
    def _():
        lower[...] = jnp.zeros_like(lower)

    for copy in own:
        copy.wait()
    for copy in forward_first():
        copy.wait_recv()
    up = pltpu.make_async_remote_copy(
        src_ref=recv.at[0], dst_ref=upper,
        send_sem=up_send, recv_sem=up_recv, device_id=down_id, device_id_type=mesh_id,
    )

    @pl.when(has_below)
    def _():
        pl.semaphore_wait(ready, 1)
        up.start()

    for copy in material:
        copy.wait()
    for copy in forward_phi():
        copy.wait_recv()

    @pl.when(odd_slab)
    def _():
        chip_phi().start()
        chip_row(0).start()

    @pl.when(is_middle)
    def _():
        for peer in peers:
            middle_phi(peer).wait_recv()
            middle_row(0, peer).wait_recv()

    @pl.when(even_slab)
    def _():
        chip_phi().wait_recv()
        chip_row(0).wait_recv()

    @pl.when(has_above)
    def _():
        up.wait_recv()

    @pl.loop(0, GROUP)
    def _(q):
        for ij in range(PAIRS):
            top = phi_recv[q, ij]
            row = edge[PLANES, q, ij, top_row, :]
            recv[PLANES, q, ij, 0] = upper[q, ij, 0] - (slab_next_row(top, row) - top)
            recv[PLANES, q, ij, 1] = upper[q, ij, 1] - (slab_next_lane(top) - top)

    down = pltpu.make_async_remote_copy(
        src_ref=hsend.at[PLANES], dst_ref=lower,
        send_sem=low_send, recv_sem=low_recv, device_id=up_id, device_id_type=mesh_id,
    )

    def nonlinear(p):
        @pl.loop(0, GROUP)
        def _(q):
            for i in range(2):
                for j in range(OWN):
                    ij = i * OWN + j
                    one, two = recv[p, q, ij, 0], recv[p, q, ij, 1]
                    row = edge[p, q, ij, top_row, :]
                    flux[3 * i, q, j] = (slab_next_row(two, row) - two) - (slab_next_lane(one) - one)
                    flux[3 * i + 1, q, j] = two - recv[p + 1, q, ij, 1]
                    flux[3 * i + 2, q, j] = recv[p + 1, q, ij, 0] - one

        @pl.loop(0, 6)
        def _(pc):
            for t, (kind, orders) in enumerate(CLASSES):
                where = [coef_index(kind, m) for m in orders]
                terms = [flux[pc, c // OWN, c % OWN] for c in where]
                for n in range(FOLDS):
                    wave[n, t, pc] = combine(terms, [factor(kind, m, n) for m in orders])

        density, region = dens[p], regn[p]
        iron = region == 0
        share = jnp.where(iron, density * density * density, 0.0) * jnp.float32(1.0 - iron_floor)
        slope = jnp.where(iron, 3.0 * density * density, 0.0)
        base = jnp.where(region == 1, jnp.float32(magnet_reluct), jnp.float32(1.0))

        def samples(n, total):
            state = [[], [], []]
            adjoint = [[], [], []]
            for pc in range(6):
                ce, co, se, so = (wave[n, t, pc] for t in range(4))
                a, b, d, f = ce + co, ce - co, se + so, se - so
                (state if pc < 3 else adjoint)[pc % 3] = (a + d, a - d, b - f, b + f)
            field = [[], [], []]
            part = None
            for v in range(4):
                s = [state[c][v] for c in range(3)]
                g = [adjoint[c][v] for c in range(3)]
                square = s[0] * s[0] + s[1] * s[1] + s[2] * s[2]
                inner = s[0] * g[0] + s[1] * g[1] + s[2] * g[2]
                r = 1.0 / (square + 1.0)
                t = share * r
                ri = r * inner
                nu = base - t
                mu = (t + t) * ri
                part = ri if part is None else part + ri
                for c in range(3):
                    field[c].append(nu * g[c] + mu * s[c])
            for c in range(3):
                w, x, y, z = field[c]
                a, d = w + x, w - x
                b, f = z + y, z - y
                fold[n, 0, c] = a + b
                fold[n, 1, c] = a - b
                fold[n, 2, c] = d + f
                fold[n, 3, c] = d - f
            ends = (n == 0) | (n == FOLDS - 1)
            return total + part * jnp.where(ends, 0.5, 1.0)

        total = lax.fori_loop(0, FOLDS, samples, jnp.zeros((ROWS, NZ), jnp.float32))
        grad[p] = total * slope * jnp.float32((1.0 - iron_floor) / NT)

        @pl.when(odd_slab & (p < PLANES - 1))
        def _():
            psi_row(p + 1).wait_recv()

        for t, (kind, orders) in enumerate(CLASSES):
            for c in (1, 2, 0):
                terms = [fold[n, t, c] for n in range(FOLDS)]
                for m in orders:
                    scales = [
                        factor(kind, m, n) * (1.0 if 0 < n < FOLDS - 1 else 0.5) * 2.0 / NT
                        for n in range(FOLDS)
                    ]
                    got = combine(terms, scales)
                    at = coef_index(kind, m)
                    q, j = at // OWN, at % OWN
                    old = psi[p + 1, at]
                    if c == 1:
                        row = psi_edge[p + 1, at, end_row, :]
                        hsend[p + 1, q, j, 0] = got - (slab_prior_row(old, row) - old)
                    elif c == 2:
                        hsend[p + 1, q, j, 1] = got - (slab_prior_lane(old) - old)
                    else:
                        psi[p, at] = old + got

    def give_back(u):
        for copy in backward(u):
            copy.start()

        @pl.when(is_middle & (u < PLANES))
        def _():
            for copy in fix_row(u):
                copy.start()

            fix[u] = psi[u, pl.ds(me * OWN, OWN)]

        hrecv[u, slab] = hsend[u, me]

    @pl.loop(0, PLANES)
    def _(k):
        p = PLANES - 1 - k

        @pl.when(p > 0)
        def _():
            for copy in forward(p):
                copy.wait_recv()

            @pl.when(odd_slab)
            def _():
                chip_row(p).start()

            @pl.when(is_middle)
            def _():
                for peer in peers:
                    middle_row(p, peer).wait_recv()

            @pl.when(even_slab)
            def _():
                chip_row(p).wait_recv()

        nonlinear(p)

        @pl.when(even_slab)
        def _():
            psi_row(p).start()

        @pl.when((k == 0) & has_above)
        def _():
            down.start()

        give_back(p + 1)

    @pl.when(has_below)
    def _():
        down.wait_recv()

    @pl.when(odd_slab)
    def _():
        psi_row(0).wait_recv()

    for q in range(GROUP):
        for j in range(OWN):
            old = psi[0, q * OWN + j]
            row = psi_edge[0, q * OWN + j, end_row, :]
            hsend[0, q, j, 0] = lower[q, j, 0] - (slab_prior_row(old, row) - old)
            hsend[0, q, j, 1] = lower[q, j, 1] - (slab_prior_lane(old) - old)
    give_back(0)

    swap = to_sample(grad, grad_out, g_send, g_recv, lax.rem(me + 2, GROUP))

    @pl.when(swaps)
    def _():
        swap.start()

    @pl.when(jnp.logical_not(swaps))
    def _():
        grad_out[...] = grad[...]

    def arrived(u):
        for copy in backward(u):
            copy.wait_recv()

        @pl.when(off_middle & (u < PLANES))
        def _():
            fix_row(u)[0].wait_recv()

    def field_one(u, j):
        parts = [hrecv[u, s, j, 0] for s in range(GROUP)]
        parts[2] = parts[2] - jnp.where(slab_row == 0, fix[u, j, end_row, :], 0.0)
        return jnp.concatenate(parts, axis=0)

    def field_two(u, j):
        return hrecv[u, :, j, 1].reshape(NY, NZ)

    objective.wait()
    arrived(PLANES)

    @pl.loop(0, PLANES)
    def _(k):
        p = PLANES - 1 - k
        arrived(p)

        for j in range(OWN):
            one, two = field_one(p + 1, j), field_two(p + 1, j)
            first_part = (prior_lane(one) - one) - (prior_row(two) - two)
            second_part = field_two(p, j) - two
            third_part = one - field_one(p, j)
            for c, part in enumerate((first_part, second_part, third_part)):
                out[j, c, p] = obj[j, c, p] - part

    @pl.when(swaps)
    def _():
        swap.wait()

    @pl.when(has_below)
    def _():
        up.wait_send()

    @pl.when(has_above)
    def _():
        down.wait_send()

    for copy in forward_first() + forward_phi() + backward(PLANES):
        copy.wait_send()

    @pl.when(off_middle)
    def _():
        middle_phi(me).wait_send()

    @pl.when(odd_slab)
    def _():
        chip_phi().wait_send()

    @pl.loop(0, PLANES)
    def _(p):
        for copy in backward(p):
            copy.wait_send()

        @pl.when(p > 0)
        def _():
            for copy in forward(p):
                copy.wait_send()

        @pl.when(off_middle)
        def _():
            middle_row(p, me).wait_send()

        @pl.when(odd_slab)
        def _():
            chip_row(p).wait_send()

        @pl.when(even_slab)
        def _():
            psi_row(p).wait_send()

        @pl.when(is_middle)
        def _():
            for copy in fix_row(p):
                copy.wait_send()


def write_out(held, held_grad, out_hbm, grad_hbm, sems):
    copies = [pltpu.make_async_copy(held.at[j], out_hbm.at[j], sems.at[j]) for j in range(OWN)]
    copies.append(pltpu.make_async_copy(held_grad, grad_hbm, sems.at[OWN]))
    for copy in copies:
        copy.start()
    for copy in copies:
        copy.wait()


def local(state_hat, adjoint_hat, objective_hat, density, region):
    f32 = jnp.float32
    hbm = pl.BlockSpec(memory_space=pl.ANY)
    dma = pltpu.SemaphoreType.DMA
    links = (PLANES + 1, GROUP - 1)
    residual = (OWN, 3, PLANES, NY, NZ)
    gradient = (PLANES, ROWS, NZ)
    vmem = pl.BlockSpec(memory_space=pltpu.VMEM)
    held = pl.pallas_call(
        kernel,
        out_shape=(pltpu.VMEM(residual, f32), pltpu.VMEM(gradient, f32)),
        in_specs=[hbm] * 5,
        out_specs=(vmem, vmem),
        scratch_shapes=[
            pltpu.VMEM((2, PLANES, OWN, 3, NY, NZ), f32),
            pltpu.VMEM((PLANES, 2, OWN, NY, NZ), f32),
            pltpu.VMEM((OWN, 3, PLANES, NY, NZ), f32),
            pltpu.VMEM((PLANES, ROWS, NZ), f32),
            pltpu.VMEM((PLANES, ROWS, NZ), jnp.int32),
            pltpu.VMEM((GROUP, PAIRS, 2, ROWS, NZ), f32),
            pltpu.VMEM((GROUP, OWN, 2, ROWS, NZ), f32),
            pltpu.VMEM((PLANES, GROUP, PAIRS, 2, ROWS, NZ), f32),
            pltpu.VMEM((PLANES + 1, GROUP, PAIRS, 2, ROWS, NZ), f32),
            pltpu.VMEM((GROUP, PAIRS, ROWS, NZ), f32),
            pltpu.VMEM((GROUP, PAIRS, ROWS, NZ), f32),
            pltpu.VMEM((PLANES + 1, GROUP, PAIRS, ROWS, NZ), f32),
            pltpu.VMEM((PLANES + 1, GROUP, OWN, 2, ROWS, NZ), f32),
            pltpu.VMEM((PLANES + 1, GROUP, OWN, 2, ROWS, NZ), f32),
            pltpu.VMEM((6, GROUP, OWN, ROWS, NZ), f32),
            pltpu.VMEM((FOLDS, 4, 6, ROWS, NZ), f32),
            pltpu.VMEM((FOLDS, 4, 3, ROWS, NZ), f32),
            pltpu.VMEM((PLANES + 1, NCOEF, ROWS, NZ), f32),
            pltpu.VMEM((PLANES + 1, NCOEF, ROWS, NZ), f32),
            pltpu.VMEM((PLANES + 1, OWN, ROWS, NZ), f32),
            pltpu.VMEM((PLANES, ROWS, NZ), f32),
            dma((2, PLANES)), dma, dma((2,)), dma((2,)), dma, dma, dma, dma,
            dma((PLANES + 2, GROUP - 1)), dma((PLANES + 2, GROUP - 1)),
            dma((PLANES + 1, GROUP - 1)), dma((PLANES + 1, GROUP - 1)),
            dma((PLANES + 1,)), dma((PLANES + 1, GROUP)),
            dma((PLANES + 1,)), dma((PLANES + 1,)),
            dma((PLANES,)), dma((PLANES,)),
            dma((PLANES, GROUP - 1)), dma((PLANES,)),
            dma, dma, pltpu.SemaphoreType.REGULAR,
        ],
        compiler_params=pltpu.CompilerParams(
            collective_id=0, has_side_effects=True, vmem_limit_bytes=60 * 1024 * 1024
        ),
    )(state_hat, adjoint_hat, objective_hat, density, region)
    return pl.pallas_call(
        write_out,
        out_shape=(jax.ShapeDtypeStruct(residual, f32), jax.ShapeDtypeStruct(gradient, f32)),
        in_specs=[vmem, vmem],
        out_specs=(hbm, hbm),
        scratch_shapes=[dma((OWN + 1,))],
        compiler_params=pltpu.CompilerParams(vmem_limit_bytes=1024 * 1024),
    )(*held)


def solution(mesh):
    in_specs = (
        P("sample", None, "space", None, None),
        P("sample", None, "space", None, None),
        P("sample", None, "space", None, None),
        P("space", None, None),
        P("space", None, None),
    )
    out_specs = (P("sample", None, "space", None, None), P("space", "sample", None))
    return jax.shard_map(local, mesh=mesh, in_specs=in_specs, out_specs=out_specs, check_vma=False)
```

```python
import math

import jax
import jax.numpy as jnp
from jax import lax
from jax.experimental import pallas as pl
from jax.experimental.pallas import tpu as pltpu
from jax.sharding import PartitionSpec as P

NT = 40
NCOEF = 20
NY = 32
NZ = 128
PLANES = 8
GROUP = 4
OWN = NCOEF // GROUP
ROWS = NY // GROUP
FOLDS = NT // 4 + 1
PAIRS = 2 * OWN
RUN = 4

magnet_reluct = 0.95
iron_floor = 0.05

CLASSES = (
    ("cos", (2, 4, 6, 8, 10)),
    ("cos", (1, 3, 5, 7, 9)),
    ("sin", (2, 4, 6, 8, 10)),
    ("sin", (1, 3, 5, 7, 9)),
)


def coef_index(kind, order):
    return 2 * (order - 1) + (0 if kind == "cos" else 1)


def factor(kind, order, n):
    turn = (n * order) % NT
    quarter = NT // 4
    if kind == "sin":
        turn = (turn - quarter) % NT
    if turn % quarter == 0:
        return (1.0, 0.0, -1.0, 0.0)[turn // quarter]
    return math.cos(2.0 * math.pi * turn / NT)


def combine(terms, constants):
    total = None
    for term, constant in zip(terms, constants):
        if constant == 0.0:
            continue
        if constant == 1.0:
            piece = term
        elif constant == -1.0:
            piece = -term
        else:
            piece = term * jnp.float32(constant)
        total = piece if total is None else total + piece
    return jnp.zeros_like(terms[0]) if total is None else total


def kernel(
    state_hbm, adjoint_hbm, objective_hbm, density_hbm, region_hbm,
    out, grad_out,
    pot, phi, obj, dens, regn, upper, send, recv, phi_send, phi_recv, edge,
    bsend, brecv, zsend, zrecv, flux, wave, fold, field, field_edge, fix, below_sum, grad,
    in_sems, obj_sem, mat_sems, own_sems, up_send, up_recv, low_send, low_recv,
    f_send, f_recv, b_send, b_recv, e_send, e_recv, c_send, c_recv,
    s_send, s_recv, x_send, x_recv, g_send, g_recv, ready,
):
    me = lax.axis_index("sample")
    block = lax.axis_index("space")
    blocks = lax.axis_size("space")
    above = lax.rem(block + 1, blocks)
    below = lax.rem(block + blocks - 1, blocks)
    has_above, has_below = block < blocks - 1, block > 0
    mesh_id = pl.DeviceIdType.MESH

    def turned(index, where):
        return lax.rem(index + 2 * lax.rem(where // RUN, 2), GROUP)

    swaps = lax.rem(block // RUN, 2) == 1
    slab = turned(me, block)
    odd_slab = lax.rem(me, 2) == 1
    even_slab = jnp.logical_not(odd_slab)
    partner = me + 1 - 2 * lax.rem(me, 2)
    middle = turned(1, block)
    is_middle = me == middle
    off_middle = me != middle
    up_id = {"space": above, "sample": turned(slab, above)}
    down_id = {"space": below, "sample": turned(slab, below)}
    peers = [lax.rem(me + 2, GROUP), lax.rem(partner + 2, GROUP), partner]
    arguments = (state_hbm, adjoint_hbm)

    def to_sample(source, target, send_sem, recv_sem, peer):
        return pltpu.make_async_remote_copy(
            src_ref=source, dst_ref=target, send_sem=send_sem, recv_sem=recv_sem,
            device_id={"sample": peer}, device_id_type=mesh_id,
        )

    barrier = pltpu.get_barrier_semaphore()
    for peer in peers:
        pl.semaphore_signal(barrier, inc=1, device_id={"sample": peer}, device_id_type=mesh_id)

    @pl.when(has_below)
    def _():
        pl.semaphore_signal(barrier, inc=1, device_id=down_id, device_id_type=mesh_id)

    def slab_rows(s):
        return pl.ds(pl.multiple_of(s * ROWS, ROWS), ROWS)

    def load(p):
        return [
            pltpu.make_async_copy(ref.at[:, :, p], pot.at[i, p], in_sems.at[i, p])
            for i, ref in enumerate(arguments)
        ]

    own = [
        pltpu.make_async_copy(
            ref.at[:, pl.ds(1, 2), 0, slab_rows(slab)], recv.at[0, me, pl.ds(i * OWN, OWN)], own_sems.at[i]
        )
        for i, ref in enumerate(arguments)
    ]
    for copy in own:
        copy.start()

    @pl.loop(0, PLANES)
    def _(p):
        for copy in load(p):
            copy.start()

    material = [
        pltpu.make_async_copy(density_hbm.at[:, slab_rows(slab)], dens, mat_sems.at[0]),
        pltpu.make_async_copy(region_hbm.at[:, slab_rows(slab)], regn, mat_sems.at[1]),
    ]
    for copy in material:
        copy.start()
    objective = pltpu.make_async_copy(objective_hbm, obj, obj_sem)
    objective.start()

    def forward_first():
        return [
            to_sample(
                ref.at[:, pl.ds(1, 2), 0, slab_rows(turned(peer, block))],
                recv.at[0, me, pl.ds(i * OWN, OWN)],
                f_send.at[i * (PLANES + 1), r], f_recv.at[i * (PLANES + 1), r], peer,
            )
            for r, peer in enumerate(peers)
            for i, ref in enumerate(arguments)
        ]

    def forward(p):
        return [
            to_sample(
                send.at[p, turned(peer, block)], recv.at[p, me], f_send.at[p, r], f_recv.at[p, r], peer
            )
            for r, peer in enumerate(peers)
        ]

    def forward_phi():
        return [
            to_sample(
                phi_send.at[turned(peer, block)], phi_recv.at[me],
                f_send.at[PLANES, r], f_recv.at[PLANES, r], peer,
            )
            for r, peer in enumerate(peers)
        ]

    def backward(p):
        return [
            to_sample(bsend.at[p, peer], brecv.at[p, slab], b_send.at[p, r], b_recv.at[p, r], peer)
            for r, peer in enumerate(peers)
        ]

    def backward_zero():
        return [
            to_sample(zsend.at[peer], zrecv.at[slab], b_send.at[PLANES, r], b_recv.at[PLANES, r], peer)
            for r, peer in enumerate(peers)
        ]

    top_row, end_row = pl.ds(0, 1), pl.ds(ROWS - 1, 1)

    def middle_row(p, q):
        source = send.at[p, 2, :, 1, top_row]
        return to_sample(source, edge.at[p, q, :, top_row], e_send.at[p], e_recv.at[p, q], middle)

    def middle_phi(q):
        source = phi_send.at[2, :, top_row]
        return to_sample(source, edge.at[PLANES, q, :, top_row], e_send.at[PLANES], e_recv.at[PLANES, q], middle)

    def chip_row(p):
        return to_sample(recv.at[p, :, :, 1, top_row], edge.at[p, :, :, top_row], c_send.at[p], c_recv.at[p], partner)

    def chip_phi():
        return to_sample(
            phi_recv.at[:, :, top_row], edge.at[PLANES, :, :, top_row],
            c_send.at[PLANES], c_recv.at[PLANES], partner,
        )

    def last_rows(p, some):
        if isinstance(p, int) and p == PLANES:
            return field.at[PLANES, 2, some, end_row]
        return field.at[p + 1, 0, some, end_row]

    def field_row(p):
        return to_sample(
            last_rows(p, pl.ds(0, NCOEF)), field_edge.at[p, :, end_row], s_send.at[p], s_recv.at[p], partner
        )

    def fix_row(p):
        return [
            to_sample(
                last_rows(p, pl.ds(peer * OWN, OWN)), fix.at[p, :, end_row], x_send.at[p, r], x_recv.at[p], peer
            )
            for r, peer in enumerate(peers)
        ]

    row_id = lax.broadcasted_iota(jnp.int32, (NY, NZ), 0)
    lane_id = lax.broadcasted_iota(jnp.int32, (NY, NZ), 1)
    slab_row = lax.broadcasted_iota(jnp.int32, (ROWS, NZ), 0)
    slab_lane = lax.broadcasted_iota(jnp.int32, (ROWS, NZ), 1)

    def next_row(a):
        return jnp.where(row_id == NY - 1, 0.0, pltpu.roll(a, NY - 1, 0))

    def next_lane(a):
        return jnp.where(lane_id == NZ - 1, 0.0, pltpu.roll(a, NZ - 1, 1))

    def prior_row(a):
        return jnp.where(row_id == 0, 0.0, pltpu.roll(a, 1, 0))

    def prior_lane(a):
        return jnp.where(lane_id == 0, 0.0, pltpu.roll(a, 1, 1))

    def slab_next_row(a, row):
        return jnp.where(slab_row == ROWS - 1, row, pltpu.roll(a, ROWS - 1, 0))

    def slab_next_lane(a):
        return jnp.where(slab_lane == NZ - 1, 0.0, pltpu.roll(a, NZ - 1, 1))

    def slab_prior_row(a, row):
        return jnp.where(slab_row == 0, row, pltpu.roll(a, 1, 0))

    def slab_prior_lane(a):
        return jnp.where(slab_lane == 0, 0.0, pltpu.roll(a, 1, 1))

    pl.semaphore_wait(barrier, GROUP - 1 + has_above.astype(jnp.int32))
    for copy in forward_first():
        copy.start()

    @pl.when(has_above)
    def _():
        pl.semaphore_signal(ready, inc=1, device_id=up_id, device_id_type=mesh_id)

    for copy in load(0):
        copy.wait()
    for i in range(2):
        for j in range(OWN):
            phi[0, i, j] = pot[i, 0, j, 0]
            send[0, 2, i * OWN + j, 1] = pot[i, 0, j, 2, pl.ds(2 * ROWS, ROWS), :]

    @pl.loop(1, PLANES)
    def _(p):
        for copy in load(p):
            copy.wait()

        for i in range(2):
            @pl.loop(0, OWN)
            def _(j):
                phi[p, i, j] = phi[p - 1, i, j] + pot[i, p, j, 0]

    for i in range(2):
        for j in range(OWN):
            phi_send[:, i * OWN + j] = phi[PLANES - 1, i, j].reshape(GROUP, ROWS, NZ)
    phi_recv[me] = phi_send[slab]
    for copy in forward_phi():
        copy.start()

    @pl.when(off_middle)
    def _():
        middle_phi(me).start()
        middle_row(0, me).start()

    @pl.when(is_middle)
    def _():
        for ij in range(PAIRS):
            edge[PLANES, me, ij] = phi_send[2, ij]
            edge[0, me, ij] = send[0, 2, ij, 1]

    @pl.loop(0, PLANES - 1)
    def _(k):
        p = PLANES - 1 - k
        for i in range(2):
            for j in range(OWN):
                under = phi[p - 1, i, j]
                one = pot[i, p, j, 1] - (next_row(under) - under)
                two = pot[i, p, j, 2] - (next_lane(under) - under)
                send[p, :, i * OWN + j, 0] = one.reshape(GROUP, ROWS, NZ)
                send[p, :, i * OWN + j, 1] = two.reshape(GROUP, ROWS, NZ)
        for copy in forward(p):
            copy.start()

        @pl.when(off_middle)
        def _():
            middle_row(p, me).start()

        @pl.when(is_middle)
        def _():
            for ij in range(PAIRS):
                edge[p, me, ij] = send[p, 2, ij, 1]

        recv[p, me] = send[p, slab]

    @pl.when(even_slab)
    def _():
        @pl.loop(0, PLANES + 1)
        def _(p):
            field_edge[p] = jnp.zeros((NCOEF, ROWS, NZ), jnp.float32)

    @pl.when(slab == GROUP - 1)
    def _():
        @pl.loop(0, PLANES + 1)
        def _(p):
            edge[p] = jnp.zeros((GROUP, PAIRS, ROWS, NZ), jnp.float32)

    @pl.when(jnp.logical_not(has_above))
    def _():
        upper[...] = jnp.zeros_like(upper)

    @pl.when(jnp.logical_not(has_below))
    def _():
        field[0, pl.ds(1, 2)] = jnp.zeros((2, NCOEF, ROWS, NZ), jnp.float32)

    for copy in own:
        copy.wait()
    for copy in forward_first():
        copy.wait_recv()
    up = pltpu.make_async_remote_copy(
        src_ref=recv.at[0], dst_ref=upper,
        send_sem=up_send, recv_sem=up_recv, device_id=down_id, device_id_type=mesh_id,
    )

    @pl.when(has_below)
    def _():
        pl.semaphore_wait(ready, 1)
        up.start()

    for copy in material:
        copy.wait()
    for copy in forward_phi():
        copy.wait_recv()

    @pl.when(odd_slab)
    def _():
        chip_phi().start()
        chip_row(0).start()

    @pl.when(is_middle)
    def _():
        for peer in peers:
            middle_phi(peer).wait_recv()
            middle_row(0, peer).wait_recv()

    @pl.when(even_slab)
    def _():
        chip_phi().wait_recv()
        chip_row(0).wait_recv()

    @pl.when(has_above)
    def _():
        up.wait_recv()

    @pl.loop(0, GROUP)
    def _(q):
        for ij in range(PAIRS):
            top = phi_recv[q, ij]
            row = edge[PLANES, q, ij, top_row, :]
            recv[PLANES, q, ij, 0] = upper[q, ij, 0] - (slab_next_row(top, row) - top)
            recv[PLANES, q, ij, 1] = upper[q, ij, 1] - (slab_next_lane(top) - top)

    down = pltpu.make_async_remote_copy(
        src_ref=field.at[PLANES, pl.ds(1, 2)], dst_ref=field.at[0, pl.ds(1, 2)],
        send_sem=low_send, recv_sem=low_recv, device_id=up_id, device_id_type=mesh_id,
    )

    def nonlinear(p):
        @pl.loop(0, GROUP)
        def _(q):
            for i in range(2):
                for j in range(OWN):
                    ij = i * OWN + j
                    one, two = recv[p, q, ij, 0], recv[p, q, ij, 1]
                    row = edge[p, q, ij, top_row, :]
                    flux[3 * i, q, j] = (slab_next_row(two, row) - two) - (slab_next_lane(one) - one)
                    flux[3 * i + 1, q, j] = two - recv[p + 1, q, ij, 1]
                    flux[3 * i + 2, q, j] = recv[p + 1, q, ij, 0] - one

        @pl.loop(0, 6)
        def _(pc):
            for t, (kind, orders) in enumerate(CLASSES):
                where = [coef_index(kind, m) for m in orders]
                terms = [flux[pc, c // OWN, c % OWN] for c in where]
                for n in range(FOLDS):
                    wave[n, t, pc] = combine(terms, [factor(kind, m, n) for m in orders])

        density, region = dens[p], regn[p]
        iron = region == 0
        share = jnp.where(iron, density * density * density, 0.0) * jnp.float32(1.0 - iron_floor)
        slope = jnp.where(iron, 3.0 * density * density, 0.0)
        base = jnp.where(region == 1, jnp.float32(magnet_reluct), jnp.float32(1.0))

        def samples(n, total):
            state = [[], [], []]
            adjoint = [[], [], []]
            for pc in range(6):
                ce, co, se, so = (wave[n, t, pc] for t in range(4))
                a, b, d, f = ce + co, ce - co, se + so, se - so
                (state if pc < 3 else adjoint)[pc % 3] = (a + d, a - d, b - f, b + f)
            values = [[], [], []]
            part = None
            for v in range(4):
                s = [state[c][v] for c in range(3)]
                g = [adjoint[c][v] for c in range(3)]
                square = s[0] * s[0] + s[1] * s[1] + s[2] * s[2]
                inner = s[0] * g[0] + s[1] * g[1] + s[2] * g[2]
                r = 1.0 / (square + 1.0)
                t = share * r
                ri = r * inner
                nu = base - t
                mu = (t + t) * ri
                part = ri if part is None else part + ri
                for c in range(3):
                    values[c].append(nu * g[c] + mu * s[c])
            for c in range(3):
                w, x, y, z = values[c]
                a, d = w + x, w - x
                b, f = z + y, z - y
                fold[n, 0, c] = a + b
                fold[n, 1, c] = a - b
                fold[n, 2, c] = d + f
                fold[n, 3, c] = d - f
            ends = (n == 0) | (n == FOLDS - 1)
            return total + part * jnp.where(ends, 0.5, 1.0)

        total = lax.fori_loop(0, FOLDS, samples, jnp.zeros((ROWS, NZ), jnp.float32))
        grad[p] = total * slope * jnp.float32((1.0 - iron_floor) / NT)

        for t, (kind, orders) in enumerate(CLASSES):
            for c in range(3):
                terms = [fold[n, t, c] for n in range(FOLDS)]
                for m in orders:
                    scales = [
                        factor(kind, m, n) * (1.0 if 0 < n < FOLDS - 1 else 0.5) * 2.0 / NT
                        for n in range(FOLDS)
                    ]
                    field[p + 1, c, coef_index(kind, m)] = combine(terms, scales)

    def give_back(p):
        @pl.when(odd_slab)
        def _():
            field_row(p).wait_recv()

        @pl.when(is_middle)
        def _():
            for copy in fix_row(p):
                copy.start()

            fix[p] = field[p + 1, 0, pl.ds(me * OWN, OWN)]

        @pl.loop(0, GROUP)
        def _(q):
            for j in range(OWN):
                at = q * OWN + j
                zero, one, two = (field[p + 1, c, at] for c in range(3))
                row = field_edge[p, at, end_row, :]
                bsend[p, q, j, 0] = (field[p, 2, at] - two) - (slab_prior_lane(zero) - zero)
                bsend[p, q, j, 1] = (slab_prior_row(zero, row) - zero) - (field[p, 1, at] - one)

        for copy in backward(p):
            copy.start()
        brecv[p, slab] = bsend[p, me]

    def give_back_zero():
        @pl.when(odd_slab)
        def _():
            field_row(PLANES).wait_recv()

        @pl.when(is_middle)
        def _():
            for copy in fix_row(PLANES):
                copy.start()

            fix[PLANES] = field[PLANES, 2, pl.ds(me * OWN, OWN)]

        @pl.loop(0, GROUP)
        def _(q):
            for j in range(OWN):
                at = q * OWN + j
                one, two = field[PLANES, 1, at], field[PLANES, 2, at]
                row = field_edge[PLANES, at, end_row, :]
                zsend[q, j] = (slab_prior_lane(one) - one) - (slab_prior_row(two, row) - two)

        for copy in backward_zero():
            copy.start()
        zrecv[slab] = zsend[me]

    @pl.loop(0, PLANES)
    def _(k):
        p = PLANES - 1 - k

        @pl.when(p > 0)
        def _():
            for copy in forward(p):
                copy.wait_recv()

            @pl.when(odd_slab)
            def _():
                chip_row(p).start()

            @pl.when(is_middle)
            def _():
                for peer in peers:
                    middle_row(p, peer).wait_recv()

            @pl.when(even_slab)
            def _():
                chip_row(p).wait_recv()

        nonlinear(p)

        @pl.when(even_slab)
        def _():
            field_row(p).start()

        @pl.when(k == 0)
        def _():
            @pl.when(even_slab)
            def _():
                field_row(PLANES).start()

            @pl.when(has_above)
            def _():
                down.start()

            give_back_zero()

        @pl.when(k > 0)
        def _():
            give_back(p + 1)

    @pl.when(has_below)
    def _():
        down.wait_recv()

    give_back(0)

    swap = to_sample(grad, grad_out, g_send, g_recv, lax.rem(me + 2, GROUP))

    @pl.when(swaps)
    def _():
        swap.start()

    @pl.when(jnp.logical_not(swaps))
    def _():
        grad_out[...] = grad[...]

    def fixed(parts, p, j, sign):
        row = jnp.where(slab_row == 0, fix[p, j, end_row, :], 0.0)
        parts[2] = parts[2] + row if sign > 0 else parts[2] - row
        return jnp.concatenate(parts, axis=0)

    objective.wait()
    for copy in backward_zero():
        copy.wait_recv()

    @pl.when(off_middle)
    def _():
        fix_row(PLANES)[0].wait_recv()

    for j in range(OWN):
        below_sum[j] = fixed([zrecv[q, j] for q in range(GROUP)], PLANES, j, -1)

    @pl.loop(0, PLANES)
    def _(k):
        p = PLANES - 1 - k
        for copy in backward(p):
            copy.wait_recv()

        @pl.when(off_middle)
        def _():
            fix_row(p)[0].wait_recv()

        for j in range(OWN):
            zero = below_sum[j]
            one = brecv[p, :, j, 0].reshape(NY, NZ)
            two = fixed([brecv[p, q, j, 1] for q in range(GROUP)], p, j, 1)
            for c, part in enumerate((zero, one, two)):
                out[j, c, p] = obj[j, c, p] - part
            below_sum[j] = zero - (prior_row(one) - one) - (prior_lane(two) - two)

    @pl.when(swaps)
    def _():
        swap.wait()

    @pl.when(has_below)
    def _():
        up.wait_send()

    @pl.when(has_above)
    def _():
        down.wait_send()

    for copy in forward_first() + forward_phi() + backward_zero():
        copy.wait_send()

    @pl.when(off_middle)
    def _():
        middle_phi(me).wait_send()

    @pl.when(odd_slab)
    def _():
        chip_phi().wait_send()

    @pl.when(even_slab)
    def _():
        field_row(PLANES).wait_send()

    @pl.when(is_middle)
    def _():
        for copy in fix_row(PLANES):
            copy.wait_send()

    @pl.loop(0, PLANES)
    def _(p):
        for copy in backward(p):
            copy.wait_send()

        @pl.when(p > 0)
        def _():
            for copy in forward(p):
                copy.wait_send()

        @pl.when(off_middle)
        def _():
            middle_row(p, me).wait_send()

        @pl.when(odd_slab)
        def _():
            chip_row(p).wait_send()

        @pl.when(even_slab)
        def _():
            field_row(p).wait_send()

        @pl.when(is_middle)
        def _():
            for copy in fix_row(p):
                copy.wait_send()


def write_out(held, held_grad, out_hbm, grad_hbm, sems):
    copies = [pltpu.make_async_copy(held.at[j], out_hbm.at[j], sems.at[j]) for j in range(OWN)]
    copies.append(pltpu.make_async_copy(held_grad, grad_hbm, sems.at[OWN]))
    for copy in copies:
        copy.start()
    for copy in copies:
        copy.wait()


def local(state_hat, adjoint_hat, objective_hat, density, region):
    f32 = jnp.float32
    hbm = pl.BlockSpec(memory_space=pl.ANY)
    dma = pltpu.SemaphoreType.DMA
    links = (PLANES + 1, GROUP - 1)
    residual = (OWN, 3, PLANES, NY, NZ)
    gradient = (PLANES, ROWS, NZ)
    vmem = pl.BlockSpec(memory_space=pltpu.VMEM)
    held = pl.pallas_call(
        kernel,
        out_shape=(pltpu.VMEM(residual, f32), pltpu.VMEM(gradient, f32)),
        in_specs=[hbm] * 5,
        out_specs=(vmem, vmem),
        scratch_shapes=[
            pltpu.VMEM((2, PLANES, OWN, 3, NY, NZ), f32),
            pltpu.VMEM((PLANES, 2, OWN, NY, NZ), f32),
            pltpu.VMEM((OWN, 3, PLANES, NY, NZ), f32),
            pltpu.VMEM((PLANES, ROWS, NZ), f32),
            pltpu.VMEM((PLANES, ROWS, NZ), jnp.int32),
            pltpu.VMEM((GROUP, PAIRS, 2, ROWS, NZ), f32),
            pltpu.VMEM((PLANES, GROUP, PAIRS, 2, ROWS, NZ), f32),
            pltpu.VMEM((PLANES + 1, GROUP, PAIRS, 2, ROWS, NZ), f32),
            pltpu.VMEM((GROUP, PAIRS, ROWS, NZ), f32),
            pltpu.VMEM((GROUP, PAIRS, ROWS, NZ), f32),
            pltpu.VMEM((PLANES + 1, GROUP, PAIRS, ROWS, NZ), f32),
            pltpu.VMEM((PLANES, GROUP, OWN, 2, ROWS, NZ), f32),
            pltpu.VMEM((PLANES, GROUP, OWN, 2, ROWS, NZ), f32),
            pltpu.VMEM((GROUP, OWN, ROWS, NZ), f32),
            pltpu.VMEM((GROUP, OWN, ROWS, NZ), f32),
            pltpu.VMEM((6, GROUP, OWN, ROWS, NZ), f32),
            pltpu.VMEM((FOLDS, 4, 6, ROWS, NZ), f32),
            pltpu.VMEM((FOLDS, 4, 3, ROWS, NZ), f32),
            pltpu.VMEM((PLANES + 1, 3, NCOEF, ROWS, NZ), f32),
            pltpu.VMEM((PLANES + 1, NCOEF, ROWS, NZ), f32),
            pltpu.VMEM((PLANES + 1, OWN, ROWS, NZ), f32),
            pltpu.VMEM((OWN, NY, NZ), f32),
            pltpu.VMEM((PLANES, ROWS, NZ), f32),
            dma((2, PLANES)), dma, dma((2,)), dma((2,)), dma, dma, dma, dma,
            dma((PLANES + 2, GROUP - 1)), dma((PLANES + 2, GROUP - 1)),
            dma((PLANES + 1, GROUP - 1)), dma((PLANES + 1, GROUP - 1)),
            dma((PLANES + 1,)), dma((PLANES + 1, GROUP)),
            dma((PLANES + 1,)), dma((PLANES + 1,)),
            dma((PLANES + 1,)), dma((PLANES + 1,)),
            dma((PLANES + 1, GROUP - 1)), dma((PLANES + 1,)),
            dma, dma, pltpu.SemaphoreType.REGULAR,
        ],
        compiler_params=pltpu.CompilerParams(
            collective_id=0, has_side_effects=True, vmem_limit_bytes=60 * 1024 * 1024
        ),
    )(state_hat, adjoint_hat, objective_hat, density, region)
    return pl.pallas_call(
        write_out,
        out_shape=(jax.ShapeDtypeStruct(residual, f32), jax.ShapeDtypeStruct(gradient, f32)),
        in_specs=[vmem, vmem],
        out_specs=(hbm, hbm),
        scratch_shapes=[dma((OWN + 1,))],
        compiler_params=pltpu.CompilerParams(vmem_limit_bytes=1024 * 1024),
    )(*held)


def solution(mesh):
    in_specs = (
        P("sample", None, "space", None, None),
        P("sample", None, "space", None, None),
        P("sample", None, "space", None, None),
        P("space", None, None),
        P("space", None, None),
    )
    out_specs = (P("sample", None, "space", None, None), P("space", "sample", None))
    return jax.shard_map(local, mesh=mesh, in_specs=in_specs, out_specs=out_specs, check_vma=False)
```

```python
import math

import jax
import jax.numpy as jnp
from jax import lax
from jax.experimental import pallas as pl
from jax.experimental.pallas import tpu as pltpu
from jax.sharding import PartitionSpec as P

NT = 40
NCOEF = 20
NY = 32
NZ = 128
PLANES = 8
GROUP = 4
OWN = NCOEF // GROUP
ROWS = NY // GROUP
FOLDS = NT // 4 + 1
PAIRS = 2 * OWN
RUN = 4

magnet_reluct = 0.95
iron_floor = 0.05

CLASSES = (
    ("cos", (2, 4, 6, 8, 10)),
    ("cos", (1, 3, 5, 7, 9)),
    ("sin", (2, 4, 6, 8, 10)),
    ("sin", (1, 3, 5, 7, 9)),
)


def coef_index(kind, order):
    return 2 * (order - 1) + (0 if kind == "cos" else 1)


def factor(kind, order, n):
    turn = (n * order) % NT
    quarter = NT // 4
    if kind == "sin":
        turn = (turn - quarter) % NT
    if turn % quarter == 0:
        return (1.0, 0.0, -1.0, 0.0)[turn // quarter]
    return math.cos(2.0 * math.pi * turn / NT)


def combine(terms, constants):
    total = None
    for term, constant in zip(terms, constants):
        if constant == 0.0:
            continue
        if constant == 1.0:
            piece = term
        elif constant == -1.0:
            piece = -term
        else:
            piece = term * jnp.float32(constant)
        total = piece if total is None else total + piece
    return jnp.zeros_like(terms[0]) if total is None else total


def kernel(
    state_hbm, adjoint_hbm, objective_hbm, density_hbm, region_hbm,
    out, grad_out,
    pot, phi, obj, dens, regn, upper, send, recv, phi_send, phi_recv, edge,
    bsend, brecv, zsend, zrecv, flux, wave, fold, field, field_edge, fix, below_sum, grad,
    in_sems, obj_sem, mat_sems, own_sem, up_send, up_recv, low_send, low_recv,
    f_send, p_send, f_recv, b_send, z_send, b_recv, chip_send, chip_recv, mid_send, mid_recv,
    g_send, g_recv, ready,
):
    me = lax.axis_index("sample")
    block = lax.axis_index("space")
    blocks = lax.axis_size("space")
    above = lax.rem(block + 1, blocks)
    below = lax.rem(block + blocks - 1, blocks)
    has_above, has_below = block < blocks - 1, block > 0
    mesh_id = pl.DeviceIdType.MESH

    def turned(index, where):
        return lax.rem(index + 2 * lax.rem(where // RUN, 2), GROUP)

    swaps = lax.rem(block // RUN, 2) == 1
    slab = turned(me, block)
    odd_slab = lax.rem(me, 2) == 1
    even_slab = jnp.logical_not(odd_slab)
    partner = me + 1 - 2 * lax.rem(me, 2)
    middle = turned(1, block)
    is_middle = me == middle
    off_middle = me != middle
    up_id = {"space": above, "sample": turned(slab, above)}
    down_id = {"space": below, "sample": turned(slab, below)}
    peers = [lax.rem(me + 2, GROUP), lax.rem(partner + 2, GROUP), partner]
    arguments = (state_hbm, adjoint_hbm)

    def to_sample(source, target, send_sem, recv_sem, peer):
        return pltpu.make_async_remote_copy(
            src_ref=source, dst_ref=target, send_sem=send_sem, recv_sem=recv_sem,
            device_id={"sample": peer}, device_id_type=mesh_id,
        )

    barrier = pltpu.get_barrier_semaphore()
    for peer in peers:
        pl.semaphore_signal(barrier, inc=1, device_id={"sample": peer}, device_id_type=mesh_id)

    ends, begins = lax.rem(block, RUN) == RUN - 1, lax.rem(block, RUN) == 0
    waits_above, waits_below = has_above & ends, has_below & jnp.logical_not(begins)
    tells_above, tells_below = has_above & jnp.logical_not(ends), has_below & begins

    @pl.when(tells_above)
    def _():
        pl.semaphore_signal(barrier, inc=1, device_id=up_id, device_id_type=mesh_id)

    @pl.when(tells_below)
    def _():
        pl.semaphore_signal(barrier, inc=1, device_id=down_id, device_id_type=mesh_id)

    def slab_rows(s):
        return pl.ds(pl.multiple_of(s * ROWS, ROWS), ROWS)

    def load(p):
        return [
            pltpu.make_async_copy(ref.at[:, :, p], pot.at[p, i], in_sems.at[jnp.minimum(p, 1)])
            for i, ref in enumerate(arguments)
        ]

    def all_of(ref, sem):
        return pltpu.make_async_copy(ref, ref, sem)

    own = [
        pltpu.make_async_copy(
            ref.at[:, pl.ds(1, 2), 0, slab_rows(slab)], recv.at[0, me, pl.ds(i * OWN, OWN)], own_sem
        )
        for i, ref in enumerate(arguments)
    ]
    for copy in own:
        copy.start()

    @pl.loop(0, PLANES)
    def _(p):
        for copy in load(p):
            copy.start()

    material = [
        pltpu.make_async_copy(density_hbm.at[:, slab_rows(slab)], dens, mat_sems.at[0]),
        pltpu.make_async_copy(region_hbm.at[:, slab_rows(slab)], regn, mat_sems.at[1]),
    ]
    for copy in material:
        copy.start()
    objective = pltpu.make_async_copy(objective_hbm, obj, obj_sem)
    objective.start()

    def forward_first():
        return [
            to_sample(
                ref.at[:, pl.ds(1, 2), 0, slab_rows(turned(peer, block))],
                recv.at[0, me, pl.ds(i * OWN, OWN)],
                f_send, f_recv.at[0], peer,
            )
            for peer in peers
            for i, ref in enumerate(arguments)
        ]

    def forward(p):
        return [
            to_sample(
                send.at[p, turned(peer, block)], recv.at[p, me], f_send, f_recv.at[p], peer
            )
            for peer in peers
        ]

    def forward_came(p):
        all_of(recv.at[p, pl.ds(0, GROUP - 1)], f_recv.at[p]).wait()

    def forward_phi():
        return [
            to_sample(
                phi_send.at[turned(peer, block)], phi_recv.at[me],
                p_send, f_recv.at[PLANES], peer,
            )
            for peer in peers
        ]

    def backward(p):
        return [
            to_sample(bsend.at[p, peer], brecv.at[p, slab], b_send, b_recv.at[p], peer)
            for peer in peers
        ]

    def backward_zero():
        return [
            to_sample(zsend.at[peer], zrecv.at[slab], z_send, b_recv.at[PLANES], peer)
            for peer in peers
        ]

    top_row, end_row = pl.ds(0, 1), pl.ds(ROWS - 1, 1)

    def middle_row(p, q):
        source = send.at[p, 2, :, 1, top_row]
        return to_sample(source, edge.at[p, q, :, top_row], mid_send, mid_recv.at[p], middle)

    def middle_phi(q):
        source = phi_send.at[2, :, top_row]
        return to_sample(source, edge.at[PLANES, q, :, top_row], mid_send, mid_recv.at[PLANES], middle)

    def middle_came(p):
        all_of(edge.at[p, pl.ds(0, GROUP - 1), :, top_row], mid_recv.at[p]).wait()

    def chip_row(p):
        return to_sample(recv.at[p, :, :, 1, top_row], edge.at[p, :, :, top_row], chip_send, chip_recv.at[p], partner)

    def chip_phi():
        return to_sample(
            phi_recv.at[:, :, top_row], edge.at[PLANES, :, :, top_row],
            chip_send, chip_recv.at[PLANES], partner,
        )

    def last_rows(p, some):
        if isinstance(p, int) and p == PLANES:
            return field.at[PLANES, 2, some, end_row]
        return field.at[p + 1, 0, some, end_row]

    def field_row(p):
        return to_sample(
            last_rows(p, pl.ds(0, NCOEF)), field_edge.at[p, :, end_row], chip_send, chip_recv.at[p], partner
        )

    def fix_row(p):
        return [
            to_sample(
                last_rows(p, pl.ds(peer * OWN, OWN)), fix.at[p, :, end_row], mid_send, mid_recv.at[p], peer
            )
            for peer in peers
        ]

    row_id = lax.broadcasted_iota(jnp.int32, (NY, NZ), 0)
    lane_id = lax.broadcasted_iota(jnp.int32, (NY, NZ), 1)
    slab_row = lax.broadcasted_iota(jnp.int32, (ROWS, NZ), 0)
    slab_lane = lax.broadcasted_iota(jnp.int32, (ROWS, NZ), 1)

    def next_row(a):
        return jnp.where(row_id == NY - 1, 0.0, pltpu.roll(a, NY - 1, 0))

    def next_lane(a):
        return jnp.where(lane_id == NZ - 1, 0.0, pltpu.roll(a, NZ - 1, 1))

    def prior_row(a):
        return jnp.where(row_id == 0, 0.0, pltpu.roll(a, 1, 0))

    def prior_lane(a):
        return jnp.where(lane_id == 0, 0.0, pltpu.roll(a, 1, 1))

    def slab_next_row(a, row):
        return jnp.where(slab_row == ROWS - 1, row, pltpu.roll(a, ROWS - 1, 0))

    def slab_next_lane(a):
        return jnp.where(slab_lane == NZ - 1, 0.0, pltpu.roll(a, NZ - 1, 1))

    def slab_prior_row(a, row):
        return jnp.where(slab_row == 0, row, pltpu.roll(a, 1, 0))

    def slab_prior_lane(a):
        return jnp.where(slab_lane == 0, 0.0, pltpu.roll(a, 1, 1))

    pl.semaphore_wait(barrier, GROUP - 1 + waits_above.astype(jnp.int32) + waits_below.astype(jnp.int32))
    for copy in forward_first():
        copy.start()

    @pl.when(waits_above)
    def _():
        pl.semaphore_signal(ready.at[0], inc=1, device_id=up_id, device_id_type=mesh_id)

    @pl.when(waits_below)
    def _():
        pl.semaphore_signal(ready.at[1], inc=1, device_id=down_id, device_id_type=mesh_id)

    all_of(pot.at[0], in_sems.at[0]).wait()
    for i in range(2):
        for j in range(OWN):
            phi[0, i, j] = pot[0, i, j, 0]
            send[0, 2, i * OWN + j, 1] = pot[0, i, j, 2, pl.ds(2 * ROWS, ROWS), :]

    all_of(pot.at[pl.ds(1, PLANES - 1)], in_sems.at[1]).wait()

    @pl.loop(1, PLANES)
    def _(p):
        for i in range(2):
            @pl.loop(0, OWN)
            def _(j):
                phi[p, i, j] = phi[p - 1, i, j] + pot[p, i, j, 0]

    for i in range(2):
        for j in range(OWN):
            phi_send[:, i * OWN + j] = phi[PLANES - 1, i, j].reshape(GROUP, ROWS, NZ)
    phi_recv[me] = phi_send[slab]
    for copy in forward_phi():
        copy.start()

    @pl.when(off_middle)
    def _():
        middle_phi(me).start()
        middle_row(0, me).start()

    @pl.when(is_middle)
    def _():
        for ij in range(PAIRS):
            edge[PLANES, me, ij] = phi_send[2, ij]
            edge[0, me, ij] = send[0, 2, ij, 1]

    @pl.loop(0, PLANES - 1)
    def _(k):
        p = PLANES - 1 - k
        for i in range(2):
            for j in range(OWN):
                under = phi[p - 1, i, j]
                one = pot[p, i, j, 1] - (next_row(under) - under)
                two = pot[p, i, j, 2] - (next_lane(under) - under)
                send[p, :, i * OWN + j, 0] = one.reshape(GROUP, ROWS, NZ)
                send[p, :, i * OWN + j, 1] = two.reshape(GROUP, ROWS, NZ)
        for copy in forward(p):
            copy.start()

        @pl.when(off_middle)
        def _():
            middle_row(p, me).start()

        @pl.when(is_middle)
        def _():
            for ij in range(PAIRS):
                edge[p, me, ij] = send[p, 2, ij, 1]

        recv[p, me] = send[p, slab]

    @pl.when(even_slab)
    def _():
        @pl.loop(0, PLANES + 1)
        def _(p):
            field_edge[p] = jnp.zeros((NCOEF, ROWS, NZ), jnp.float32)

    @pl.when(slab == GROUP - 1)
    def _():
        @pl.loop(0, PLANES + 1)
        def _(p):
            edge[p] = jnp.zeros((GROUP, PAIRS, ROWS, NZ), jnp.float32)

    @pl.when(jnp.logical_not(has_above))
    def _():
        upper[...] = jnp.zeros_like(upper)

    @pl.when(jnp.logical_not(has_below))
    def _():
        field[0, pl.ds(1, 2)] = jnp.zeros((2, NCOEF, ROWS, NZ), jnp.float32)

    all_of(recv.at[0, 0], own_sem).wait()
    forward_came(0)
    up = pltpu.make_async_remote_copy(
        src_ref=recv.at[0], dst_ref=upper,
        send_sem=up_send, recv_sem=up_recv, device_id=down_id, device_id_type=mesh_id,
    )

    @pl.when(tells_below)
    def _():
        pl.semaphore_wait(ready.at[0], 1)

    @pl.when(has_below)
    def _():
        up.start()

    for copy in material:
        copy.wait()
    all_of(phi_recv.at[pl.ds(0, GROUP - 1)], f_recv.at[PLANES]).wait()

    @pl.when(odd_slab)
    def _():
        chip_phi().start()
        chip_row(0).start()

    @pl.when(is_middle)
    def _():
        middle_came(PLANES)
        middle_came(0)

    @pl.when(even_slab)
    def _():
        chip_phi().wait_recv()
        chip_row(0).wait_recv()

    @pl.when(has_above)
    def _():
        up.wait_recv()

    @pl.loop(0, GROUP)
    def _(q):
        for ij in range(PAIRS):
            top = phi_recv[q, ij]
            row = edge[PLANES, q, ij, top_row, :]
            recv[PLANES, q, ij, 0] = upper[q, ij, 0] - (slab_next_row(top, row) - top)
            recv[PLANES, q, ij, 1] = upper[q, ij, 1] - (slab_next_lane(top) - top)

    down = pltpu.make_async_remote_copy(
        src_ref=field.at[PLANES, pl.ds(1, 2)], dst_ref=field.at[0, pl.ds(1, 2)],
        send_sem=low_send, recv_sem=low_recv, device_id=up_id, device_id_type=mesh_id,
    )

    def nonlinear(p):
        @pl.loop(0, GROUP)
        def _(q):
            for i in range(2):
                for j in range(OWN):
                    ij = i * OWN + j
                    one, two = recv[p, q, ij, 0], recv[p, q, ij, 1]
                    row = edge[p, q, ij, top_row, :]
                    flux[3 * i, q, j] = (slab_next_row(two, row) - two) - (slab_next_lane(one) - one)
                    flux[3 * i + 1, q, j] = two - recv[p + 1, q, ij, 1]
                    flux[3 * i + 2, q, j] = recv[p + 1, q, ij, 0] - one

        @pl.loop(0, 6)
        def _(pc):
            for t, (kind, orders) in enumerate(CLASSES):
                where = [coef_index(kind, m) for m in orders]
                terms = [flux[pc, c // OWN, c % OWN] for c in where]
                for n in range(FOLDS):
                    wave[n, t, pc] = combine(terms, [factor(kind, m, n) for m in orders])

        density, region = dens[p], regn[p]
        iron = region == 0
        share = jnp.where(iron, density * density * density, 0.0) * jnp.float32(1.0 - iron_floor)
        slope = jnp.where(iron, 3.0 * density * density, 0.0)
        base = jnp.where(region == 1, jnp.float32(magnet_reluct), jnp.float32(1.0))

        def samples(n, total):
            state = [[], [], []]
            adjoint = [[], [], []]
            for pc in range(6):
                ce, co, se, so = (wave[n, t, pc] for t in range(4))
                a, b, d, f = ce + co, ce - co, se + so, se - so
                (state if pc < 3 else adjoint)[pc % 3] = (a + d, a - d, b - f, b + f)
            values = [[], [], []]
            part = None
            for v in range(4):
                s = [state[c][v] for c in range(3)]
                g = [adjoint[c][v] for c in range(3)]
                square = s[0] * s[0] + s[1] * s[1] + s[2] * s[2]
                inner = s[0] * g[0] + s[1] * g[1] + s[2] * g[2]
                r = 1.0 / (square + 1.0)
                t = share * r
                ri = r * inner
                nu = base - t
                mu = (t + t) * ri
                part = ri if part is None else part + ri
                for c in range(3):
                    values[c].append(nu * g[c] + mu * s[c])
            for c in range(3):
                w, x, y, z = values[c]
                a, d = w + x, w - x
                b, f = z + y, z - y
                fold[n, 0, c] = a + b
                fold[n, 1, c] = a - b
                fold[n, 2, c] = d + f
                fold[n, 3, c] = d - f
            ends = (n == 0) | (n == FOLDS - 1)
            return total + part * jnp.where(ends, 0.5, 1.0)

        total = lax.fori_loop(0, FOLDS, samples, jnp.zeros((ROWS, NZ), jnp.float32))
        grad[p] = total * slope * jnp.float32((1.0 - iron_floor) / NT)

        for t, (kind, orders) in enumerate(CLASSES):
            for c in range(3):
                terms = [fold[n, t, c] for n in range(FOLDS)]
                for m in orders:
                    scales = [
                        factor(kind, m, n) * (1.0 if 0 < n < FOLDS - 1 else 0.5) * 2.0 / NT
                        for n in range(FOLDS)
                    ]
                    field[p + 1, c, coef_index(kind, m)] = combine(terms, scales)

    def give_back(p):
        @pl.when(odd_slab)
        def _():
            field_row(p).wait_recv()

        @pl.when(is_middle)
        def _():
            for copy in fix_row(p):
                copy.start()

            fix[p] = field[p + 1, 0, pl.ds(me * OWN, OWN)]

        @pl.loop(0, GROUP)
        def _(q):
            for j in range(OWN):
                at = q * OWN + j
                zero, one, two = (field[p + 1, c, at] for c in range(3))
                row = field_edge[p, at, end_row, :]
                bsend[p, q, j, 0] = (field[p, 2, at] - two) - (slab_prior_lane(zero) - zero)
                bsend[p, q, j, 1] = (slab_prior_row(zero, row) - zero) - (field[p, 1, at] - one)

        for copy in backward(p):
            copy.start()
        brecv[p, slab] = bsend[p, me]

    def give_back_zero():
        @pl.when(odd_slab)
        def _():
            field_row(PLANES).wait_recv()

        @pl.when(is_middle)
        def _():
            for copy in fix_row(PLANES):
                copy.start()

            fix[PLANES] = field[PLANES, 2, pl.ds(me * OWN, OWN)]

        @pl.loop(0, GROUP)
        def _(q):
            for j in range(OWN):
                at = q * OWN + j
                one, two = field[PLANES, 1, at], field[PLANES, 2, at]
                row = field_edge[PLANES, at, end_row, :]
                zsend[q, j] = (slab_prior_lane(one) - one) - (slab_prior_row(two, row) - two)

        for copy in backward_zero():
            copy.start()
        zrecv[slab] = zsend[me]

    @pl.loop(0, PLANES)
    def _(k):
        p = PLANES - 1 - k

        @pl.when(p > 0)
        def _():
            forward_came(p)

            @pl.when(odd_slab)
            def _():
                chip_row(p).start()

            @pl.when(is_middle)
            def _():
                middle_came(p)

            @pl.when(even_slab)
            def _():
                chip_row(p).wait_recv()

        nonlinear(p)

        @pl.when(even_slab)
        def _():
            field_row(p).start()

        @pl.when(k == 0)
        def _():
            @pl.when(even_slab)
            def _():
                field_row(PLANES).start()

            @pl.when(tells_above)
            def _():
                pl.semaphore_wait(ready.at[1], 1)

            @pl.when(has_above)
            def _():
                down.start()

            give_back_zero()

        @pl.when(k > 0)
        def _():
            give_back(p + 1)

    @pl.when(has_below)
    def _():
        down.wait_recv()

    give_back(0)

    swap = to_sample(grad, grad_out, g_send, g_recv, lax.rem(me + 2, GROUP))

    @pl.when(swaps)
    def _():
        swap.start()

    @pl.when(jnp.logical_not(swaps))
    def _():
        grad_out[...] = grad[...]

    def fixed(parts, p, j, sign):
        row = jnp.where(slab_row == 0, fix[p, j, end_row, :], 0.0)
        parts[2] = parts[2] + row if sign > 0 else parts[2] - row
        return jnp.concatenate(parts, axis=0)

    objective.wait()
    all_of(zrecv.at[pl.ds(0, GROUP - 1)], b_recv.at[PLANES]).wait()

    @pl.when(off_middle)
    def _():
        fix_row(PLANES)[0].wait_recv()

    for j in range(OWN):
        below_sum[j] = fixed([zrecv[q, j] for q in range(GROUP)], PLANES, j, -1)

    @pl.loop(0, PLANES)
    def _(k):
        p = PLANES - 1 - k
        all_of(brecv.at[p, pl.ds(0, GROUP - 1)], b_recv.at[p]).wait()

        @pl.when(off_middle)
        def _():
            fix_row(p)[0].wait_recv()

        for j in range(OWN):
            zero = below_sum[j]
            one = brecv[p, :, j, 0].reshape(NY, NZ)
            two = fixed([brecv[p, q, j, 1] for q in range(GROUP)], p, j, 1)
            for c, part in enumerate((zero, one, two)):
                out[j, c, p] = obj[j, c, p] - part
            below_sum[j] = zero - (prior_row(one) - one) - (prior_lane(two) - two)

    @pl.when(swaps)
    def _():
        swap.wait()

    @pl.when(has_below)
    def _():
        up.wait_send()

    @pl.when(has_above)
    def _():
        down.wait_send()

    all_of(send.at[:, pl.ds(0, GROUP - 1)], f_send).wait()
    all_of(phi_send.at[pl.ds(0, GROUP - 1)], p_send).wait()
    all_of(bsend.at[:, pl.ds(0, GROUP - 1)], b_send).wait()
    all_of(zsend.at[pl.ds(0, GROUP - 1)], z_send).wait()

    @pl.when(off_middle)
    def _():
        all_of(edge.at[:, 0, :, top_row], mid_send).wait()

    @pl.when(is_middle)
    def _():
        all_of(field_edge.at[:, pl.ds(0, OWN * (GROUP - 1)), end_row], mid_send).wait()

    @pl.when(odd_slab)
    def _():
        all_of(edge.at[:, :, :, top_row], chip_send).wait()

    @pl.when(even_slab)
    def _():
        all_of(field_edge.at[:, :, end_row], chip_send).wait()


def write_out(held, held_grad, out_hbm, grad_hbm, sems):
    copies = [pltpu.make_async_copy(held.at[j], out_hbm.at[j], sems.at[j]) for j in range(OWN)]
    copies.append(pltpu.make_async_copy(held_grad, grad_hbm, sems.at[OWN]))
    for copy in copies:
        copy.start()
    for copy in copies:
        copy.wait()


def local(state_hat, adjoint_hat, objective_hat, density, region):
    f32 = jnp.float32
    hbm = pl.BlockSpec(memory_space=pl.ANY)
    dma = pltpu.SemaphoreType.DMA
    links = (PLANES + 1, GROUP - 1)
    residual = (OWN, 3, PLANES, NY, NZ)
    gradient = (PLANES, ROWS, NZ)
    vmem = pl.BlockSpec(memory_space=pltpu.VMEM)
    held = pl.pallas_call(
        kernel,
        out_shape=(pltpu.VMEM(residual, f32), pltpu.VMEM(gradient, f32)),
        in_specs=[hbm] * 5,
        out_specs=(vmem, vmem),
        scratch_shapes=[
            pltpu.VMEM((PLANES, 2, OWN, 3, NY, NZ), f32),
            pltpu.VMEM((PLANES, 2, OWN, NY, NZ), f32),
            pltpu.VMEM((OWN, 3, PLANES, NY, NZ), f32),
            pltpu.VMEM((PLANES, ROWS, NZ), f32),
            pltpu.VMEM((PLANES, ROWS, NZ), jnp.int32),
            pltpu.VMEM((GROUP, PAIRS, 2, ROWS, NZ), f32),
            pltpu.VMEM((PLANES, GROUP, PAIRS, 2, ROWS, NZ), f32),
            pltpu.VMEM((PLANES + 1, GROUP, PAIRS, 2, ROWS, NZ), f32),
            pltpu.VMEM((GROUP, PAIRS, ROWS, NZ), f32),
            pltpu.VMEM((GROUP, PAIRS, ROWS, NZ), f32),
            pltpu.VMEM((PLANES + 1, GROUP, PAIRS, ROWS, NZ), f32),
            pltpu.VMEM((PLANES, GROUP, OWN, 2, ROWS, NZ), f32),
            pltpu.VMEM((PLANES, GROUP, OWN, 2, ROWS, NZ), f32),
            pltpu.VMEM((GROUP, OWN, ROWS, NZ), f32),
            pltpu.VMEM((GROUP, OWN, ROWS, NZ), f32),
            pltpu.VMEM((6, GROUP, OWN, ROWS, NZ), f32),
            pltpu.VMEM((FOLDS, 4, 6, ROWS, NZ), f32),
            pltpu.VMEM((FOLDS, 4, 3, ROWS, NZ), f32),
            pltpu.VMEM((PLANES + 1, 3, NCOEF, ROWS, NZ), f32),
            pltpu.VMEM((PLANES + 1, NCOEF, ROWS, NZ), f32),
            pltpu.VMEM((PLANES + 1, OWN, ROWS, NZ), f32),
            pltpu.VMEM((OWN, NY, NZ), f32),
            pltpu.VMEM((PLANES, ROWS, NZ), f32),
            dma((2,)), dma, dma((2,)), dma, dma, dma, dma, dma,
            dma, dma, dma((PLANES + 1,)), dma, dma, dma((PLANES + 1,)),
            dma, dma((PLANES + 1,)), dma, dma((PLANES + 1,)),
            dma, dma, pltpu.SemaphoreType.REGULAR((2,)),
        ],
        compiler_params=pltpu.CompilerParams(
            collective_id=0, has_side_effects=True, vmem_limit_bytes=60 * 1024 * 1024
        ),
    )(state_hat, adjoint_hat, objective_hat, density, region)
    return pl.pallas_call(
        write_out,
        out_shape=(jax.ShapeDtypeStruct(residual, f32), jax.ShapeDtypeStruct(gradient, f32)),
        in_specs=[vmem, vmem],
        out_specs=(hbm, hbm),
        scratch_shapes=[dma((OWN + 1,))],
        compiler_params=pltpu.CompilerParams(vmem_limit_bytes=1024 * 1024),
    )(*held)


def solution(mesh):
    in_specs = (
        P("sample", None, "space", None, None),
        P("sample", None, "space", None, None),
        P("sample", None, "space", None, None),
        P("space", None, None),
        P("space", None, None),
    )
    out_specs = (P("sample", None, "space", None, None), P("space", "sample", None))
    return jax.shard_map(local, mesh=mesh, in_specs=in_specs, out_specs=out_specs, check_vma=False)
```

```python
import math

import jax
import jax.numpy as jnp
from jax import lax
from jax.experimental import pallas as pl
from jax.experimental.pallas import tpu as pltpu
from jax.sharding import PartitionSpec as P

NT = 40
NCOEF = 20
NY = 32
NZ = 128
PLANES = 8
GROUP = 4
OWN = NCOEF // GROUP
ROWS = NY // GROUP
FOLDS = NT // 4 + 1
PAIRS = 2 * OWN
RUN = 4

magnet_reluct = 0.95
iron_floor = 0.05

CLASSES = (
    ("cos", (2, 4, 6, 8, 10)),
    ("cos", (1, 3, 5, 7, 9)),
    ("sin", (2, 4, 6, 8, 10)),
    ("sin", (1, 3, 5, 7, 9)),
)


def coef_index(kind, order):
    return 2 * (order - 1) + (0 if kind == "cos" else 1)


def factor(kind, order, n):
    turn = (n * order) % NT
    quarter = NT // 4
    if kind == "sin":
        turn = (turn - quarter) % NT
    if turn % quarter == 0:
        return (1.0, 0.0, -1.0, 0.0)[turn // quarter]
    return math.cos(2.0 * math.pi * turn / NT)


def combine(terms, constants):
    total = None
    for term, constant in zip(terms, constants):
        if constant == 0.0:
            continue
        if constant == 1.0:
            piece = term
        elif constant == -1.0:
            piece = -term
        else:
            piece = term * jnp.float32(constant)
        total = piece if total is None else total + piece
    return jnp.zeros_like(terms[0]) if total is None else total


def kernel(
    state_hbm, adjoint_hbm, objective_hbm, density_hbm, region_hbm,
    out, grad_out,
    pot, phi, obj, dens, regn, upper, send, recv, phi_send, phi_recv, edge,
    bsend, brecv, zsend, zrecv, flux, wave, fold, field, field_edge, fix, below_sum, grad,
    in_sems, obj_sem, mat_sems, own_sem, up_send, up_recv, low_send, low_recv,
    f_send, p_send, f_recv, b_send, z_send, b_recv, chip_send, chip_recv, mid_send, mid_recv,
    g_send, g_recv, ready,
):
    me = lax.axis_index("sample")
    block = lax.axis_index("space")
    blocks = lax.axis_size("space")
    above = lax.rem(block + 1, blocks)
    below = lax.rem(block + blocks - 1, blocks)
    has_above, has_below = block < blocks - 1, block > 0
    mesh_id = pl.DeviceIdType.MESH

    def turned(index, where):
        return lax.rem(index + 2 * lax.rem(where // RUN, 2), GROUP)

    swaps = lax.rem(block // RUN, 2) == 1
    slab = turned(me, block)
    odd_slab = lax.rem(me, 2) == 1
    even_slab = jnp.logical_not(odd_slab)
    partner = me + 1 - 2 * lax.rem(me, 2)
    middle = turned(1, block)
    is_middle = me == middle
    off_middle = me != middle
    up_id = {"space": above, "sample": turned(slab, above)}
    down_id = {"space": below, "sample": turned(slab, below)}
    peers = [lax.rem(me + 2, GROUP), lax.rem(partner + 2, GROUP), partner]
    arguments = (state_hbm, adjoint_hbm)

    def to_sample(source, target, send_sem, recv_sem, peer):
        return pltpu.make_async_remote_copy(
            src_ref=source, dst_ref=target, send_sem=send_sem, recv_sem=recv_sem,
            device_id={"sample": peer}, device_id_type=mesh_id,
        )

    barrier = pltpu.get_barrier_semaphore()
    for peer in peers:
        pl.semaphore_signal(barrier, inc=1, device_id={"sample": peer}, device_id_type=mesh_id)

    ends, begins = lax.rem(block, RUN) == RUN - 1, lax.rem(block, RUN) == 0
    waits_above, waits_below = has_above & ends, has_below & jnp.logical_not(begins)
    tells_above, tells_below = has_above & jnp.logical_not(ends), has_below & begins

    @pl.when(tells_above)
    def _():
        pl.semaphore_signal(barrier, inc=1, device_id=up_id, device_id_type=mesh_id)

    @pl.when(tells_below)
    def _():
        pl.semaphore_signal(barrier, inc=1, device_id=down_id, device_id_type=mesh_id)

    def slab_rows(s):
        return pl.ds(pl.multiple_of(s * ROWS, ROWS), ROWS)

    def load(p):
        return [
            pltpu.make_async_copy(ref.at[:, :, p], pot.at[p, i], in_sems.at[min(p, 1) if isinstance(p, int) else 1])
            for i, ref in enumerate(arguments)
        ]

    def all_of(ref, sem):
        return pltpu.make_async_copy(ref, ref, sem)

    for copy in load(0):
        copy.start()

    own = [
        pltpu.make_async_copy(
            ref.at[:, pl.ds(1, 2), 0, slab_rows(slab)], recv.at[0, me, pl.ds(i * OWN, OWN)], own_sem
        )
        for i, ref in enumerate(arguments)
    ]
    for copy in own:
        copy.start()

    @pl.loop(1, PLANES)
    def _(p):
        for copy in load(p):
            copy.start()

    material = [
        pltpu.make_async_copy(density_hbm.at[:, slab_rows(slab)], dens, mat_sems.at[0]),
        pltpu.make_async_copy(region_hbm.at[:, slab_rows(slab)], regn, mat_sems.at[1]),
    ]
    for copy in material:
        copy.start()
    objective = pltpu.make_async_copy(objective_hbm, obj, obj_sem)
    objective.start()

    def forward_first():
        return [
            to_sample(
                pot.at[0, i, :, pl.ds(1, 2), slab_rows(turned(peer, block))],
                recv.at[0, me, pl.ds(i * OWN, OWN)],
                f_send, f_recv.at[0], peer,
            )
            for peer in peers
            for i in range(2)
        ]

    def forward(p):
        return [
            to_sample(
                send.at[p, turned(peer, block)], recv.at[p, me], f_send, f_recv.at[p], peer
            )
            for peer in peers
        ]

    def forward_came(p):
        all_of(recv.at[p, pl.ds(0, GROUP - 1)], f_recv.at[p]).wait()

    def forward_phi():
        return [
            to_sample(
                phi_send.at[turned(peer, block)], phi_recv.at[me],
                p_send, f_recv.at[PLANES], peer,
            )
            for peer in peers
        ]

    def backward(p):
        return [
            to_sample(bsend.at[p, peer], brecv.at[p, slab], b_send, b_recv.at[p], peer)
            for peer in peers
        ]

    def backward_zero():
        return [
            to_sample(zsend.at[peer], zrecv.at[slab], z_send, b_recv.at[PLANES], peer)
            for peer in peers
        ]

    top_row, end_row = pl.ds(0, 1), pl.ds(ROWS - 1, 1)

    def middle_row(p, q):
        source = send.at[p, 2, :, 1, top_row]
        return to_sample(source, edge.at[p, q, :, top_row], mid_send, mid_recv.at[p], middle)

    def middle_phi(q):
        source = phi_send.at[2, :, top_row]
        return to_sample(source, edge.at[PLANES, q, :, top_row], mid_send, mid_recv.at[PLANES], middle)

    def middle_came(p):
        all_of(edge.at[p, pl.ds(0, GROUP - 1), :, top_row], mid_recv.at[p]).wait()

    def chip_row(p):
        return to_sample(recv.at[p, :, :, 1, top_row], edge.at[p, :, :, top_row], chip_send, chip_recv.at[p], partner)

    def chip_phi():
        return to_sample(
            phi_recv.at[:, :, top_row], edge.at[PLANES, :, :, top_row],
            chip_send, chip_recv.at[PLANES], partner,
        )

    def last_rows(p, some):
        if isinstance(p, int) and p == PLANES:
            return field.at[PLANES, 2, some, end_row]
        return field.at[p + 1, 0, some, end_row]

    def field_row(p):
        return to_sample(
            last_rows(p, pl.ds(0, NCOEF)), field_edge.at[p, :, end_row], chip_send, chip_recv.at[p], partner
        )

    def fix_row(p):
        return [
            to_sample(
                last_rows(p, pl.ds(peer * OWN, OWN)), fix.at[p, :, end_row], mid_send, mid_recv.at[p], peer
            )
            for peer in peers
        ]

    row_id = lax.broadcasted_iota(jnp.int32, (NY, NZ), 0)
    lane_id = lax.broadcasted_iota(jnp.int32, (NY, NZ), 1)
    slab_row = lax.broadcasted_iota(jnp.int32, (ROWS, NZ), 0)
    slab_lane = lax.broadcasted_iota(jnp.int32, (ROWS, NZ), 1)

    def next_row(a):
        return jnp.where(row_id == NY - 1, 0.0, pltpu.roll(a, NY - 1, 0))

    def next_lane(a):
        return jnp.where(lane_id == NZ - 1, 0.0, pltpu.roll(a, NZ - 1, 1))

    def prior_row(a):
        return jnp.where(row_id == 0, 0.0, pltpu.roll(a, 1, 0))

    def prior_lane(a):
        return jnp.where(lane_id == 0, 0.0, pltpu.roll(a, 1, 1))

    def slab_next_row(a, row):
        return jnp.where(slab_row == ROWS - 1, row, pltpu.roll(a, ROWS - 1, 0))

    def slab_next_lane(a):
        return jnp.where(slab_lane == NZ - 1, 0.0, pltpu.roll(a, NZ - 1, 1))

    def slab_prior_row(a, row):
        return jnp.where(slab_row == 0, row, pltpu.roll(a, 1, 0))

    def slab_prior_lane(a):
        return jnp.where(slab_lane == 0, 0.0, pltpu.roll(a, 1, 1))

    pl.semaphore_wait(barrier, GROUP - 1 + waits_above.astype(jnp.int32) + waits_below.astype(jnp.int32))
    all_of(pot.at[0], in_sems.at[0]).wait()
    for copy in forward_first():
        copy.start()

    @pl.when(waits_above)
    def _():
        pl.semaphore_signal(ready.at[0], inc=1, device_id=up_id, device_id_type=mesh_id)

    @pl.when(waits_below)
    def _():
        pl.semaphore_signal(ready.at[1], inc=1, device_id=down_id, device_id_type=mesh_id)

    for i in range(2):
        for j in range(OWN):
            phi[0, i, j] = pot[0, i, j, 0]
            send[0, 2, i * OWN + j, 1] = pot[0, i, j, 2, pl.ds(2 * ROWS, ROWS), :]

    all_of(pot.at[pl.ds(1, PLANES - 1)], in_sems.at[1]).wait()

    @pl.loop(1, PLANES)
    def _(p):
        for i in range(2):
            @pl.loop(0, OWN)
            def _(j):
                phi[p, i, j] = phi[p - 1, i, j] + pot[p, i, j, 0]

    for i in range(2):
        for j in range(OWN):
            phi_send[:, i * OWN + j] = phi[PLANES - 1, i, j].reshape(GROUP, ROWS, NZ)
    phi_recv[me] = phi_send[slab]
    for copy in forward_phi():
        copy.start()

    @pl.when(off_middle)
    def _():
        middle_phi(me).start()
        middle_row(0, me).start()

    @pl.when(is_middle)
    def _():
        for ij in range(PAIRS):
            edge[PLANES, me, ij] = phi_send[2, ij]
            edge[0, me, ij] = send[0, 2, ij, 1]

    @pl.loop(0, PLANES - 1)
    def _(k):
        p = PLANES - 1 - k
        for i in range(2):
            for j in range(OWN):
                under = phi[p - 1, i, j]
                one = pot[p, i, j, 1] - (next_row(under) - under)
                two = pot[p, i, j, 2] - (next_lane(under) - under)
                send[p, :, i * OWN + j, 0] = one.reshape(GROUP, ROWS, NZ)
                send[p, :, i * OWN + j, 1] = two.reshape(GROUP, ROWS, NZ)
        for copy in forward(p):
            copy.start()

        @pl.when(off_middle)
        def _():
            middle_row(p, me).start()

        @pl.when(is_middle)
        def _():
            for ij in range(PAIRS):
                edge[p, me, ij] = send[p, 2, ij, 1]

        recv[p, me] = send[p, slab]

    @pl.when(even_slab)
    def _():
        @pl.loop(0, PLANES + 1)
        def _(p):
            field_edge[p] = jnp.zeros((NCOEF, ROWS, NZ), jnp.float32)

    @pl.when(slab == GROUP - 1)
    def _():
        @pl.loop(0, PLANES + 1)
        def _(p):
            edge[p] = jnp.zeros((GROUP, PAIRS, ROWS, NZ), jnp.float32)

    @pl.when(jnp.logical_not(has_above))
    def _():
        upper[...] = jnp.zeros_like(upper)

    @pl.when(jnp.logical_not(has_below))
    def _():
        field[0, pl.ds(1, 2)] = jnp.zeros((2, NCOEF, ROWS, NZ), jnp.float32)

    all_of(recv.at[0, 0], own_sem).wait()
    forward_came(0)
    up = pltpu.make_async_remote_copy(
        src_ref=recv.at[0], dst_ref=upper,
        send_sem=up_send, recv_sem=up_recv, device_id=down_id, device_id_type=mesh_id,
    )

    @pl.when(tells_below)
    def _():
        pl.semaphore_wait(ready.at[0], 1)

    @pl.when(has_below)
    def _():
        up.start()

    for copy in material:
        copy.wait()
    all_of(phi_recv.at[pl.ds(0, GROUP - 1)], f_recv.at[PLANES]).wait()

    @pl.when(odd_slab)
    def _():
        chip_phi().start()
        chip_row(0).start()

    @pl.when(is_middle)
    def _():
        middle_came(PLANES)
        middle_came(0)

    @pl.when(even_slab)
    def _():
        chip_phi().wait_recv()
        chip_row(0).wait_recv()

    @pl.when(has_above)
    def _():
        up.wait_recv()

    @pl.loop(0, GROUP)
    def _(q):
        for ij in range(PAIRS):
            top = phi_recv[q, ij]
            row = edge[PLANES, q, ij, top_row, :]
            recv[PLANES, q, ij, 0] = upper[q, ij, 0] - (slab_next_row(top, row) - top)
            recv[PLANES, q, ij, 1] = upper[q, ij, 1] - (slab_next_lane(top) - top)

    down = pltpu.make_async_remote_copy(
        src_ref=field.at[PLANES, pl.ds(1, 2)], dst_ref=field.at[0, pl.ds(1, 2)],
        send_sem=low_send, recv_sem=low_recv, device_id=up_id, device_id_type=mesh_id,
    )

    def nonlinear(p):
        @pl.loop(0, GROUP)
        def _(q):
            for i in range(2):
                for j in range(OWN):
                    ij = i * OWN + j
                    one, two = recv[p, q, ij, 0], recv[p, q, ij, 1]
                    row = edge[p, q, ij, top_row, :]
                    flux[3 * i, q, j] = (slab_next_row(two, row) - two) - (slab_next_lane(one) - one)
                    flux[3 * i + 1, q, j] = two - recv[p + 1, q, ij, 1]
                    flux[3 * i + 2, q, j] = recv[p + 1, q, ij, 0] - one

        @pl.loop(0, 6)
        def _(pc):
            for t, (kind, orders) in enumerate(CLASSES):
                where = [coef_index(kind, m) for m in orders]
                terms = [flux[pc, c // OWN, c % OWN] for c in where]
                for n in range(FOLDS):
                    wave[n, t, pc] = combine(terms, [factor(kind, m, n) for m in orders])

        density, region = dens[p], regn[p]
        iron = region == 0
        share = jnp.where(iron, density * density * density, 0.0) * jnp.float32(1.0 - iron_floor)
        slope = jnp.where(iron, 3.0 * density * density, 0.0)
        base = jnp.where(region == 1, jnp.float32(magnet_reluct), jnp.float32(1.0))

        def samples(n, total):
            state = [[], [], []]
            adjoint = [[], [], []]
            for pc in range(6):
                ce, co, se, so = (wave[n, t, pc] for t in range(4))
                a, b, d, f = ce + co, ce - co, se + so, se - so
                (state if pc < 3 else adjoint)[pc % 3] = (a + d, a - d, b - f, b + f)
            values = [[], [], []]
            part = None
            for v in range(4):
                s = [state[c][v] for c in range(3)]
                g = [adjoint[c][v] for c in range(3)]
                square = s[0] * s[0] + s[1] * s[1] + s[2] * s[2]
                inner = s[0] * g[0] + s[1] * g[1] + s[2] * g[2]
                r = 1.0 / (square + 1.0)
                t = share * r
                ri = r * inner
                nu = base - t
                mu = (t + t) * ri
                part = ri if part is None else part + ri
                for c in range(3):
                    values[c].append(nu * g[c] + mu * s[c])
            for c in range(3):
                w, x, y, z = values[c]
                a, d = w + x, w - x
                b, f = z + y, z - y
                fold[n, 0, c] = a + b
                fold[n, 1, c] = a - b
                fold[n, 2, c] = d + f
                fold[n, 3, c] = d - f
            ends = (n == 0) | (n == FOLDS - 1)
            return total + part * jnp.where(ends, 0.5, 1.0)

        total = lax.fori_loop(0, FOLDS, samples, jnp.zeros((ROWS, NZ), jnp.float32))
        grad[p] = total * slope * jnp.float32((1.0 - iron_floor) / NT)

        for t, (kind, orders) in enumerate(CLASSES):
            for c in range(3):
                terms = [fold[n, t, c] for n in range(FOLDS)]
                for m in orders:
                    scales = [
                        factor(kind, m, n) * (1.0 if 0 < n < FOLDS - 1 else 0.5) * 2.0 / NT
                        for n in range(FOLDS)
                    ]
                    field[p + 1, c, coef_index(kind, m)] = combine(terms, scales)

    def give_back(p):
        @pl.when(odd_slab)
        def _():
            field_row(p).wait_recv()

        @pl.when(is_middle)
        def _():
            for copy in fix_row(p):
                copy.start()

            fix[p] = field[p + 1, 0, pl.ds(me * OWN, OWN)]

        @pl.loop(0, GROUP)
        def _(q):
            for j in range(OWN):
                at = q * OWN + j
                zero, one, two = (field[p + 1, c, at] for c in range(3))
                row = field_edge[p, at, end_row, :]
                bsend[p, q, j, 0] = (field[p, 2, at] - two) - (slab_prior_lane(zero) - zero)
                bsend[p, q, j, 1] = (slab_prior_row(zero, row) - zero) - (field[p, 1, at] - one)

        for copy in backward(p):
            copy.start()
        brecv[p, slab] = bsend[p, me]

    def give_back_zero():
        @pl.when(odd_slab)
        def _():
            field_row(PLANES).wait_recv()

        @pl.when(is_middle)
        def _():
            for copy in fix_row(PLANES):
                copy.start()

            fix[PLANES] = field[PLANES, 2, pl.ds(me * OWN, OWN)]

        @pl.loop(0, GROUP)
        def _(q):
            for j in range(OWN):
                at = q * OWN + j
                one, two = field[PLANES, 1, at], field[PLANES, 2, at]
                row = field_edge[PLANES, at, end_row, :]
                zsend[q, j] = (slab_prior_lane(one) - one) - (slab_prior_row(two, row) - two)

        for copy in backward_zero():
            copy.start()
        zrecv[slab] = zsend[me]

    @pl.loop(0, PLANES)
    def _(k):
        p = PLANES - 1 - k

        @pl.when(p > 0)
        def _():
            forward_came(p)

            @pl.when(odd_slab)
            def _():
                chip_row(p).start()

            @pl.when(is_middle)
            def _():
                middle_came(p)

            @pl.when(even_slab)
            def _():
                chip_row(p).wait_recv()

        nonlinear(p)

        @pl.when(even_slab)
        def _():
            field_row(p).start()

        @pl.when(k == 0)
        def _():
            @pl.when(even_slab)
            def _():
                field_row(PLANES).start()

            @pl.when(tells_above)
            def _():
                pl.semaphore_wait(ready.at[1], 1)

            @pl.when(has_above)
            def _():
                down.start()

            give_back_zero()

        @pl.when(k > 0)
        def _():
            give_back(p + 1)

    @pl.when(has_below)
    def _():
        down.wait_recv()

    give_back(0)

    swap = to_sample(grad, grad_out, g_send, g_recv, lax.rem(me + 2, GROUP))

    @pl.when(swaps)
    def _():
        swap.start()

    @pl.when(jnp.logical_not(swaps))
    def _():
        grad_out[...] = grad[...]

    def fixed(parts, p, j, sign):
        row = jnp.where(slab_row == 0, fix[p, j, end_row, :], 0.0)
        parts[2] = parts[2] + row if sign > 0 else parts[2] - row
        return jnp.concatenate(parts, axis=0)

    objective.wait()
    all_of(zrecv.at[pl.ds(0, GROUP - 1)], b_recv.at[PLANES]).wait()

    @pl.when(off_middle)
    def _():
        fix_row(PLANES)[0].wait_recv()

    for j in range(OWN):
        below_sum[j] = fixed([zrecv[q, j] for q in range(GROUP)], PLANES, j, -1)

    @pl.loop(0, PLANES)
    def _(k):
        p = PLANES - 1 - k
        all_of(brecv.at[p, pl.ds(0, GROUP - 1)], b_recv.at[p]).wait()

        @pl.when(off_middle)
        def _():
            fix_row(p)[0].wait_recv()

        for j in range(OWN):
            zero = below_sum[j]
            one = brecv[p, :, j, 0].reshape(NY, NZ)
            two = fixed([brecv[p, q, j, 1] for q in range(GROUP)], p, j, 1)
            for c, part in enumerate((zero, one, two)):
                out[j, c, p] = obj[j, c, p] - part
            below_sum[j] = zero - (prior_row(one) - one) - (prior_lane(two) - two)

    @pl.when(swaps)
    def _():
        swap.wait()

    @pl.when(has_below)
    def _():
        up.wait_send()

    @pl.when(has_above)
    def _():
        down.wait_send()

    all_of(send.at[:, pl.ds(0, GROUP - 1)], f_send).wait()
    all_of(phi_send.at[pl.ds(0, GROUP - 1)], p_send).wait()
    all_of(bsend.at[:, pl.ds(0, GROUP - 1)], b_send).wait()
    all_of(zsend.at[pl.ds(0, GROUP - 1)], z_send).wait()

    @pl.when(off_middle)
    def _():
        all_of(edge.at[:, 0, :, top_row], mid_send).wait()

    @pl.when(is_middle)
    def _():
        all_of(field_edge.at[:, pl.ds(0, OWN * (GROUP - 1)), end_row], mid_send).wait()

    @pl.when(odd_slab)
    def _():
        all_of(edge.at[:, :, :, top_row], chip_send).wait()

    @pl.when(even_slab)
    def _():
        all_of(field_edge.at[:, :, end_row], chip_send).wait()


def write_out(held, held_grad, out_hbm, grad_hbm, sems):
    copies = [pltpu.make_async_copy(held.at[j], out_hbm.at[j], sems.at[j]) for j in range(OWN)]
    copies.append(pltpu.make_async_copy(held_grad, grad_hbm, sems.at[OWN]))
    for copy in copies:
        copy.start()
    for copy in copies:
        copy.wait()


def local(state_hat, adjoint_hat, objective_hat, density, region):
    f32 = jnp.float32
    hbm = pl.BlockSpec(memory_space=pl.ANY)
    dma = pltpu.SemaphoreType.DMA
    links = (PLANES + 1, GROUP - 1)
    residual = (OWN, 3, PLANES, NY, NZ)
    gradient = (PLANES, ROWS, NZ)
    vmem = pl.BlockSpec(memory_space=pltpu.VMEM)
    held = pl.pallas_call(
        kernel,
        out_shape=(pltpu.VMEM(residual, f32), pltpu.VMEM(gradient, f32)),
        in_specs=[hbm] * 5,
        out_specs=(vmem, vmem),
        scratch_shapes=[
            pltpu.VMEM((PLANES, 2, OWN, 3, NY, NZ), f32),
            pltpu.VMEM((PLANES, 2, OWN, NY, NZ), f32),
            pltpu.VMEM((OWN, 3, PLANES, NY, NZ), f32),
            pltpu.VMEM((PLANES, ROWS, NZ), f32),
            pltpu.VMEM((PLANES, ROWS, NZ), jnp.int32),
            pltpu.VMEM((GROUP, PAIRS, 2, ROWS, NZ), f32),
            pltpu.VMEM((PLANES, GROUP, PAIRS, 2, ROWS, NZ), f32),
            pltpu.VMEM((PLANES + 1, GROUP, PAIRS, 2, ROWS, NZ), f32),
            pltpu.VMEM((GROUP, PAIRS, ROWS, NZ), f32),
            pltpu.VMEM((GROUP, PAIRS, ROWS, NZ), f32),
            pltpu.VMEM((PLANES + 1, GROUP, PAIRS, ROWS, NZ), f32),
            pltpu.VMEM((PLANES, GROUP, OWN, 2, ROWS, NZ), f32),
            pltpu.VMEM((PLANES, GROUP, OWN, 2, ROWS, NZ), f32),
            pltpu.VMEM((GROUP, OWN, ROWS, NZ), f32),
            pltpu.VMEM((GROUP, OWN, ROWS, NZ), f32),
            pltpu.VMEM((6, GROUP, OWN, ROWS, NZ), f32),
            pltpu.VMEM((FOLDS, 4, 6, ROWS, NZ), f32),
            pltpu.VMEM((FOLDS, 4, 3, ROWS, NZ), f32),
            pltpu.VMEM((PLANES + 1, 3, NCOEF, ROWS, NZ), f32),
            pltpu.VMEM((PLANES + 1, NCOEF, ROWS, NZ), f32),
            pltpu.VMEM((PLANES + 1, OWN, ROWS, NZ), f32),
            pltpu.VMEM((OWN, NY, NZ), f32),
            pltpu.VMEM((PLANES, ROWS, NZ), f32),
            dma((2,)), dma, dma((2,)), dma, dma, dma, dma, dma,
            dma, dma, dma((PLANES + 1,)), dma, dma, dma((PLANES + 1,)),
            dma, dma((PLANES + 1,)), dma, dma((PLANES + 1,)),
            dma, dma, pltpu.SemaphoreType.REGULAR((2,)),
        ],
        compiler_params=pltpu.CompilerParams(
            collective_id=0, has_side_effects=True, vmem_limit_bytes=60 * 1024 * 1024
        ),
    )(state_hat, adjoint_hat, objective_hat, density, region)
    return pl.pallas_call(
        write_out,
        out_shape=(jax.ShapeDtypeStruct(residual, f32), jax.ShapeDtypeStruct(gradient, f32)),
        in_specs=[vmem, vmem],
        out_specs=(hbm, hbm),
        scratch_shapes=[dma((OWN + 1,))],
        compiler_params=pltpu.CompilerParams(vmem_limit_bytes=1024 * 1024),
    )(*held)


def solution(mesh):
    in_specs = (
        P("sample", None, "space", None, None),
        P("sample", None, "space", None, None),
        P("sample", None, "space", None, None),
        P("space", None, None),
        P("space", None, None),
    )
    out_specs = (P("sample", None, "space", None, None), P("space", "sample", None))
    return jax.shard_map(local, mesh=mesh, in_specs=in_specs, out_specs=out_specs, check_vma=False)
```

```python
import math

import jax
import jax.numpy as jnp
from jax import lax
from jax.experimental import pallas as pl
from jax.experimental.pallas import tpu as pltpu
from jax.sharding import PartitionSpec as P

NT = 40
NCOEF = 20
NY = 32
NZ = 128
PLANES = 8
GROUP = 4
OWN = NCOEF // GROUP
ROWS = NY // GROUP
FOLDS = NT // 4 + 1
PAIRS = 2 * OWN
RUN = 4
HALF = PLANES // 2

magnet_reluct = 0.95
iron_floor = 0.05

CLASSES = (
    ("cos", (2, 4, 6, 8, 10)),
    ("cos", (1, 3, 5, 7, 9)),
    ("sin", (2, 4, 6, 8, 10)),
    ("sin", (1, 3, 5, 7, 9)),
)


def coef_index(kind, order):
    return 2 * (order - 1) + (0 if kind == "cos" else 1)


def factor(kind, order, n):
    turn = (n * order) % NT
    quarter = NT // 4
    if kind == "sin":
        turn = (turn - quarter) % NT
    if turn % quarter == 0:
        return (1.0, 0.0, -1.0, 0.0)[turn // quarter]
    return math.cos(2.0 * math.pi * turn / NT)


def combine(terms, constants):
    total = None
    for term, constant in zip(terms, constants):
        if constant == 0.0:
            continue
        if constant == 1.0:
            piece = term
        elif constant == -1.0:
            piece = -term
        else:
            piece = term * jnp.float32(constant)
        total = piece if total is None else total + piece
    return jnp.zeros_like(terms[0]) if total is None else total


def kernel(
    state_hbm, adjoint_hbm, objective_hbm, density_hbm, region_hbm,
    out, grad_out,
    pot, phi, obj, dens, regn, upper, send, recv, phi_send, phi_recv, edge,
    bsend, brecv, zsend, zrecv, flux, wave, fold, field, field_edge, fix, below_sum, grad,
    in_sems, obj_sem, mat_sems, own_sem, up_send, up_recv, low_send, low_recv,
    f_send, p_send, f_recv, b_send, z_send, b_recv, chip_send, chip_recv, mid_send, mid_recv,
    g_send, g_recv, ready,
):
    me = lax.axis_index("sample")
    block = lax.axis_index("space")
    blocks = lax.axis_size("space")
    above = lax.rem(block + 1, blocks)
    below = lax.rem(block + blocks - 1, blocks)
    has_above, has_below = block < blocks - 1, block > 0
    mesh_id = pl.DeviceIdType.MESH

    def turned(index, where):
        return lax.rem(index + 2 * lax.rem(where // RUN, 2), GROUP)

    swaps = lax.rem(block // RUN, 2) == 1
    slab = turned(me, block)
    odd_slab = lax.rem(me, 2) == 1
    even_slab = jnp.logical_not(odd_slab)
    partner = me + 1 - 2 * lax.rem(me, 2)
    middle = turned(1, block)
    is_middle = me == middle
    off_middle = me != middle
    up_id = {"space": above, "sample": turned(slab, above)}
    down_id = {"space": below, "sample": turned(slab, below)}
    peers = [lax.rem(me + 2, GROUP), lax.rem(partner + 2, GROUP), partner]
    arguments = (state_hbm, adjoint_hbm)

    def to_sample(source, target, send_sem, recv_sem, peer):
        return pltpu.make_async_remote_copy(
            src_ref=source, dst_ref=target, send_sem=send_sem, recv_sem=recv_sem,
            device_id={"sample": peer}, device_id_type=mesh_id,
        )

    barrier = pltpu.get_barrier_semaphore()
    for peer in peers:
        pl.semaphore_signal(barrier, inc=1, device_id={"sample": peer}, device_id_type=mesh_id)

    ends, begins = lax.rem(block, RUN) == RUN - 1, lax.rem(block, RUN) == 0
    waits_above, waits_below = has_above & ends, has_below & jnp.logical_not(begins)
    tells_above, tells_below = has_above & jnp.logical_not(ends), has_below & begins

    @pl.when(tells_above)
    def _():
        pl.semaphore_signal(barrier, inc=1, device_id=up_id, device_id_type=mesh_id)

    @pl.when(tells_below)
    def _():
        pl.semaphore_signal(barrier, inc=1, device_id=down_id, device_id_type=mesh_id)

    def slab_rows(s):
        return pl.ds(pl.multiple_of(s * ROWS, ROWS), ROWS)

    def load(p):
        return [
            pltpu.make_async_copy(ref.at[:, :, p], pot.at[p, i], in_sems.at[min(p, 1) if isinstance(p, int) else 1])
            for i, ref in enumerate(arguments)
        ]

    def all_of(ref, sem):
        return pltpu.make_async_copy(ref, ref, sem)

    for copy in load(0):
        copy.start()

    own = [
        pltpu.make_async_copy(
            ref.at[:, pl.ds(1, 2), 0, slab_rows(slab)], recv.at[0, me, pl.ds(i * OWN, OWN)], own_sem
        )
        for i, ref in enumerate(arguments)
    ]
    for copy in own:
        copy.start()

    @pl.loop(1, PLANES)
    def _(p):
        for copy in load(p):
            copy.start()

    material = [
        pltpu.make_async_copy(density_hbm.at[:, slab_rows(slab)], dens, mat_sems.at[0]),
        pltpu.make_async_copy(region_hbm.at[:, slab_rows(slab)], regn, mat_sems.at[1]),
    ]
    for copy in material:
        copy.start()
    objective = pltpu.make_async_copy(objective_hbm, obj, obj_sem)
    objective.start()

    def forward_first():
        return [
            to_sample(
                pot.at[0, i, :, pl.ds(1, 2), slab_rows(turned(peer, block))],
                recv.at[0, me, pl.ds(i * OWN, OWN)],
                f_send, f_recv.at[0], peer,
            )
            for peer in peers
            for i in range(2)
        ]

    def forward(p):
        return [
            to_sample(
                send.at[p, turned(peer, block)], recv.at[p, me], f_send, f_recv.at[3 - p // HALF], peer
            )
            for peer in peers
        ]

    groups = (pl.ds(0, 1), pl.ds(PLANES, 1), pl.ds(HALF, HALF), pl.ds(1, HALF - 1))

    def forward_came(g):
        all_of(recv.at[groups[g], pl.ds(0, GROUP - 1)], f_recv.at[g]).wait()

    def forward_phi():
        return [
            to_sample(
                phi_send.at[turned(peer, block)], phi_recv.at[me],
                p_send, f_recv.at[1], peer,
            )
            for peer in peers
        ]

    def backward(p, g):
        return [
            to_sample(bsend.at[p, peer], brecv.at[p, slab], b_send, b_recv.at[g], peer)
            for peer in peers
        ]

    def backward_zero():
        return [
            to_sample(zsend.at[peer], zrecv.at[slab], z_send, b_recv.at[2], peer)
            for peer in peers
        ]

    top_row, end_row = pl.ds(0, 1), pl.ds(ROWS - 1, 1)

    def middle_row(p, q, g):
        source = send.at[p, 2, :, 1, top_row]
        return to_sample(source, edge.at[p, q, :, top_row], mid_send, mid_recv.at[g], middle)

    def middle_phi(q):
        source = phi_send.at[2, :, top_row]
        return to_sample(source, edge.at[PLANES, q, :, top_row], mid_send, mid_recv.at[1], middle)

    def middle_came(g):
        all_of(edge.at[groups[g], pl.ds(0, GROUP - 1), :, top_row], mid_recv.at[g]).wait()

    def chip_row(p):
        return to_sample(recv.at[p, :, :, 1, top_row], edge.at[p, :, :, top_row], chip_send, chip_recv.at[p], partner)

    def chip_phi():
        return to_sample(
            phi_recv.at[:, :, top_row], edge.at[PLANES, :, :, top_row],
            chip_send, chip_recv.at[PLANES], partner,
        )

    def last_rows(p, some):
        if isinstance(p, int) and p == PLANES:
            return field.at[PLANES, 2, some, end_row]
        return field.at[p + 1, 0, some, end_row]

    def field_row(p):
        return to_sample(
            last_rows(p, pl.ds(0, NCOEF)), field_edge.at[p, :, end_row], chip_send, chip_recv.at[p], partner
        )

    def fix_row(p, g):
        return [
            to_sample(
                last_rows(p, pl.ds(peer * OWN, OWN)), fix.at[p, :, end_row], mid_send, mid_recv.at[g], peer
            )
            for peer in peers
        ]

    row_id = lax.broadcasted_iota(jnp.int32, (NY, NZ), 0)
    lane_id = lax.broadcasted_iota(jnp.int32, (NY, NZ), 1)
    slab_row = lax.broadcasted_iota(jnp.int32, (ROWS, NZ), 0)
    slab_lane = lax.broadcasted_iota(jnp.int32, (ROWS, NZ), 1)

    def next_row(a):
        return jnp.where(row_id == NY - 1, 0.0, pltpu.roll(a, NY - 1, 0))

    def next_lane(a):
        return jnp.where(lane_id == NZ - 1, 0.0, pltpu.roll(a, NZ - 1, 1))

    def prior_row(a):
        return jnp.where(row_id == 0, 0.0, pltpu.roll(a, 1, 0))

    def prior_lane(a):
        return jnp.where(lane_id == 0, 0.0, pltpu.roll(a, 1, 1))

    def slab_next_row(a, row):
        return jnp.where(slab_row == ROWS - 1, row, pltpu.roll(a, ROWS - 1, 0))

    def slab_next_lane(a):
        return jnp.where(slab_lane == NZ - 1, 0.0, pltpu.roll(a, NZ - 1, 1))

    def slab_prior_row(a, row):
        return jnp.where(slab_row == 0, row, pltpu.roll(a, 1, 0))

    def slab_prior_lane(a):
        return jnp.where(slab_lane == 0, 0.0, pltpu.roll(a, 1, 1))

    pl.semaphore_wait(barrier, GROUP - 1 + waits_above.astype(jnp.int32) + waits_below.astype(jnp.int32))
    all_of(pot.at[0], in_sems.at[0]).wait()
    for copy in forward_first():
        copy.start()

    @pl.when(waits_above)
    def _():
        pl.semaphore_signal(ready.at[0], inc=1, device_id=up_id, device_id_type=mesh_id)

    @pl.when(waits_below)
    def _():
        pl.semaphore_signal(ready.at[1], inc=1, device_id=down_id, device_id_type=mesh_id)

    for i in range(2):
        for j in range(OWN):
            phi[0, i, j] = pot[0, i, j, 0]
            send[0, 2, i * OWN + j, 1] = pot[0, i, j, 2, pl.ds(2 * ROWS, ROWS), :]

    all_of(pot.at[pl.ds(1, PLANES - 1)], in_sems.at[1]).wait()

    @pl.loop(1, PLANES)
    def _(p):
        for i in range(2):
            @pl.loop(0, OWN)
            def _(j):
                phi[p, i, j] = phi[p - 1, i, j] + pot[p, i, j, 0]

    for i in range(2):
        for j in range(OWN):
            phi_send[:, i * OWN + j] = phi[PLANES - 1, i, j].reshape(GROUP, ROWS, NZ)
    phi_recv[me] = phi_send[slab]
    for copy in forward_phi():
        copy.start()

    @pl.when(off_middle)
    def _():
        middle_phi(me).start()
        middle_row(0, me, 0).start()

    @pl.when(is_middle)
    def _():
        for ij in range(PAIRS):
            edge[PLANES, me, ij] = phi_send[2, ij]
            edge[0, me, ij] = send[0, 2, ij, 1]

    @pl.loop(0, PLANES - 1)
    def _(k):
        p = PLANES - 1 - k
        for i in range(2):
            for j in range(OWN):
                under = phi[p - 1, i, j]
                one = pot[p, i, j, 1] - (next_row(under) - under)
                two = pot[p, i, j, 2] - (next_lane(under) - under)
                send[p, :, i * OWN + j, 0] = one.reshape(GROUP, ROWS, NZ)
                send[p, :, i * OWN + j, 1] = two.reshape(GROUP, ROWS, NZ)
        for copy in forward(p):
            copy.start()

        @pl.when(off_middle)
        def _():
            middle_row(p, me, 3 - p // HALF).start()

        @pl.when(is_middle)
        def _():
            for ij in range(PAIRS):
                edge[p, me, ij] = send[p, 2, ij, 1]

        recv[p, me] = send[p, slab]

    @pl.when(even_slab)
    def _():
        @pl.loop(0, PLANES + 1)
        def _(p):
            field_edge[p] = jnp.zeros((NCOEF, ROWS, NZ), jnp.float32)

    @pl.when(slab == GROUP - 1)
    def _():
        @pl.loop(0, PLANES + 1)
        def _(p):
            edge[p] = jnp.zeros((GROUP, PAIRS, ROWS, NZ), jnp.float32)

    @pl.when(jnp.logical_not(has_above))
    def _():
        upper[...] = jnp.zeros_like(upper)

    @pl.when(jnp.logical_not(has_below))
    def _():
        field[0, pl.ds(1, 2)] = jnp.zeros((2, NCOEF, ROWS, NZ), jnp.float32)

    all_of(recv.at[0, 0], own_sem).wait()
    forward_came(0)
    up = pltpu.make_async_remote_copy(
        src_ref=recv.at[0], dst_ref=upper,
        send_sem=up_send, recv_sem=up_recv, device_id=down_id, device_id_type=mesh_id,
    )

    @pl.when(tells_below)
    def _():
        pl.semaphore_wait(ready.at[0], 1)

    @pl.when(has_below)
    def _():
        up.start()

    for copy in material:
        copy.wait()
    all_of(phi_recv.at[pl.ds(0, GROUP - 1)], f_recv.at[1]).wait()

    @pl.when(odd_slab)
    def _():
        chip_phi().start()
        chip_row(0).start()

    @pl.when(is_middle)
    def _():
        middle_came(1)
        middle_came(0)

    @pl.when(even_slab)
    def _():
        chip_phi().wait_recv()
        chip_row(0).wait_recv()

    @pl.when(has_above)
    def _():
        up.wait_recv()

    @pl.loop(0, GROUP)
    def _(q):
        for ij in range(PAIRS):
            top = phi_recv[q, ij]
            row = edge[PLANES, q, ij, top_row, :]
            recv[PLANES, q, ij, 0] = upper[q, ij, 0] - (slab_next_row(top, row) - top)
            recv[PLANES, q, ij, 1] = upper[q, ij, 1] - (slab_next_lane(top) - top)

    down = pltpu.make_async_remote_copy(
        src_ref=field.at[PLANES, pl.ds(1, 2)], dst_ref=field.at[0, pl.ds(1, 2)],
        send_sem=low_send, recv_sem=low_recv, device_id=up_id, device_id_type=mesh_id,
    )

    def nonlinear(p):
        @pl.loop(0, GROUP)
        def _(q):
            for i in range(2):
                for j in range(OWN):
                    ij = i * OWN + j
                    one, two = recv[p, q, ij, 0], recv[p, q, ij, 1]
                    row = edge[p, q, ij, top_row, :]
                    flux[3 * i, q, j] = (slab_next_row(two, row) - two) - (slab_next_lane(one) - one)
                    flux[3 * i + 1, q, j] = two - recv[p + 1, q, ij, 1]
                    flux[3 * i + 2, q, j] = recv[p + 1, q, ij, 0] - one

        @pl.loop(0, 6)
        def _(pc):
            for t, (kind, orders) in enumerate(CLASSES):
                where = [coef_index(kind, m) for m in orders]
                terms = [flux[pc, c // OWN, c % OWN] for c in where]
                for n in range(FOLDS):
                    wave[n, t, pc] = combine(terms, [factor(kind, m, n) for m in orders])

        density, region = dens[p], regn[p]
        iron = region == 0
        share = jnp.where(iron, density * density * density, 0.0) * jnp.float32(1.0 - iron_floor)
        slope = jnp.where(iron, 3.0 * density * density, 0.0)
        base = jnp.where(region == 1, jnp.float32(magnet_reluct), jnp.float32(1.0))

        def samples(n, total):
            state = [[], [], []]
            adjoint = [[], [], []]
            for pc in range(6):
                ce, co, se, so = (wave[n, t, pc] for t in range(4))
                a, b, d, f = ce + co, ce - co, se + so, se - so
                (state if pc < 3 else adjoint)[pc % 3] = (a + d, a - d, b - f, b + f)
            values = [[], [], []]
            part = None
            for v in range(4):
                s = [state[c][v] for c in range(3)]
                g = [adjoint[c][v] for c in range(3)]
                square = s[0] * s[0] + s[1] * s[1] + s[2] * s[2]
                inner = s[0] * g[0] + s[1] * g[1] + s[2] * g[2]
                r = 1.0 / (square + 1.0)
                t = share * r
                ri = r * inner
                nu = base - t
                mu = (t + t) * ri
                part = ri if part is None else part + ri
                for c in range(3):
                    values[c].append(nu * g[c] + mu * s[c])
            for c in range(3):
                w, x, y, z = values[c]
                a, d = w + x, w - x
                b, f = z + y, z - y
                fold[n, 0, c] = a + b
                fold[n, 1, c] = a - b
                fold[n, 2, c] = d + f
                fold[n, 3, c] = d - f
            ends = (n == 0) | (n == FOLDS - 1)
            return total + part * jnp.where(ends, 0.5, 1.0)

        total = lax.fori_loop(0, FOLDS, samples, jnp.zeros((ROWS, NZ), jnp.float32))
        grad[p] = total * slope * jnp.float32((1.0 - iron_floor) / NT)

        for t, (kind, orders) in enumerate(CLASSES):
            for c in range(3):
                terms = [fold[n, t, c] for n in range(FOLDS)]
                for m in orders:
                    scales = [
                        factor(kind, m, n) * (1.0 if 0 < n < FOLDS - 1 else 0.5) * 2.0 / NT
                        for n in range(FOLDS)
                    ]
                    field[p + 1, c, coef_index(kind, m)] = combine(terms, scales)

    def give_back(p, g):
        @pl.when(odd_slab)
        def _():
            field_row(p).wait_recv()

        @pl.when(is_middle)
        def _():
            for copy in fix_row(p, g):
                copy.start()

            fix[p] = field[p + 1, 0, pl.ds(me * OWN, OWN)]

        @pl.loop(0, GROUP)
        def _(q):
            for j in range(OWN):
                at = q * OWN + j
                zero, one, two = (field[p + 1, c, at] for c in range(3))
                row = field_edge[p, at, end_row, :]
                bsend[p, q, j, 0] = (field[p, 2, at] - two) - (slab_prior_lane(zero) - zero)
                bsend[p, q, j, 1] = (slab_prior_row(zero, row) - zero) - (field[p, 1, at] - one)

        for copy in backward(p, g):
            copy.start()
        brecv[p, slab] = bsend[p, me]

    def give_back_zero():
        @pl.when(odd_slab)
        def _():
            field_row(PLANES).wait_recv()

        @pl.when(is_middle)
        def _():
            for copy in fix_row(PLANES, 1):
                copy.start()

            fix[PLANES] = field[PLANES, 2, pl.ds(me * OWN, OWN)]

        @pl.loop(0, GROUP)
        def _(q):
            for j in range(OWN):
                at = q * OWN + j
                one, two = field[PLANES, 1, at], field[PLANES, 2, at]
                row = field_edge[PLANES, at, end_row, :]
                zsend[q, j] = (slab_prior_lane(one) - one) - (slab_prior_row(two, row) - two)

        @pl.when(has_below)
        def _():
            for copy in backward_zero():
                copy.start()

        zrecv[slab] = zsend[me]

    @pl.loop(0, PLANES)
    def _(k):
        p = PLANES - 1 - k

        for g, at in ((2, PLANES - 1), (3, HALF - 1)):
            @pl.when(p == at)
            def _():
                forward_came(g)

                @pl.when(is_middle)
                def _():
                    middle_came(g)

        @pl.when(p > 0)
        def _():
            @pl.when(odd_slab)
            def _():
                chip_row(p).start()

            @pl.when(even_slab)
            def _():
                chip_row(p).wait_recv()

        nonlinear(p)

        @pl.when(even_slab)
        def _():
            field_row(p).start()

        @pl.when(k == 0)
        def _():
            @pl.when(even_slab)
            def _():
                field_row(PLANES).start()

            @pl.when(tells_above)
            def _():
                pl.semaphore_wait(ready.at[1], 1)

            @pl.when(has_above)
            def _():
                down.start()

            give_back_zero()

        @pl.when(k > 0)
        def _():
            give_back(p + 1, 1)

    @pl.when(has_below)
    def _():
        down.wait_recv()

    give_back(0, 0)

    swap = to_sample(grad, grad_out, g_send, g_recv, lax.rem(me + 2, GROUP))

    @pl.when(swaps)
    def _():
        swap.start()

    @pl.when(jnp.logical_not(swaps))
    def _():
        grad_out[...] = grad[...]

    def fixed(parts, p, j, sign):
        row = jnp.where(slab_row == 0, fix[p, j, end_row, :], 0.0)
        parts[2] = parts[2] + row if sign > 0 else parts[2] - row
        return jnp.concatenate(parts, axis=0)

    objective.wait()
    all_of(brecv.at[pl.ds(1, PLANES - 1), pl.ds(0, GROUP - 1)], b_recv.at[1]).wait()

    @pl.when(off_middle)
    def _():
        all_of(fix.at[pl.ds(1, PLANES), :, end_row], mid_recv.at[1]).wait()

    @pl.when(has_below)
    def _():
        all_of(zrecv.at[pl.ds(0, GROUP - 1)], b_recv.at[2]).wait()
        for j in range(OWN):
            below_sum[j] = fixed([zrecv[q, j] for q in range(GROUP)], PLANES, j, -1)

    @pl.when(jnp.logical_not(has_below))
    def _():
        below_sum[...] = jnp.zeros_like(below_sum)

    @pl.loop(0, PLANES)
    def _(k):
        p = PLANES - 1 - k

        @pl.when(p == 0)
        def _():
            all_of(brecv.at[0, pl.ds(0, GROUP - 1)], b_recv.at[0]).wait()

            @pl.when(off_middle)
            def _():
                all_of(fix.at[0, :, end_row], mid_recv.at[0]).wait()

        for j in range(OWN):
            zero = below_sum[j]
            one = brecv[p, :, j, 0].reshape(NY, NZ)
            two = fixed([brecv[p, q, j, 1] for q in range(GROUP)], p, j, 1)
            for c, part in enumerate((zero, one, two)):
                out[j, c, p] = obj[j, c, p] - part
            below_sum[j] = zero - (prior_row(one) - one) - (prior_lane(two) - two)

    @pl.when(jnp.logical_not(has_below))
    def _():
        @pl.loop(0, PLANES)
        def _(p):
            for j in range(OWN):
                out[j, 0, p] = out[j, 0, p] + below_sum[j]

    @pl.when(swaps)
    def _():
        swap.wait()

    @pl.when(has_below)
    def _():
        up.wait_send()

    @pl.when(has_above)
    def _():
        down.wait_send()

    all_of(send.at[:, pl.ds(0, GROUP - 1)], f_send).wait()
    all_of(phi_send.at[pl.ds(0, GROUP - 1)], p_send).wait()
    all_of(bsend.at[:, pl.ds(0, GROUP - 1)], b_send).wait()

    @pl.when(has_below)
    def _():
        all_of(zsend.at[pl.ds(0, GROUP - 1)], z_send).wait()

    @pl.when(off_middle)
    def _():
        all_of(edge.at[:, 0, :, top_row], mid_send).wait()

    @pl.when(is_middle)
    def _():
        all_of(field_edge.at[:, pl.ds(0, OWN * (GROUP - 1)), end_row], mid_send).wait()

    @pl.when(odd_slab)
    def _():
        all_of(edge.at[:, :, :, top_row], chip_send).wait()

    @pl.when(even_slab)
    def _():
        all_of(field_edge.at[:, :, end_row], chip_send).wait()


def write_out(held, held_grad, out_hbm, grad_hbm, sems):
    copies = [pltpu.make_async_copy(held.at[j], out_hbm.at[j], sems.at[j]) for j in range(OWN)]
    copies.append(pltpu.make_async_copy(held_grad, grad_hbm, sems.at[OWN]))
    for copy in copies:
        copy.start()
    for copy in copies:
        copy.wait()


def local(state_hat, adjoint_hat, objective_hat, density, region):
    f32 = jnp.float32
    hbm = pl.BlockSpec(memory_space=pl.ANY)
    dma = pltpu.SemaphoreType.DMA
    links = (PLANES + 1, GROUP - 1)
    residual = (OWN, 3, PLANES, NY, NZ)
    gradient = (PLANES, ROWS, NZ)
    vmem = pl.BlockSpec(memory_space=pltpu.VMEM)
    held = pl.pallas_call(
        kernel,
        out_shape=(pltpu.VMEM(residual, f32), pltpu.VMEM(gradient, f32)),
        in_specs=[hbm] * 5,
        out_specs=(vmem, vmem),
        scratch_shapes=[
            pltpu.VMEM((PLANES, 2, OWN, 3, NY, NZ), f32),
            pltpu.VMEM((PLANES, 2, OWN, NY, NZ), f32),
            pltpu.VMEM((OWN, 3, PLANES, NY, NZ), f32),
            pltpu.VMEM((PLANES, ROWS, NZ), f32),
            pltpu.VMEM((PLANES, ROWS, NZ), jnp.int32),
            pltpu.VMEM((GROUP, PAIRS, 2, ROWS, NZ), f32),
            pltpu.VMEM((PLANES, GROUP, PAIRS, 2, ROWS, NZ), f32),
            pltpu.VMEM((PLANES + 1, GROUP, PAIRS, 2, ROWS, NZ), f32),
            pltpu.VMEM((GROUP, PAIRS, ROWS, NZ), f32),
            pltpu.VMEM((GROUP, PAIRS, ROWS, NZ), f32),
            pltpu.VMEM((PLANES + 1, GROUP, PAIRS, ROWS, NZ), f32),
            pltpu.VMEM((PLANES, GROUP, OWN, 2, ROWS, NZ), f32),
            pltpu.VMEM((PLANES, GROUP, OWN, 2, ROWS, NZ), f32),
            pltpu.VMEM((GROUP, OWN, ROWS, NZ), f32),
            pltpu.VMEM((GROUP, OWN, ROWS, NZ), f32),
            pltpu.VMEM((6, GROUP, OWN, ROWS, NZ), f32),
            pltpu.VMEM((FOLDS, 4, 6, ROWS, NZ), f32),
            pltpu.VMEM((FOLDS, 4, 3, ROWS, NZ), f32),
            pltpu.VMEM((PLANES + 1, 3, NCOEF, ROWS, NZ), f32),
            pltpu.VMEM((PLANES + 1, NCOEF, ROWS, NZ), f32),
            pltpu.VMEM((PLANES + 1, OWN, ROWS, NZ), f32),
            pltpu.VMEM((OWN, NY, NZ), f32),
            pltpu.VMEM((PLANES, ROWS, NZ), f32),
            dma((2,)), dma, dma((2,)), dma, dma, dma, dma, dma,
            dma, dma, dma((4,)), dma, dma, dma((3,)),
            dma, dma((PLANES + 1,)), dma, dma((4,)),
            dma, dma, pltpu.SemaphoreType.REGULAR((2,)),
        ],
        compiler_params=pltpu.CompilerParams(
            collective_id=0, has_side_effects=True, vmem_limit_bytes=60 * 1024 * 1024
        ),
    )(state_hat, adjoint_hat, objective_hat, density, region)
    return pl.pallas_call(
        write_out,
        out_shape=(jax.ShapeDtypeStruct(residual, f32), jax.ShapeDtypeStruct(gradient, f32)),
        in_specs=[vmem, vmem],
        out_specs=(hbm, hbm),
        scratch_shapes=[dma((OWN + 1,))],
        compiler_params=pltpu.CompilerParams(vmem_limit_bytes=1024 * 1024),
    )(*held)


def solution(mesh):
    in_specs = (
        P("sample", None, "space", None, None),
        P("sample", None, "space", None, None),
        P("sample", None, "space", None, None),
        P("space", None, None),
        P("space", None, None),
    )
    out_specs = (P("sample", None, "space", None, None), P("space", "sample", None))
    return jax.shard_map(local, mesh=mesh, in_specs=in_specs, out_specs=out_specs, check_vma=False)
```

```python
import math

import jax
import jax.numpy as jnp
from jax import lax
from jax.experimental import pallas as pl
from jax.experimental.pallas import tpu as pltpu
from jax.sharding import PartitionSpec as P

NT = 40
NCOEF = 20
NY = 32
NZ = 128
PLANES = 8
GROUP = 4
OWN = NCOEF // GROUP
ROWS = NY // GROUP
FOLDS = NT // 4 + 1
PAIRS = 2 * OWN
RUN = 4
HALF = PLANES // 2

magnet_reluct = 0.95
iron_floor = 0.05

CLASSES = (
    ("cos", (2, 4, 6, 8, 10)),
    ("cos", (1, 3, 5, 7, 9)),
    ("sin", (2, 4, 6, 8, 10)),
    ("sin", (1, 3, 5, 7, 9)),
)


def coef_index(kind, order):
    return 2 * (order - 1) + (0 if kind == "cos" else 1)


def factor(kind, order, n):
    turn = (n * order) % NT
    quarter = NT // 4
    if kind == "sin":
        turn = (turn - quarter) % NT
    if turn % quarter == 0:
        return (1.0, 0.0, -1.0, 0.0)[turn // quarter]
    return math.cos(2.0 * math.pi * turn / NT)


def combine(terms, constants):
    total = None
    for term, constant in zip(terms, constants):
        if constant == 0.0:
            continue
        if constant == 1.0:
            piece = term
        elif constant == -1.0:
            piece = -term
        else:
            piece = term * jnp.float32(constant)
        total = piece if total is None else total + piece
    return jnp.zeros_like(terms[0]) if total is None else total


def kernel(
    state_hbm, adjoint_hbm, objective_hbm, density_hbm, region_hbm,
    out, grad_out,
    pot, phi, obj, dens, regn, upper, send, recv, phi_send, phi_recv, edge,
    bsend, brecv, zsend, zrecv, flux, wave, fold, field, field_edge, fix, below_sum, grad,
    in_sems, obj_sem, mat_sems, up_send, up_recv, low_send, low_recv,
    f_send, p_send, f_recv, b_send, z_send, b_recv, chip_send, chip_recv, mid_send, mid_recv,
    g_send, g_recv, ready,
):
    me = lax.axis_index("sample")
    block = lax.axis_index("space")
    blocks = lax.axis_size("space")
    above = lax.rem(block + 1, blocks)
    below = lax.rem(block + blocks - 1, blocks)
    has_above, has_below = block < blocks - 1, block > 0
    mesh_id = pl.DeviceIdType.MESH

    def turned(index, where):
        return lax.rem(index + 2 * lax.rem(where // RUN, 2), GROUP)

    swaps = lax.rem(block // RUN, 2) == 1
    slab = turned(me, block)
    odd_slab = lax.rem(me, 2) == 1
    even_slab = jnp.logical_not(odd_slab)
    partner = me + 1 - 2 * lax.rem(me, 2)
    middle = turned(1, block)
    is_middle = me == middle
    off_middle = me != middle
    up_id = {"space": above, "sample": turned(slab, above)}
    down_id = {"space": below, "sample": turned(slab, below)}
    peers = [lax.rem(me + 2, GROUP), lax.rem(partner + 2, GROUP), partner]
    arguments = (state_hbm, adjoint_hbm)

    def to_sample(source, target, send_sem, recv_sem, peer):
        return pltpu.make_async_remote_copy(
            src_ref=source, dst_ref=target, send_sem=send_sem, recv_sem=recv_sem,
            device_id={"sample": peer}, device_id_type=mesh_id,
        )

    barrier = pltpu.get_barrier_semaphore()
    for peer in peers:
        pl.semaphore_signal(barrier, inc=1, device_id={"sample": peer}, device_id_type=mesh_id)

    ends, begins = lax.rem(block, RUN) == RUN - 1, lax.rem(block, RUN) == 0
    waits_above, waits_below = has_above & ends, has_below & jnp.logical_not(begins)
    tells_above, tells_below = has_above & jnp.logical_not(ends), has_below & begins

    @pl.when(tells_above)
    def _():
        pl.semaphore_signal(barrier, inc=1, device_id=up_id, device_id_type=mesh_id)

    @pl.when(tells_below)
    def _():
        pl.semaphore_signal(barrier, inc=1, device_id=down_id, device_id_type=mesh_id)

    def slab_rows(s):
        return pl.ds(pl.multiple_of(s * ROWS, ROWS), ROWS)

    def load(p):
        return [
            pltpu.make_async_copy(ref.at[:, :, p], pot.at[p, i], in_sems.at[min(p, 1) if isinstance(p, int) else 1])
            for i, ref in enumerate(arguments)
        ]

    def all_of(ref, sem):
        return pltpu.make_async_copy(ref, ref, sem)

    for copy in load(0):
        copy.start()

    @pl.loop(1, PLANES)
    def _(p):
        for copy in load(p):
            copy.start()

    material = [
        pltpu.make_async_copy(density_hbm.at[:, slab_rows(slab)], dens, mat_sems.at[0]),
        pltpu.make_async_copy(region_hbm.at[:, slab_rows(slab)], regn, mat_sems.at[1]),
    ]
    for copy in material:
        copy.start()
    objective = pltpu.make_async_copy(objective_hbm, obj, obj_sem)
    objective.start()

    def forward_first():
        return [
            to_sample(
                pot.at[0, i, :, pl.ds(1, 2), slab_rows(turned(peer, block))],
                recv.at[0, me, pl.ds(i * OWN, OWN)],
                f_send, f_recv.at[0], peer,
            )
            for peer in peers
            for i in range(2)
        ]

    def forward(p):
        return [
            to_sample(
                send.at[p, turned(peer, block)], recv.at[p, me], f_send, f_recv.at[3 - p // HALF], peer
            )
            for peer in peers
        ]

    groups = (pl.ds(0, 1), pl.ds(PLANES, 1), pl.ds(HALF, HALF), pl.ds(1, HALF - 1))

    def forward_came(g):
        all_of(recv.at[groups[g], pl.ds(0, GROUP - 1)], f_recv.at[g]).wait()

    def forward_phi():
        return [
            to_sample(
                phi_send.at[turned(peer, block)], phi_recv.at[me],
                p_send, f_recv.at[1], peer,
            )
            for peer in peers
        ]

    def backward(p, g):
        return [
            to_sample(bsend.at[p, peer], brecv.at[p, slab], b_send, b_recv.at[g], peer)
            for peer in peers
        ]

    def backward_zero():
        return [
            to_sample(zsend.at[peer], zrecv.at[slab], z_send, b_recv.at[2], peer)
            for peer in peers
        ]

    top_row, end_row = pl.ds(0, 1), pl.ds(ROWS - 1, 1)

    def middle_row(p, q, g):
        source = send.at[p, 2, :, 1, top_row]
        return to_sample(source, edge.at[p, q, :, top_row], mid_send, mid_recv.at[g], middle)

    def middle_phi(q):
        source = phi_send.at[2, :, top_row]
        return to_sample(source, edge.at[PLANES, q, :, top_row], mid_send, mid_recv.at[1], middle)

    def middle_came(g):
        all_of(edge.at[groups[g], pl.ds(0, GROUP - 1), :, top_row], mid_recv.at[g]).wait()

    def chip_row(p):
        return to_sample(recv.at[p, :, :, 1, top_row], edge.at[p, :, :, top_row], chip_send, chip_recv.at[p], partner)

    def chip_phi():
        return to_sample(
            phi_recv.at[:, :, top_row], edge.at[PLANES, :, :, top_row],
            chip_send, chip_recv.at[PLANES], partner,
        )

    def last_rows(p, some):
        if isinstance(p, int) and p == PLANES:
            return field.at[PLANES, 2, some, end_row]
        return field.at[p + 1, 0, some, end_row]

    def field_row(p):
        return to_sample(
            last_rows(p, pl.ds(0, NCOEF)), field_edge.at[p, :, end_row], chip_send, chip_recv.at[p], partner
        )

    def fix_row(p, g):
        return [
            to_sample(
                last_rows(p, pl.ds(peer * OWN, OWN)), fix.at[p, :, end_row], mid_send, mid_recv.at[g], peer
            )
            for peer in peers
        ]

    row_id = lax.broadcasted_iota(jnp.int32, (NY, NZ), 0)
    lane_id = lax.broadcasted_iota(jnp.int32, (NY, NZ), 1)
    slab_row = lax.broadcasted_iota(jnp.int32, (ROWS, NZ), 0)
    slab_lane = lax.broadcasted_iota(jnp.int32, (ROWS, NZ), 1)

    def next_row(a):
        return jnp.where(row_id == NY - 1, 0.0, pltpu.roll(a, NY - 1, 0))

    def next_lane(a):
        return jnp.where(lane_id == NZ - 1, 0.0, pltpu.roll(a, NZ - 1, 1))

    def prior_row(a):
        return jnp.where(row_id == 0, 0.0, pltpu.roll(a, 1, 0))

    def prior_lane(a):
        return jnp.where(lane_id == 0, 0.0, pltpu.roll(a, 1, 1))

    def slab_next_row(a, row):
        return jnp.where(slab_row == ROWS - 1, row, pltpu.roll(a, ROWS - 1, 0))

    def slab_next_lane(a):
        return jnp.where(slab_lane == NZ - 1, 0.0, pltpu.roll(a, NZ - 1, 1))

    def slab_prior_row(a, row):
        return jnp.where(slab_row == 0, row, pltpu.roll(a, 1, 0))

    def slab_prior_lane(a):
        return jnp.where(slab_lane == 0, 0.0, pltpu.roll(a, 1, 1))

    pl.semaphore_wait(barrier, GROUP - 1 + waits_above.astype(jnp.int32) + waits_below.astype(jnp.int32))
    all_of(pot.at[0], in_sems.at[0]).wait()
    for copy in forward_first():
        copy.start()

    @pl.when(waits_above)
    def _():
        pl.semaphore_signal(ready.at[0], inc=1, device_id=up_id, device_id_type=mesh_id)

    @pl.when(waits_below)
    def _():
        pl.semaphore_signal(ready.at[1], inc=1, device_id=down_id, device_id_type=mesh_id)

    for i in range(2):
        for j in range(OWN):
            phi[0, i, j] = pot[0, i, j, 0]
            recv[0, me, i * OWN + j] = pot[0, i, j, pl.ds(1, 2), slab_rows(slab), :]
            send[0, 2, i * OWN + j, 1] = pot[0, i, j, 2, pl.ds(2 * ROWS, ROWS), :]

    all_of(pot.at[pl.ds(1, PLANES - 1)], in_sems.at[1]).wait()

    @pl.loop(1, PLANES)
    def _(p):
        for i in range(2):
            @pl.loop(0, OWN)
            def _(j):
                phi[p, i, j] = phi[p - 1, i, j] + pot[p, i, j, 0]

    for i in range(2):
        for j in range(OWN):
            phi_send[:, i * OWN + j] = phi[PLANES - 1, i, j].reshape(GROUP, ROWS, NZ)
    phi_recv[me] = phi_send[slab]
    for copy in forward_phi():
        copy.start()

    @pl.when(off_middle)
    def _():
        middle_phi(me).start()
        middle_row(0, me, 0).start()

    @pl.when(is_middle)
    def _():
        for ij in range(PAIRS):
            edge[PLANES, me, ij] = phi_send[2, ij]
            edge[0, me, ij] = send[0, 2, ij, 1]

    @pl.loop(0, PLANES - 1)
    def _(k):
        p = PLANES - 1 - k
        for i in range(2):
            for j in range(OWN):
                under = phi[p - 1, i, j]
                one = pot[p, i, j, 1] - (next_row(under) - under)
                two = pot[p, i, j, 2] - (next_lane(under) - under)
                send[p, :, i * OWN + j, 0] = one.reshape(GROUP, ROWS, NZ)
                send[p, :, i * OWN + j, 1] = two.reshape(GROUP, ROWS, NZ)
        for copy in forward(p):
            copy.start()

        @pl.when(off_middle)
        def _():
            middle_row(p, me, 3 - p // HALF).start()

        @pl.when(is_middle)
        def _():
            for ij in range(PAIRS):
                edge[p, me, ij] = send[p, 2, ij, 1]

        recv[p, me] = send[p, slab]

    @pl.when(even_slab)
    def _():
        @pl.loop(0, PLANES + 1)
        def _(p):
            field_edge[p] = jnp.zeros((NCOEF, ROWS, NZ), jnp.float32)

    @pl.when(slab == GROUP - 1)
    def _():
        @pl.loop(0, PLANES + 1)
        def _(p):
            edge[p] = jnp.zeros((GROUP, PAIRS, ROWS, NZ), jnp.float32)

    @pl.when(jnp.logical_not(has_above))
    def _():
        upper[...] = jnp.zeros_like(upper)

    @pl.when(jnp.logical_not(has_below))
    def _():
        field[0, pl.ds(1, 2)] = jnp.zeros((2, NCOEF, ROWS, NZ), jnp.float32)

    forward_came(0)
    up = pltpu.make_async_remote_copy(
        src_ref=recv.at[0], dst_ref=upper,
        send_sem=up_send, recv_sem=up_recv, device_id=down_id, device_id_type=mesh_id,
    )

    @pl.when(tells_below)
    def _():
        pl.semaphore_wait(ready.at[0], 1)

    @pl.when(has_below)
    def _():
        up.start()

    for copy in material:
        copy.wait()
    all_of(phi_recv.at[pl.ds(0, GROUP - 1)], f_recv.at[1]).wait()

    @pl.when(odd_slab)
    def _():
        chip_phi().start()
        chip_row(0).start()

    @pl.when(is_middle)
    def _():
        middle_came(1)
        middle_came(0)

    @pl.when(even_slab)
    def _():
        chip_phi().wait_recv()
        chip_row(0).wait_recv()

    @pl.when(has_above)
    def _():
        up.wait_recv()

    @pl.loop(0, GROUP)
    def _(q):
        for ij in range(PAIRS):
            top = phi_recv[q, ij]
            row = edge[PLANES, q, ij, top_row, :]
            recv[PLANES, q, ij, 0] = upper[q, ij, 0] - (slab_next_row(top, row) - top)
            recv[PLANES, q, ij, 1] = upper[q, ij, 1] - (slab_next_lane(top) - top)

    down = pltpu.make_async_remote_copy(
        src_ref=field.at[PLANES, pl.ds(1, 2)], dst_ref=field.at[0, pl.ds(1, 2)],
        send_sem=low_send, recv_sem=low_recv, device_id=up_id, device_id_type=mesh_id,
    )

    def nonlinear(p):
        @pl.loop(0, GROUP)
        def _(q):
            for i in range(2):
                for j in range(OWN):
                    ij = i * OWN + j
                    one, two = recv[p, q, ij, 0], recv[p, q, ij, 1]
                    row = edge[p, q, ij, top_row, :]
                    flux[3 * i, q, j] = (slab_next_row(two, row) - two) - (slab_next_lane(one) - one)
                    flux[3 * i + 1, q, j] = two - recv[p + 1, q, ij, 1]
                    flux[3 * i + 2, q, j] = recv[p + 1, q, ij, 0] - one

        @pl.loop(0, 6)
        def _(pc):
            for t, (kind, orders) in enumerate(CLASSES):
                where = [coef_index(kind, m) for m in orders]
                terms = [flux[pc, c // OWN, c % OWN] for c in where]
                for n in range(FOLDS):
                    wave[n, t, pc] = combine(terms, [factor(kind, m, n) for m in orders])

        density, region = dens[p], regn[p]
        iron = region == 0
        share = jnp.where(iron, density * density * density, 0.0) * jnp.float32(1.0 - iron_floor)
        slope = jnp.where(iron, 3.0 * density * density, 0.0)
        base = jnp.where(region == 1, jnp.float32(magnet_reluct), jnp.float32(1.0))

        def samples(n, total):
            state = [[], [], []]
            adjoint = [[], [], []]
            for pc in range(6):
                ce, co, se, so = (wave[n, t, pc] for t in range(4))
                a, b, d, f = ce + co, ce - co, se + so, se - so
                (state if pc < 3 else adjoint)[pc % 3] = (a + d, a - d, b - f, b + f)
            values = [[], [], []]
            part = None
            for v in range(4):
                s = [state[c][v] for c in range(3)]
                g = [adjoint[c][v] for c in range(3)]
                square = s[0] * s[0] + s[1] * s[1] + s[2] * s[2]
                inner = s[0] * g[0] + s[1] * g[1] + s[2] * g[2]
                r = 1.0 / (square + 1.0)
                t = share * r
                ri = r * inner
                nu = base - t
                mu = (t + t) * ri
                part = ri if part is None else part + ri
                for c in range(3):
                    values[c].append(nu * g[c] + mu * s[c])
            for c in range(3):
                w, x, y, z = values[c]
                a, d = w + x, w - x
                b, f = z + y, z - y
                fold[n, 0, c] = a + b
                fold[n, 1, c] = a - b
                fold[n, 2, c] = d + f
                fold[n, 3, c] = d - f
            ends = (n == 0) | (n == FOLDS - 1)
            return total + part * jnp.where(ends, 0.5, 1.0)

        total = lax.fori_loop(0, FOLDS, samples, jnp.zeros((ROWS, NZ), jnp.float32))
        grad[p] = total * slope * jnp.float32((1.0 - iron_floor) / NT)

        for t, (kind, orders) in enumerate(CLASSES):
            for c in range(3):
                terms = [fold[n, t, c] for n in range(FOLDS)]
                for m in orders:
                    scales = [
                        factor(kind, m, n) * (1.0 if 0 < n < FOLDS - 1 else 0.5) * 2.0 / NT
                        for n in range(FOLDS)
                    ]
                    field[p + 1, c, coef_index(kind, m)] = combine(terms, scales)

    def give_back(p, g):
        @pl.when(odd_slab)
        def _():
            field_row(p).wait_recv()

        @pl.when(is_middle)
        def _():
            for copy in fix_row(p, g):
                copy.start()

            fix[p] = field[p + 1, 0, pl.ds(me * OWN, OWN)]

        @pl.loop(0, GROUP)
        def _(q):
            for j in range(OWN):
                at = q * OWN + j
                zero, one, two = (field[p + 1, c, at] for c in range(3))
                row = field_edge[p, at, end_row, :]
                bsend[p, q, j, 0] = (field[p, 2, at] - two) - (slab_prior_lane(zero) - zero)
                bsend[p, q, j, 1] = (slab_prior_row(zero, row) - zero) - (field[p, 1, at] - one)

        for copy in backward(p, g):
            copy.start()
        brecv[p, slab] = bsend[p, me]

    def give_back_zero():
        @pl.when(odd_slab)
        def _():
            field_row(PLANES).wait_recv()

        @pl.when(is_middle)
        def _():
            for copy in fix_row(PLANES, 1):
                copy.start()

            fix[PLANES] = field[PLANES, 2, pl.ds(me * OWN, OWN)]

        @pl.loop(0, GROUP)
        def _(q):
            for j in range(OWN):
                at = q * OWN + j
                one, two = field[PLANES, 1, at], field[PLANES, 2, at]
                row = field_edge[PLANES, at, end_row, :]
                zsend[q, j] = (slab_prior_lane(one) - one) - (slab_prior_row(two, row) - two)

        @pl.when(has_below)
        def _():
            for copy in backward_zero():
                copy.start()

        zrecv[slab] = zsend[me]

    @pl.loop(0, PLANES)
    def _(k):
        p = PLANES - 1 - k

        for g, at in ((2, PLANES - 1), (3, HALF - 1)):
            @pl.when(p == at)
            def _():
                forward_came(g)

                @pl.when(is_middle)
                def _():
                    middle_came(g)

        @pl.when(p > 0)
        def _():
            @pl.when(odd_slab)
            def _():
                chip_row(p).start()

            @pl.when(even_slab)
            def _():
                chip_row(p).wait_recv()

        nonlinear(p)

        @pl.when(even_slab)
        def _():
            field_row(p).start()

        @pl.when(k == 0)
        def _():
            @pl.when(even_slab)
            def _():
                field_row(PLANES).start()

            @pl.when(tells_above)
            def _():
                pl.semaphore_wait(ready.at[1], 1)

            @pl.when(has_above)
            def _():
                down.start()

            give_back_zero()

        @pl.when(k > 0)
        def _():
            give_back(p + 1, 1)

    @pl.when(has_below)
    def _():
        down.wait_recv()

    give_back(0, 0)

    swap = to_sample(grad, grad_out, g_send, g_recv, lax.rem(me + 2, GROUP))

    @pl.when(swaps)
    def _():
        swap.start()

    @pl.when(jnp.logical_not(swaps))
    def _():
        grad_out[...] = grad[...]

    def fixed(parts, p, j, sign):
        row = jnp.where(slab_row == 0, fix[p, j, end_row, :], 0.0)
        parts[2] = parts[2] + row if sign > 0 else parts[2] - row
        return jnp.concatenate(parts, axis=0)

    objective.wait()
    all_of(brecv.at[pl.ds(1, PLANES - 1), pl.ds(0, GROUP - 1)], b_recv.at[1]).wait()

    @pl.when(off_middle)
    def _():
        all_of(fix.at[pl.ds(1, PLANES), :, end_row], mid_recv.at[1]).wait()

    @pl.when(has_below)
    def _():
        all_of(zrecv.at[pl.ds(0, GROUP - 1)], b_recv.at[2]).wait()
        for j in range(OWN):
            below_sum[j] = fixed([zrecv[q, j] for q in range(GROUP)], PLANES, j, -1)

    @pl.when(jnp.logical_not(has_below))
    def _():
        below_sum[...] = jnp.zeros_like(below_sum)

    @pl.loop(0, PLANES)
    def _(k):
        p = PLANES - 1 - k

        @pl.when(p == 0)
        def _():
            all_of(brecv.at[0, pl.ds(0, GROUP - 1)], b_recv.at[0]).wait()

            @pl.when(off_middle)
            def _():
                all_of(fix.at[0, :, end_row], mid_recv.at[0]).wait()

        for j in range(OWN):
            zero = below_sum[j]
            one = brecv[p, :, j, 0].reshape(NY, NZ)
            two = fixed([brecv[p, q, j, 1] for q in range(GROUP)], p, j, 1)
            for c, part in enumerate((zero, one, two)):
                out[j, c, p] = obj[j, c, p] - part
            below_sum[j] = zero - (prior_row(one) - one) - (prior_lane(two) - two)

    @pl.when(jnp.logical_not(has_below))
    def _():
        @pl.loop(0, PLANES)
        def _(p):
            for j in range(OWN):
                out[j, 0, p] = out[j, 0, p] + below_sum[j]

    @pl.when(swaps)
    def _():
        swap.wait()

    @pl.when(has_below)
    def _():
        up.wait_send()

    @pl.when(has_above)
    def _():
        down.wait_send()

    all_of(send.at[:, pl.ds(0, GROUP - 1)], f_send).wait()
    all_of(phi_send.at[pl.ds(0, GROUP - 1)], p_send).wait()
    all_of(bsend.at[:, pl.ds(0, GROUP - 1)], b_send).wait()

    @pl.when(has_below)
    def _():
        all_of(zsend.at[pl.ds(0, GROUP - 1)], z_send).wait()

    @pl.when(off_middle)
    def _():
        all_of(edge.at[:, 0, :, top_row], mid_send).wait()

    @pl.when(is_middle)
    def _():
        all_of(field_edge.at[:, pl.ds(0, OWN * (GROUP - 1)), end_row], mid_send).wait()

    @pl.when(odd_slab)
    def _():
        all_of(edge.at[:, :, :, top_row], chip_send).wait()

    @pl.when(even_slab)
    def _():
        all_of(field_edge.at[:, :, end_row], chip_send).wait()


def write_out(held, held_grad, out_hbm, grad_hbm, sems):
    copies = [pltpu.make_async_copy(held.at[j], out_hbm.at[j], sems.at[j]) for j in range(OWN)]
    copies.append(pltpu.make_async_copy(held_grad, grad_hbm, sems.at[OWN]))
    for copy in copies:
        copy.start()
    for copy in copies:
        copy.wait()


def local(state_hat, adjoint_hat, objective_hat, density, region):
    f32 = jnp.float32
    hbm = pl.BlockSpec(memory_space=pl.ANY)
    dma = pltpu.SemaphoreType.DMA
    links = (PLANES + 1, GROUP - 1)
    residual = (OWN, 3, PLANES, NY, NZ)
    gradient = (PLANES, ROWS, NZ)
    vmem = pl.BlockSpec(memory_space=pltpu.VMEM)
    held = pl.pallas_call(
        kernel,
        out_shape=(pltpu.VMEM(residual, f32), pltpu.VMEM(gradient, f32)),
        in_specs=[hbm] * 5,
        out_specs=(vmem, vmem),
        scratch_shapes=[
            pltpu.VMEM((PLANES, 2, OWN, 3, NY, NZ), f32),
            pltpu.VMEM((PLANES, 2, OWN, NY, NZ), f32),
            pltpu.VMEM((OWN, 3, PLANES, NY, NZ), f32),
            pltpu.VMEM((PLANES, ROWS, NZ), f32),
            pltpu.VMEM((PLANES, ROWS, NZ), jnp.int32),
            pltpu.VMEM((GROUP, PAIRS, 2, ROWS, NZ), f32),
            pltpu.VMEM((PLANES, GROUP, PAIRS, 2, ROWS, NZ), f32),
            pltpu.VMEM((PLANES + 1, GROUP, PAIRS, 2, ROWS, NZ), f32),
            pltpu.VMEM((GROUP, PAIRS, ROWS, NZ), f32),
            pltpu.VMEM((GROUP, PAIRS, ROWS, NZ), f32),
            pltpu.VMEM((PLANES + 1, GROUP, PAIRS, ROWS, NZ), f32),
            pltpu.VMEM((PLANES, GROUP, OWN, 2, ROWS, NZ), f32),
            pltpu.VMEM((PLANES, GROUP, OWN, 2, ROWS, NZ), f32),
            pltpu.VMEM((GROUP, OWN, ROWS, NZ), f32),
            pltpu.VMEM((GROUP, OWN, ROWS, NZ), f32),
            pltpu.VMEM((6, GROUP, OWN, ROWS, NZ), f32),
            pltpu.VMEM((FOLDS, 4, 6, ROWS, NZ), f32),
            pltpu.VMEM((FOLDS, 4, 3, ROWS, NZ), f32),
            pltpu.VMEM((PLANES + 1, 3, NCOEF, ROWS, NZ), f32),
            pltpu.VMEM((PLANES + 1, NCOEF, ROWS, NZ), f32),
            pltpu.VMEM((PLANES + 1, OWN, ROWS, NZ), f32),
            pltpu.VMEM((OWN, NY, NZ), f32),
            pltpu.VMEM((PLANES, ROWS, NZ), f32),
            dma((2,)), dma, dma((2,)), dma, dma, dma, dma,
            dma, dma, dma((4,)), dma, dma, dma((3,)),
            dma, dma((PLANES + 1,)), dma, dma((4,)),
            dma, dma, pltpu.SemaphoreType.REGULAR((2,)),
        ],
        compiler_params=pltpu.CompilerParams(
            collective_id=0, has_side_effects=True, vmem_limit_bytes=60 * 1024 * 1024
        ),
    )(state_hat, adjoint_hat, objective_hat, density, region)
    return pl.pallas_call(
        write_out,
        out_shape=(jax.ShapeDtypeStruct(residual, f32), jax.ShapeDtypeStruct(gradient, f32)),
        in_specs=[vmem, vmem],
        out_specs=(hbm, hbm),
        scratch_shapes=[dma((OWN + 1,))],
        compiler_params=pltpu.CompilerParams(vmem_limit_bytes=1024 * 1024),
    )(*held)


def solution(mesh):
    in_specs = (
        P("sample", None, "space", None, None),
        P("sample", None, "space", None, None),
        P("sample", None, "space", None, None),
        P("space", None, None),
        P("space", None, None),
    )
    out_specs = (P("sample", None, "space", None, None), P("space", "sample", None))
    return jax.shard_map(local, mesh=mesh, in_specs=in_specs, out_specs=out_specs, check_vma=False)
```
